256 devices in a mesh: snp: 16 (over z, core), trait: 16 (over y, x).
Axes of the slice: x: 4, y: 4, z: 8, core: 2. Of those that a mesh axis runs over, the one named last changes fastest.
Arguments:
- ld_band: float32 [8192, 3072], P('snp'), may hold values from -0.109375 to 0.109375
- marginal: float32 [8192, 4096], P('snp', 'trait'), may hold values from -6 to 6
- effects_init: float32 [8192, 4096], P('snp', 'trait'), may hold values from -6 to 6
- factor_in: float32 [4096, 256], P('trait'), may hold values from -0.09375 to 0.09375
- factor_out: float32 [4096, 256], P('trait'), may hold values from -0.375 to 0.375
- ld_width: int32 [64], replicated, may hold values from 512 to 3072, as said below
- ld_starts: int32 [64], replicated, may hold values from 0 to 8191, as said below
Outputs:
- fitted: float32 [8192, 4096], P('snp', 'trait')
The draws below stay inside these ranges and needn't reach their ends.
Inputs may be any that keep to these rules, and one draw needn't show every extreme that they name: `ld_width`: every value lies in 512 to 3072; the values 3072 and 512 each occur in every draw. ld_starts[0] is 0, the values rise strictly, and the last one is 8191.
All inputs are finite; a program needn't handle non-finite values.
Results may differ from the reference program's by a relative error of at most 0.0003.
Values sent between devices are 32-bit elements; how exact they have to be, the bound alone decides.
A program may use at most 128 MiB of HBM per device.

```python
import jax
import jax.numpy as jnp
from jax import lax

K = 4096
RF = 256
WMAX = 3072
WMIN = 512
ROWS = 512
STEPS = 2
M = 8192
NBLK = 64


def draw_ld_width(key, part):
    widths = jax.random.randint(key, (NBLK,), WMIN, WMAX + 1, dtype=jnp.int32)
    widest = jax.random.randint(jax.random.fold_in(key, 11), (), 0, NBLK, dtype=jnp.int32)
    narrowest = (widest + 1 + jax.random.randint(jax.random.fold_in(key, 12), (), 0, NBLK - 1, dtype=jnp.int32)) % NBLK
    widths = widths.at[widest].set(WMAX)
    return widths.at[narrowest].set(WMIN)


def draw_ld_starts(key, part):
    picked = jax.random.permutation(key, M - 2)[:NBLK - 2] + 1
    first = jnp.zeros((1,), jnp.int32)
    last = jnp.full((1,), M - 1, jnp.int32)
    return jnp.concatenate([first, jnp.sort(picked).astype(jnp.int32), last])


def block_levels(own_key, shape, pieces, least, largest):
    factor_of, own = 1.0, jax.random.fold_in(own_key, 6)
    for axis_at, parts in pieces:
        heights = jnp.exp(jax.random.uniform(jax.random.fold_in(own, axis_at), (parts,), jnp.float32, least / len(pieces), largest / len(pieces)))
        factor_of = factor_of * jnp.repeat(heights, shape[axis_at] // parts).reshape([-1 if axis == axis_at else 1 for axis in range(len(shape))])
    return factor_of


def bell_draw(stream_key, dims, scale, most, pieces=(), kind=jnp.bfloat16):
    drawn = jax.random.normal(stream_key, dims, jnp.float32) * scale
    if len(pieces) > 0:
        drawn = block_levels(stream_key, dims, pieces, -0.22, 0.18) * drawn
    return jnp.clip(drawn, min=-most, max=most).astype(kind)


def setup_inputs(seed: int = 0) -> dict:
    streams_of = jax.random.split(jax.random.key(seed), 8)
    ld_band = bell_draw(streams_of[0], (M, WMAX), WMAX ** -0.5, 0.109375, ((0, 16),), jnp.float32)
    marginal = bell_draw(streams_of[1], (M, K), 1.0, 6.0, ((0, 16), (1, 16)), jnp.float32)
    effects_init = bell_draw(streams_of[2], (M, K), 1.0, 6.0, ((0, 16), (1, 16)), jnp.float32)
    factor_in = bell_draw(streams_of[3], (K, RF), K ** -0.5, 0.09375, ((0, 16),), jnp.float32)
    factor_out = bell_draw(streams_of[4], (K, RF), RF ** -0.5, 0.375, ((0, 16),), jnp.float32)
    ld_width = draw_ld_width(jax.random.fold_in(streams_of[7], 71), 0)
    ld_starts = draw_ld_starts(jax.random.fold_in(streams_of[7], 71), 0)
    return dict(ld_band=ld_band, marginal=marginal, effects_init=effects_init, factor_in=factor_in, factor_out=factor_out, ld_width=ld_width, ld_starts=ld_starts)


step_size = 0.5
shrinkage = 0.5


def row_reach(ld_width, ld_starts, row_index, total_rows):
    covered = (ld_starts[None, :] <= row_index[:, None]).astype(jnp.int32)
    following = jnp.concatenate([covered[:, 1:], jnp.zeros((covered.shape[0], 1), jnp.int32)], axis=1)
    row_width = jnp.sum((covered - following) * ld_width[None, :], axis=1)
    return jnp.minimum(row_width, total_rows - 1 - row_index)


def shear(ld_rows, reach):
    row_count, band_span = ld_rows.shape
    offsets = lax.broadcasted_iota(jnp.int32, ld_rows.shape, 1)
    masked_band = jnp.where(offsets < reach[:, None], ld_rows, jnp.zeros_like(ld_rows))
    padded = jnp.pad(masked_band, ((0, 0), (0, row_count + 1)))
    full_width = band_span + row_count
    flattened = jnp.concatenate([jnp.zeros((1,), ld_rows.dtype), padded.reshape(-1)])
    return flattened[: row_count * full_width].reshape(row_count, full_width)


def reference(ld_band, marginal, effects_init, factor_in, factor_out, ld_width, ld_starts):
    total_rows = ld_band.shape[0]
    row_count = ROWS
    band_span = ld_band.shape[1]
    full_width = band_span + row_count
    block_total = total_rows // row_count
    row_index = lax.iota(jnp.int32, total_rows)
    reach = row_reach(ld_width, ld_starts, row_index, total_rows)
    effects = effects_init
    for iteration in range(STEPS):
        padded_effects = jnp.concatenate([effects, jnp.zeros((band_span, effects.shape[1]), effects.dtype)], axis=0)

        def one_block(lower_pad, block_index):
            first_row = (block_index * row_count).astype(jnp.int32)
            ld_rows = lax.dynamic_slice_in_dim(ld_band, first_row, row_count, 0)
            reach_rows = lax.dynamic_slice_in_dim(reach, first_row, row_count, 0)
            sheared = shear(ld_rows, reach_rows)
            window = lax.dynamic_slice_in_dim(padded_effects, first_row, full_width, 0)
            own_rows = lax.dynamic_slice_in_dim(effects, first_row, row_count, 0)
            upper = jnp.dot(sheared, window, precision=lax.Precision.HIGHEST, preferred_element_type=jnp.float32)
            transposed = lax.dot_general(sheared, own_rows, (((0,), (0,)), ((), ())), precision=lax.Precision.HIGHEST, preferred_element_type=jnp.float32)
            current = lax.dynamic_slice_in_dim(lower_pad, first_row, full_width, 0)
            lower_pad = lax.dynamic_update_slice_in_dim(lower_pad, current + transposed, first_row, 0)
            return lower_pad, upper

        lower_pad, uppers = lax.scan(one_block, jnp.zeros_like(padded_effects), jnp.arange(block_total, dtype=jnp.int32))
        upper = uppers.reshape(total_rows, effects.shape[1])
        lower = lower_pad[:total_rows]
        scores = jnp.dot(effects, factor_in, precision=lax.Precision.HIGHEST, preferred_element_type=jnp.float32)
        projected = lax.dot_general(scores, factor_out, (((1,), (1,)), ((), ())), precision=lax.Precision.HIGHEST, preferred_element_type=jnp.float32)
        gradient = effects + upper + lower - marginal + shrinkage * (effects - projected)
        effects = effects - step_size * gradient
    return effects
```

```python
import jax
import jax.numpy as jnp
from jax import lax
from jax.experimental import pallas as pl
from jax.experimental.pallas import tpu as pltpu
from jax.sharding import PartitionSpec as P

STEPS = 2
MESH = pl.DeviceIdType.MESH
LANES = 128
GROUP = 16

step_size = 0.5
shrinkage = 0.5


def split(values):
    high = values.astype(jnp.bfloat16)
    low = (values - high.astype(jnp.float32)).astype(jnp.bfloat16)
    return high, low


def dot(left, right, contract=((1,), (0,))):
    return lax.dot_general(left, right, (contract, ((), ())), preferred_element_type=jnp.float32)


def kernel(
    total_rows,
    side,
    band_hbm,
    marginal_hbm,
    effects_hbm,
    factor_in_hbm,
    factor_out_hbm,
    width_ref,
    starts_ref,
    out_hbm,
    band,
    reach,
    upper,
    flipped,
    own,
    own_split,
    marginal,
    total,
    ahead,
    beside,
    chain,
    crossed,
    crossing,
    first,
    later,
    factor_in,
    factor_out,
    into_scores,
    from_scores,
    partial,
    from_x,
    over_x,
    from_y,
    over_y,
    scores,
    projected,
    load_sem,
    ahead_send,
    ahead_recv,
    beside_send,
    beside_recv,
    chain_send,
    chain_recv,
    cross_send,
    cross_recv,
    score_send,
    score_recv,
):
    rows = band.shape[0]
    span = band.shape[1]
    hops = span // (2 * rows)
    blocks = 2 * hops + 1
    device = lax.axis_index("snp")
    column = lax.axis_index("trait")
    devices = lax.axis_size("snp")
    core = lax.rem(device, 2)
    behind_id = (lax.rem(device + devices - 2, devices), column)
    ahead_id = (lax.rem(device + 2, devices), column)
    beside_id = (device + 1 - 2 * core, column)
    my_y = lax.div(column, side)
    my_x = lax.rem(column, side)

    def x_peer(offset):
        return lax.rem(my_x + offset, side)

    def y_peer(offset):
        return lax.rem(my_y + offset, side)

    def x_id(offset):
        return (device, my_y * side + x_peer(offset))

    def y_id(offset):
        return (device, y_peer(offset) * side + my_x)

    near = 2 * rows * (hops - 1)
    loads = [
        (effects_hbm.at[:, pl.ds(0, LANES)], own.at[0, 0]),
        (effects_hbm.at[:, pl.ds(LANES, LANES)], own.at[0, 1]),
        (band_hbm.at[:, pl.ds(near, span - near)], band.at[:, pl.ds(near, span - near)]),
        (band_hbm.at[:, pl.ds(0, near)], band.at[:, pl.ds(0, near)]),
        (factor_in_hbm, factor_in),
        (factor_out_hbm, factor_out),
        (marginal_hbm.at[:, pl.ds(0, LANES)], marginal.at[0]),
        (marginal_hbm.at[:, pl.ds(LANES, LANES)], marginal.at[1]),
    ]
    loading = [pltpu.make_async_copy(a, b, load_sem.at[i]) for i, (a, b) in enumerate(loads)]
    for copy in loading:
        copy.start()

    partners = [behind_id, ahead_id, beside_id]
    for offset in range(1, side):
        partners += [x_id(offset), y_id(offset)]
    barrier = pltpu.get_barrier_semaphore()
    for partner in partners:
        pl.semaphore_signal(barrier, inc=1, device_id=partner, device_id_type=MESH)
    pl.semaphore_wait(barrier, len(partners))

    def remote(source, target, send, recv, to):
        return pltpu.make_async_remote_copy(
            src_ref=source, dst_ref=target, send_sem=send, recv_sem=recv, device_id=to, device_id_type=MESH
        )

    def ahead_copy(step, half, slot):
        source = own.at[step, half] if isinstance(slot, int) and slot == 0 else ahead.at[step, half, slot - 1]
        return remote(
            source,
            ahead.at[step, half, slot],
            ahead_send.at[step, half, slot],
            ahead_recv.at[step, half, slot],
            behind_id,
        )

    def beside_copy(source, step, half, slot):
        return remote(
            source,
            beside.at[step, half, slot],
            beside_send.at[step, half, slot],
            beside_recv.at[step, half, slot],
            beside_id,
        )

    def chain_copy(step, half, slot):
        source = first.at[step, half] if slot == 0 else chain.at[step, half, slot - 1]
        return remote(
            source,
            chain.at[step, half, slot],
            chain_send.at[step, half, slot],
            chain_recv.at[step, half, slot],
            ahead_id,
        )

    def cross_copy(step, half, slot):
        return remote(
            crossing.at[step, half, slot],
            crossed.at[step, half, slot],
            cross_send.at[step, half, slot],
            cross_recv.at[step, half, slot],
            beside_id,
        )

    def send_own(step, half):
        ahead_copy(step, half, 0).start()

        @pl.when(core == 1)
        def _():
            beside_copy(own.at[step, half], step, half, 0).start()

    for half in range(2):
        loading[half].wait()
        send_own(0, half)

    def find_reach(group, carry):
        at = pl.multiple_of(group * GROUP, GROUP)
        index = lax.broadcasted_iota(jnp.int32, (GROUP, width_ref.shape[1]), 0) + (device * rows + at)
        entry = lax.broadcasted_iota(jnp.int32, index.shape, 1)
        covered = jnp.where(starts_ref[...] <= index, 1, 0)
        last = jnp.sum(covered, axis=1, keepdims=True) - 1
        width = jnp.sum(jnp.where(entry == last, width_ref[...], 0), axis=1, keepdims=True)
        limit = jnp.minimum(width, total_rows - 1 - index[:, :1])
        reach[pl.ds(at, GROUP), :] = jnp.broadcast_to(limit, (GROUP, LANES))
        return carry

    lax.fori_loop(0, rows // GROUP, find_reach, 0)

    half_rows = rows // 2
    per_block = rows // LANES

    def shear(low_block, high_block):
        for base in range(rows // LANES):
            def body(group, carry):
                shift = group * GROUP
                at = pl.multiple_of(base * LANES + shift, GROUP)
                lane = lax.broadcasted_iota(jnp.int32, (GROUP, LANES), 1)
                row = lax.broadcasted_iota(jnp.int32, (GROUP, LANES), 0)
                row8 = lax.broadcasted_iota(jnp.int32, (8, LANES), 0)
                limit = reach[pl.ds(at, GROUP), :]
                from_left = lane < row + (shift + 1)

                def turned(tile):
                    if tile < 0 or tile >= span // LANES:
                        return jnp.zeros((GROUP, LANES), jnp.float32)
                    values = band[pl.ds(at, GROUP), tile * LANES : (tile + 1) * LANES]
                    values = jnp.where(lane + tile * LANES < limit, values, 0.0)
                    parts = []
                    for top in range(0, GROUP, 8):
                        part = pltpu.roll(values[top : top + 8], shift + (top + 1), 1)
                        for bit in (1, 2, 4):
                            part = jnp.where(row8 & bit != 0, pltpu.roll(part, bit, 1), part)
                        parts.append(part)
                    return jnp.concatenate(parts, axis=0)

                left = turned(low_block * per_block - base - 1)
                for tile in range(low_block * per_block, high_block * per_block):
                    right = turned(tile - base)
                    high, low = split(jnp.where(from_left, left, right))
                    left = right
                    block, at_tile = tile // per_block, tile % per_block
                    row_half = base * LANES // half_rows
                    inner = pl.multiple_of(at - row_half * half_rows, GROUP)
                    lanes = slice(at_tile * LANES, (at_tile + 1) * LANES)
                    upper[block, row_half, 0, pl.ds(inner, GROUP), lanes] = high
                    upper[block, row_half, 1, pl.ds(inner, GROUP), lanes] = low
                return carry

            lax.fori_loop(0, LANES // GROUP, body, 0)

    unit_row = lax.broadcasted_iota(jnp.int32, (half_rows, half_rows), 0)
    unit_column = lax.broadcasted_iota(jnp.int32, (half_rows, half_rows), 1)
    unit = jnp.where(unit_row == unit_column, 1.0, 0.0).astype(jnp.bfloat16)

    def flip(block):
        for part in range(2):
            for i in range(2):
                for j in range(2):
                    tile = upper[block, j, part, :, i * half_rows : (i + 1) * half_rows]
                    turned = dot(unit, tile, ((1,), (1,))).astype(jnp.bfloat16)
                    flipped[block, i, part, :, j * half_rows : (j + 1) * half_rows] = turned

    def product(matrix, block, right, put):
        for i in range(2):
            left = matrix[block, i].reshape(rows, rows)
            found = dot(left, right)
            found = found[:, :LANES] + found[:, LANES:]
            put(i, found[:half_rows] + found[half_rows:])

    def store_to(ref):
        def put(i, values):
            ref[i * half_rows : (i + 1) * half_rows, :] = values

        return put

    def add_to(ref):
        def put(i, values):
            ref[i * half_rows : (i + 1) * half_rows, :] += values

        return put

    def joined(values):
        return jnp.concatenate(split(values), axis=1)

    def start(step, half):
        own_split[half] = joined(own[step, half])
        right = own_split[half]
        product(flipped, 2 * hops - 1, right, store_to(crossing.at[step, half, 0]))
        cross_copy(step, half, 0).start()
        product(flipped, 2 * hops, right, store_to(first.at[step, half]))

        @pl.when(core == 0)
        def _():
            cross_copy(step, half, 0).wait_recv()
            first[step, half] += crossed[step, half, 0]

        chain_copy(step, half, 0).start()

    def finish(step, half):
        last = hops - 1
        ahead_copy(step, half, last).wait_recv()

        @pl.when(core == 0)
        def _():
            beside_copy(ahead.at[step, half, last], step, half, last).start()

        product(upper, 2 * hops, joined(ahead[step, half, last]), add_to(total.at[half]))
        chain_copy(step, half, last).wait_recv()

        @pl.when(core == 1)
        def _():
            cross_copy(step, half, last).wait_recv()
            total[half] += crossed[step, half, last]

        beside_copy(own.at[step, half], step, half, last).wait_recv()
        product(upper, 2 * hops - 1, joined(beside[step, half, last]), add_to(total.at[half]))
        effects = own[step, half]
        gradient = (
            effects
            + (total[half] + chain[step, half, last])
            - marginal[half]
            + shrinkage * (effects - projected[half])
        )
        own[step + 1, half] = effects - step_size * gradient

    def arrive(step, half, slot):
        ahead_copy(step, half, slot).wait_recv()
        ahead_copy(step, half, slot + 1).start()
        beside_copy(ahead.at[step, half, slot], step, half, slot + core).start()
        chain_copy(step, half, slot).wait_recv()
        cross_copy(step, half, slot + 1 - core).wait_recv()
        chain[step, half, slot] += later[half, slot] + crossed[step, half, slot + 1 - core]
        chain_copy(step, half, slot + 1).start()

    def pass_on(step, half, slot):
        right = own_split[half]
        block = 2 * (hops - 1 - slot)
        product(flipped, block - 1, right, store_to(crossing.at[step, half, slot + 1]))
        cross_copy(step, half, slot + 1).start()
        product(flipped, block, right, store_to(later.at[half, slot]))

    def upper_parts(step, half, slot):
        product(upper, 2 * slot + 2, joined(ahead[step, half, slot]), add_to(total.at[half]))
        beside_copy(own.at[step, half], step, half, slot).wait_recv()
        product(upper, 2 * slot + 1, joined(beside[step, half, slot]), add_to(total.at[half]))

    quarter = rows // side
    piece = quarter // side
    x_rows = pl.ds(pl.multiple_of(my_x * quarter, quarter), quarter)
    y_rows = pl.ds(pl.multiple_of(my_y * piece, piece), piece)

    def score_copy(step, phase, offset):
        to_x = pl.ds(pl.multiple_of(x_peer(offset) * quarter, quarter), quarter)
        to_y = pl.ds(pl.multiple_of(y_peer(offset) * piece, piece), piece)
        source, target, to = [
            (partial.at[step, to_x], from_x.at[step, offset - 1], x_id(offset)),
            (over_x.at[step, to_y], from_y.at[step, offset - 1], y_id(offset)),
            (over_y.at[step, y_rows], over_y.at[step, y_rows], y_id(offset)),
            (over_y.at[step], scores.at[step, x_rows], x_id(offset)),
        ][phase]
        return remote(
            source, target, score_send.at[step, phase, offset - 1], score_recv.at[step, phase, offset - 1], to
        )

    def score_recv_wait(step, phase, offset):
        score_copy(step, phase, offset).wait_recv()

    def score_start(step):
        for i in range(2):
            at = slice(i * half_rows, (i + 1) * half_rows)
            found = dot(own_split[0, at], into_scores[0, 0])
            for half, part in ((0, 1), (1, 0), (1, 1)):
                found += dot(own_split[half, at], into_scores[half, part])
            partial[step, at] = found
        for offset in range(1, side):
            score_copy(step, 0, offset).start()

    def score_step(step, phase):
        for offset in range(1, side):
            score_copy(step, phase - 1, offset).wait_recv()
        if phase == 1:
            over_x[step] = partial[step, x_rows] + from_x[step, 0] + from_x[step, 1] + from_x[step, 2]
        if phase == 2:
            over_y[step, y_rows] = over_x[step, y_rows] + from_y[step, 0] + from_y[step, 1] + from_y[step, 2]
        if phase == 3:
            scores[step, x_rows] = over_y[step]
        if phase == 4:
            for i in range(2):
                at = slice(i * half_rows, (i + 1) * half_rows)
                high, low = split(scores[step, at])
                for half in range(2):
                    found = dot(high, from_scores[half], ((1,), (1,)))
                    found += dot(low, from_scores[half], ((1,), (1,)))
                    projected[half, at] = found[:, :LANES] + found[:, LANES:]
            return
        for offset in range(1, side):
            score_copy(step, phase, offset).start()

    loading[2].wait()
    shear(2 * hops - 1, 2 * hops + 1)
    flip(2 * hops - 1)
    flip(2 * hops)

    def prepare():
        loading[4].wait()
        loading[5].wait()
        for half in range(2):
            at = slice(half * LANES, (half + 1) * LANES)
            for part, values in enumerate(split(factor_in[at, :])):
                into_scores[half, part, :LANES] = values
                into_scores[half, part, LANES:] = values
            high, low = split(factor_out[at, :])
            from_scores[half, :LANES] = high
            from_scores[half, LANES:] = low
        loading[3].wait()
        shear(0, 2 * hops - 1)

        def flip_one(block, carry):
            flip(block)
            return carry

        lax.fori_loop(0, 2 * hops - 1, flip_one, 0)
        upper[0] = upper[0] + flipped[0]
        loading[6].wait()
        loading[7].wait()

    def step_body(step, carry):
        def stage(half, carry):
            @pl.when(step > 0)
            def _():
                finish(step - 1, half)

            @pl.when(step == 1)
            def _():
                send_own(step, half)

            @pl.when(step < STEPS)
            def _():
                start(step, half)

            return carry

        lax.fori_loop(0, 2, stage, 0)

        @pl.when(step == 0)
        def _():
            prepare()

        @pl.when(step < STEPS)
        def _():
            def gap(half, carry):
                pass_on(step, half, 0)
                product(upper, 0, own_split[half], store_to(total.at[half]))
                return carry

            lax.fori_loop(0, 2, gap, 0)
            score_start(step)
            for slot in range(hops - 1):
                def event(half, carry):
                    arrive(step, half, slot)
                    if slot + 1 < hops - 1:
                        pass_on(step, half, slot + 1)
                    upper_parts(step, half, slot)
                    for i in range(2):
                        @pl.when(half == i)
                        def _():
                            score_step(step, 2 * slot + i + 1)

                    return carry

                lax.fori_loop(0, 2, event, 0)

        return carry

    lax.fori_loop(0, STEPS + 1, step_body, 0)

    writes = [
        pltpu.make_async_copy(own.at[STEPS, half], out_hbm.at[:, pl.ds(half * LANES, LANES)], load_sem.at[half])
        for half in range(2)
    ]
    for copy in writes:
        copy.start()

    def drain(index, carry):
        step = lax.div(index, 2)
        half = lax.rem(index, 2)
        for slot in range(hops):
            ahead_copy(step, half, slot).wait_send()
            chain_copy(step, half, slot).wait_send()
            cross_copy(step, half, slot).wait_send()
            beside_copy(own.at[step, half], step, half, slot).wait_send()
        return carry

    lax.fori_loop(0, 2 * STEPS, drain, 0)
    for step in range(STEPS):
        for phase in range(4):
            for offset in range(1, side):
                score_copy(step, phase, offset).wait_send()
    for copy in writes:
        copy.wait()


def body(total_rows, side, ld_band, marginal, effects_init, factor_in, factor_out, ld_width, ld_starts):
    rows, span = ld_band.shape
    traits, factors = factor_in.shape
    hops = span // (2 * rows)
    blocks = 2 * hops + 1
    f32, bf16 = jnp.float32, jnp.bfloat16
    piece = (rows, LANES)
    quarter = rows // side
    dma = pltpu.SemaphoreType.DMA
    scratch = [
        pltpu.VMEM((rows, span), f32),
        pltpu.VMEM((rows, LANES), jnp.int32),
        pltpu.VMEM((blocks, 2, 2, rows // 2, rows), bf16),
        pltpu.VMEM((blocks, 2, 2, rows // 2, rows), bf16),
        pltpu.VMEM((STEPS + 1, 2) + piece, f32),
        pltpu.VMEM((2, rows, 2 * LANES), bf16),
        pltpu.VMEM((2,) + piece, f32),
        pltpu.VMEM((2,) + piece, f32),
        pltpu.VMEM((STEPS, 2, hops) + piece, f32),
        pltpu.VMEM((STEPS, 2, hops) + piece, f32),
        pltpu.VMEM((STEPS, 2, hops) + piece, f32),
        pltpu.VMEM((STEPS, 2, hops) + piece, f32),
        pltpu.VMEM((STEPS, 2, hops) + piece, f32),
        pltpu.VMEM((STEPS, 2) + piece, f32),
        pltpu.VMEM((2, hops - 1) + piece, f32),
        pltpu.VMEM((traits, factors), f32),
        pltpu.VMEM((traits, factors), f32),
        pltpu.VMEM((2, 2, 2 * LANES, factors), bf16),
        pltpu.VMEM((2, 2 * LANES, factors), bf16),
        pltpu.VMEM((STEPS, rows, factors), f32),
        pltpu.VMEM((STEPS, side - 1, quarter, factors), f32),
        pltpu.VMEM((STEPS, quarter, factors), f32),
        pltpu.VMEM((STEPS, side - 1, quarter // side, factors), f32),
        pltpu.VMEM((STEPS, quarter, factors), f32),
        pltpu.VMEM((STEPS, rows, factors), f32),
        pltpu.VMEM((2,) + piece, f32),
        dma((8,)),
    ]
    scratch += [dma((STEPS, 2, hops)) for _ in range(8)]
    scratch += [dma((STEPS, 4, side - 1)) for _ in range(2)]

    def call(*refs):
        kernel(total_rows, side, *refs)

    whole = pl.BlockSpec(memory_space=pl.ANY)
    table = pl.BlockSpec(memory_space=pltpu.VMEM)
    return pl.pallas_call(
        call,
        name="fit",
        out_shape=jax.ShapeDtypeStruct(effects_init.shape, f32),
        in_specs=[whole] * 5 + [table] * 2,
        out_specs=whole,
        scratch_shapes=scratch,
        compiler_params=pltpu.CompilerParams(
            collective_id=0, has_side_effects=True, vmem_limit_bytes=60 * 1024 * 1024
        ),
    )(ld_band, marginal, effects_init, factor_in, factor_out, ld_width[None, :], ld_starts[None, :])


def solution(mesh):
    side = 4
    total_rows = mesh.shape["snp"] * 512

    def run(*args):
        return body(total_rows, side, *args)

    return jax.shard_map(
        run,
        mesh=mesh,
        in_specs=(
            P("snp", None),
            P("snp", "trait"),
            P("snp", "trait"),
            P("trait", None),
            P("trait", None),
            P(),
            P(),
        ),
        out_specs=P("snp", "trait"),
        check_vma=False,
    )
```

```python
import jax
import jax.numpy as jnp
from jax import lax
from jax.experimental import pallas as pl
from jax.experimental.pallas import tpu as pltpu
from jax.sharding import PartitionSpec as P

STEPS = 2
MESH = pl.DeviceIdType.MESH
LANES = 128
GROUP = 16

step_size = 0.5
shrinkage = 0.5


def split(values):
    high = values.astype(jnp.bfloat16)
    low = (values - high.astype(jnp.float32)).astype(jnp.bfloat16)
    return high, low


def dot(left, right, contract=((1,), (0,))):
    return lax.dot_general(left, right, (contract, ((), ())), preferred_element_type=jnp.float32)


def kernel(
    total_rows,
    side,
    band_hbm,
    marginal_hbm,
    effects_hbm,
    factor_in_hbm,
    factor_out_hbm,
    width_ref,
    starts_ref,
    out_hbm,
    band,
    reach,
    upper,
    own,
    own_split,
    own_turned,
    marginal,
    total,
    ahead,
    beside,
    chain,
    crossed,
    crossing,
    first,
    later,
    home,
    factor_in,
    factor_out,
    into_scores,
    from_scores,
    partial,
    from_x,
    over_x,
    from_y,
    over_y,
    scores,
    projected,
    load_sem,
    ahead_send,
    ahead_recv,
    beside_send,
    beside_recv,
    chain_send,
    chain_recv,
    cross_send,
    cross_recv,
    score_send,
    score_recv,
):
    rows = band.shape[0]
    span = band.shape[1]
    hops = span // (2 * rows)
    blocks = 2 * hops + 1
    device = lax.axis_index("snp")
    column = lax.axis_index("trait")
    devices = lax.axis_size("snp")
    core = lax.rem(device, 2)
    behind_id = (lax.rem(device + devices - 2, devices), column)
    ahead_id = (lax.rem(device + 2, devices), column)
    beside_id = (device + 1 - 2 * core, column)
    my_y = lax.div(column, side)
    my_x = lax.rem(column, side)

    def x_peer(offset):
        return lax.rem(my_x + offset, side)

    def y_peer(offset):
        return lax.rem(my_y + offset, side)

    def x_id(offset):
        return (device, my_y * side + x_peer(offset))

    def y_id(offset):
        return (device, y_peer(offset) * side + my_x)

    near = 2 * rows * (hops - 1)
    loads = [
        (effects_hbm.at[:, pl.ds(0, LANES)], own.at[0, 0]),
        (effects_hbm.at[:, pl.ds(LANES, LANES)], own.at[0, 1]),
        (band_hbm.at[:, pl.ds(near, span - near)], band.at[:, pl.ds(near, span - near)]),
        (band_hbm.at[:, pl.ds(0, near)], band.at[:, pl.ds(0, near)]),
        (factor_in_hbm, factor_in),
        (factor_out_hbm, factor_out),
        (marginal_hbm.at[:, pl.ds(0, LANES)], marginal.at[0]),
        (marginal_hbm.at[:, pl.ds(LANES, LANES)], marginal.at[1]),
    ]
    loading = [pltpu.make_async_copy(a, b, load_sem.at[i]) for i, (a, b) in enumerate(loads)]
    for copy in loading:
        copy.start()

    partners = [behind_id, ahead_id, beside_id]
    for offset in range(1, side):
        partners += [x_id(offset), y_id(offset)]
    barrier = pltpu.get_barrier_semaphore()
    for partner in partners:
        pl.semaphore_signal(barrier, inc=1, device_id=partner, device_id_type=MESH)
    pl.semaphore_wait(barrier, len(partners))

    def remote(source, target, send, recv, to):
        return pltpu.make_async_remote_copy(
            src_ref=source, dst_ref=target, send_sem=send, recv_sem=recv, device_id=to, device_id_type=MESH
        )

    def ahead_copy(step, half, slot, source=None):
        if source is None:
            source = own.at[step, half] if slot == 0 else ahead.at[step, half, slot - 1]
        return remote(
            source,
            ahead.at[step, half, slot],
            ahead_send.at[step, half, slot],
            ahead_recv.at[step, half, slot],
            behind_id,
        )

    def beside_copy(source, step, half, slot):
        return remote(
            source,
            beside.at[step, half, slot],
            beside_send.at[step, half, slot],
            beside_recv.at[step, half, slot],
            beside_id,
        )

    def chain_copy(step, half, slot):
        source = first.at[step, half] if slot == 0 else chain.at[step, half, slot - 1]
        return remote(
            source,
            chain.at[step, half, slot],
            chain_send.at[step, half, slot],
            chain_recv.at[step, half, slot],
            ahead_id,
        )

    def cross_copy(step, half, slot):
        return remote(
            crossing.at[step, half, slot],
            crossed.at[step, half, slot],
            cross_send.at[step, half, slot],
            cross_recv.at[step, half, slot],
            beside_id,
        )

    def send_own(step, half):
        ahead_copy(step, half, 0).start()

        @pl.when(core == 1)
        def _():
            beside_copy(own.at[step, half], step, half, 0).start()

    for half in range(2):
        source = effects_hbm.at[:, pl.ds(half * LANES, LANES)]
        ahead_copy(0, half, 0, source).start()

        @pl.when(core == 1)
        def _():
            beside_copy(source, 0, half, 0).start()

    def find_reach(group, carry):
        at = pl.multiple_of(group * GROUP, GROUP)
        index = lax.broadcasted_iota(jnp.int32, (GROUP, width_ref.shape[1]), 0) + (device * rows + at)
        entry = lax.broadcasted_iota(jnp.int32, index.shape, 1)
        covered = jnp.where(starts_ref[...] <= index, 1, 0)
        last = jnp.sum(covered, axis=1, keepdims=True) - 1
        width = jnp.sum(jnp.where(entry == last, width_ref[...], 0), axis=1, keepdims=True)
        limit = jnp.minimum(width, total_rows - 1 - index[:, :1])
        reach[pl.ds(at, GROUP), :] = jnp.broadcast_to(limit, (GROUP, LANES))
        return carry

    lax.fori_loop(0, rows // GROUP, find_reach, 0)

    half_rows = rows // 2
    per_block = rows // LANES

    def shear(low_block, high_block):
        for base in range(rows // LANES):
            def body(group, carry):
                shift = group * GROUP
                at = pl.multiple_of(base * LANES + shift, GROUP)
                lane = lax.broadcasted_iota(jnp.int32, (GROUP, LANES), 1)
                row = lax.broadcasted_iota(jnp.int32, (GROUP, LANES), 0)
                row8 = lax.broadcasted_iota(jnp.int32, (8, LANES), 0)
                limit = reach[pl.ds(at, GROUP), :]
                from_left = lane < row + (shift + 1)

                def turned(tile):
                    if tile < 0 or tile >= span // LANES:
                        return jnp.zeros((GROUP, LANES), jnp.float32)
                    values = band[pl.ds(at, GROUP), tile * LANES : (tile + 1) * LANES]
                    values = jnp.where(lane + tile * LANES < limit, values, 0.0)
                    parts = []
                    for top in range(0, GROUP, 8):
                        part = pltpu.roll(values[top : top + 8], shift + (top + 1), 1)
                        for bit in (1, 2, 4):
                            part = jnp.where(row8 & bit != 0, pltpu.roll(part, bit, 1), part)
                        parts.append(part)
                    return jnp.concatenate(parts, axis=0)

                left = turned(low_block * per_block - base - 1)
                for tile in range(low_block * per_block, high_block * per_block):
                    right = turned(tile - base)
                    high, low = split(jnp.where(from_left, left, right))
                    left = right
                    block, at_tile = tile // per_block, tile % per_block
                    row_half = base * LANES // half_rows
                    inner = pl.multiple_of(at - row_half * half_rows, GROUP)
                    lanes = slice(at_tile * LANES, (at_tile + 1) * LANES)
                    upper[block, row_half, 0, pl.ds(inner, GROUP), lanes] = high
                    upper[block, row_half, 1, pl.ds(inner, GROUP), lanes] = low
                return carry

            lax.fori_loop(0, LANES // GROUP, body, 0)

    def product(block, right, put):
        for i in range(2):
            found = dot(upper[block, i].reshape(rows, rows), right)
            found = found[:, :LANES] + found[:, LANES:]
            put(i, found[:half_rows] + found[half_rows:])

    def store_to(ref):
        def put(i, values):
            ref[i * half_rows : (i + 1) * half_rows, :] = values

        return put

    def add_to(ref):
        def put(i, values):
            ref[i * half_rows : (i + 1) * half_rows, :] += values

        return put

    def lower_part(block, half, ref):
        for i in range(2):
            lanes = slice(i * half_rows, (i + 1) * half_rows)
            right = upper[block, :, :, :, lanes].reshape(2 * rows, half_rows)
            found = dot(own_turned[half], right)
            ref[:, lanes] = found[:LANES] + found[LANES:]

    def joined(values):
        return jnp.concatenate(split(values), axis=1)

    def take_own(step, half):
        values = own[step, half]
        own_split[half] = joined(values)
        for part, turned in enumerate(split(values.T)):
            for i in range(2):
                piece = turned[:, i * half_rows : (i + 1) * half_rows]
                for copy in range(2):
                    at = (2 * i + copy) * half_rows
                    own_turned[half, part * LANES : (part + 1) * LANES, at : at + half_rows] = piece

    def start(step, half):
        lower_part(2 * hops - 1, half, crossing.at[step, half, 0])
        cross_copy(step, half, 0).start()
        lower_part(2 * hops, half, first.at[step, half])

        @pl.when(core == 0)
        def _():
            cross_copy(step, half, 0).wait_recv()
            first[step, half] += crossed[step, half, 0]

        chain_copy(step, half, 0).start()

    def finish(step, half):
        last = hops - 1
        ahead_copy(step, half, last).wait_recv()

        @pl.when(core == 0)
        def _():
            beside_copy(ahead.at[step, half, last], step, half, last).start()

        product(2 * hops, joined(ahead[step, half, last]), add_to(total.at[half]))

        @pl.when(core == 1)
        def _():
            cross_copy(step, half, last).wait_recv()
            home[half] += crossed[step, half, last]

        chain_copy(step, half, last).wait_recv()
        total[half] += (home[half] + chain[step, half, last]).T
        beside_copy(own.at[step, half], step, half, last).wait_recv()
        product(2 * hops - 1, joined(beside[step, half, last]), add_to(total.at[half]))
        effects = own[step, half]
        gradient = effects + total[half] - marginal[half] + shrinkage * (effects - projected[half])
        own[step + 1, half] = effects - step_size * gradient

    def arrive(step, half, slot):
        ahead_copy(step, half, slot).wait_recv()
        ahead_copy(step, half, slot + 1).start()
        beside_copy(ahead.at[step, half, slot], step, half, slot + core).start()
        chain_copy(step, half, slot).wait_recv()
        cross_copy(step, half, slot + 1 - core).wait_recv()
        chain[step, half, slot] += later[half] + crossed[step, half, slot + 1 - core]
        chain_copy(step, half, slot + 1).start()

    def pass_on(step, half, slot):
        block = 2 * (hops - 1 - slot)
        lower_part(block - 1, half, crossing.at[step, half, slot + 1])
        cross_copy(step, half, slot + 1).start()
        lower_part(block, half, later.at[half])

    def diagonal(half):
        lower_part(0, half, home.at[half])
        product(0, own_split[half], store_to(total.at[half]))

    def upper_parts(step, half, slot):
        product(2 * slot + 2, joined(ahead[step, half, slot]), add_to(total.at[half]))
        beside_copy(own.at[step, half], step, half, slot).wait_recv()
        product(2 * slot + 1, joined(beside[step, half, slot]), add_to(total.at[half]))

    quarter = rows // side
    piece = quarter // side
    x_rows = pl.ds(pl.multiple_of(my_x * quarter, quarter), quarter)
    y_rows = pl.ds(pl.multiple_of(my_y * piece, piece), piece)

    def score_copy(step, phase, offset):
        to_x = pl.ds(pl.multiple_of(x_peer(offset) * quarter, quarter), quarter)
        to_y = pl.ds(pl.multiple_of(y_peer(offset) * piece, piece), piece)
        source, target, to = [
            (partial.at[step, to_x], from_x.at[step, offset - 1], x_id(offset)),
            (over_x.at[step, to_y], from_y.at[step, offset - 1], y_id(offset)),
            (over_y.at[step, y_rows], over_y.at[step, y_rows], y_id(offset)),
            (over_y.at[step], scores.at[step, x_rows], x_id(offset)),
        ][phase]
        return remote(
            source, target, score_send.at[step, phase, offset - 1], score_recv.at[step, phase, offset - 1], to
        )

    def score_recv_wait(step, phase, offset):
        score_copy(step, phase, offset).wait_recv()

    def score_start(step):
        for i in range(2):
            at = slice(i * half_rows, (i + 1) * half_rows)
            found = dot(own_split[0, at], into_scores[0, 0])
            for half, part in ((0, 1), (1, 0), (1, 1)):
                found += dot(own_split[half, at], into_scores[half, part])
            partial[step, at] = found
        for offset in range(1, side):
            score_copy(step, 0, offset).start()

    def score_step(step, phase):
        for offset in range(1, side):
            score_copy(step, phase - 1, offset).wait_recv()
        if phase == 1:
            over_x[step] = partial[step, x_rows] + from_x[step, 0] + from_x[step, 1] + from_x[step, 2]
        if phase == 2:
            over_y[step, y_rows] = over_x[step, y_rows] + from_y[step, 0] + from_y[step, 1] + from_y[step, 2]
        if phase == 3:
            scores[step, x_rows] = over_y[step]
        if phase == 4:
            for i in range(2):
                at = slice(i * half_rows, (i + 1) * half_rows)
                high, low = split(scores[step, at])
                for half in range(2):
                    found = dot(high, from_scores[half], ((1,), (1,)))
                    found += dot(low, from_scores[half], ((1,), (1,)))
                    projected[half, at] = found[:, :LANES] + found[:, LANES:]
            return
        for offset in range(1, side):
            score_copy(step, phase, offset).start()

    loading[0].wait()
    loading[1].wait()
    take_own(0, 0)
    loading[2].wait()
    shear(2 * hops - 1, 2 * hops + 1)

    def set_up(step, low, high):
        @pl.when(step == 0)
        def _():
            shear(low, high)

    def step_body(step, carry):
        @pl.when(step > 0)
        def _():
            score_step(step - 1, 4)

        for half in range(2):
            @pl.when(step > 0)
            def _():
                if half == 1:
                    upper_parts(step - 1, half, 1)
                finish(step - 1, half)

            @pl.when(step == STEPS)
            def _():
                write(half).start()

            @pl.when(step == 1)
            def _():
                send_own(step, half)
                take_own(step, half)

            if half == 1:
                @pl.when(step == 0)
                def _():
                    take_own(step, half)

            @pl.when(step < STEPS)
            def _():
                start(step, half)

        @pl.when(step == 0)
        def _():
            loading[3].wait()
            shear(2 * hops - 3, 2 * hops - 1)
            loading[4].wait()
            loading[5].wait()
            for half in range(2):
                at = slice(half * LANES, (half + 1) * LANES)
                for part, values in enumerate(split(factor_in[at, :])):
                    into_scores[half, part, :LANES] = values
                    into_scores[half, part, LANES:] = values
                high, low = split(factor_out[at, :])
                from_scores[half, :LANES] = high
                from_scores[half, LANES:] = low
            loading[6].wait()
            loading[7].wait()

        @pl.when(step < STEPS)
        def _():
            pass_on(step, 0, 0)
            score_start(step)
            arrive(step, 0, 0)
            pass_on(step, 1, 0)
            set_up(step, 0, 1)
            diagonal(0)
            arrive(step, 1, 0)
            score_step(step, 1)
            set_up(step, 1, 3)
            pass_on(step, 0, 1)
            diagonal(1)
            arrive(step, 0, 1)
            score_step(step, 2)
            pass_on(step, 1, 1)
            upper_parts(step, 0, 0)
            arrive(step, 1, 1)
            score_step(step, 3)
            upper_parts(step, 1, 0)
            upper_parts(step, 0, 1)

        return carry

    def write(half):
        return pltpu.make_async_copy(
            own.at[STEPS, half], out_hbm.at[:, pl.ds(half * LANES, LANES)], load_sem.at[half]
        )

    lax.fori_loop(0, STEPS + 1, step_body, 0)

    def drain(index, carry):
        step = lax.div(index, 2)
        half = lax.rem(index, 2)
        for slot in range(hops):
            ahead_copy(step, half, slot).wait_send()
            chain_copy(step, half, slot).wait_send()
            cross_copy(step, half, slot).wait_send()
            beside_copy(own.at[step, half], step, half, slot).wait_send()
        return carry

    lax.fori_loop(0, 2 * STEPS, drain, 0)
    for step in range(STEPS):
        for phase in range(4):
            for offset in range(1, side):
                score_copy(step, phase, offset).wait_send()
    for half in range(2):
        write(half).wait()


def body(total_rows, side, ld_band, marginal, effects_init, factor_in, factor_out, ld_width, ld_starts):
    rows, span = ld_band.shape
    traits, factors = factor_in.shape
    hops = span // (2 * rows)
    blocks = 2 * hops + 1
    f32, bf16 = jnp.float32, jnp.bfloat16
    piece = (rows, LANES)
    turned = (LANES, rows)
    quarter = rows // side
    dma = pltpu.SemaphoreType.DMA
    scratch = [
        pltpu.VMEM((rows, span), f32),
        pltpu.VMEM((rows, LANES), jnp.int32),
        pltpu.VMEM((blocks, 2, 2, rows // 2, rows), bf16),
        pltpu.VMEM((STEPS + 1, 2) + piece, f32),
        pltpu.VMEM((2, rows, 2 * LANES), bf16),
        pltpu.VMEM((2, 2 * LANES, 2 * rows), bf16),
        pltpu.VMEM((2,) + piece, f32),
        pltpu.VMEM((2,) + piece, f32),
        pltpu.VMEM((STEPS, 2, hops) + piece, f32),
        pltpu.VMEM((STEPS, 2, hops) + piece, f32),
        pltpu.VMEM((STEPS, 2, hops) + turned, f32),
        pltpu.VMEM((STEPS, 2, hops) + turned, f32),
        pltpu.VMEM((STEPS, 2, hops) + turned, f32),
        pltpu.VMEM((STEPS, 2) + turned, f32),
        pltpu.VMEM((2,) + turned, f32),
        pltpu.VMEM((2,) + turned, f32),
        pltpu.VMEM((traits, factors), f32),
        pltpu.VMEM((traits, factors), f32),
        pltpu.VMEM((2, 2, 2 * LANES, factors), bf16),
        pltpu.VMEM((2, 2 * LANES, factors), bf16),
        pltpu.VMEM((STEPS, rows, factors), f32),
        pltpu.VMEM((STEPS, side - 1, quarter, factors), f32),
        pltpu.VMEM((STEPS, quarter, factors), f32),
        pltpu.VMEM((STEPS, side - 1, quarter // side, factors), f32),
        pltpu.VMEM((STEPS, quarter, factors), f32),
        pltpu.VMEM((STEPS, rows, factors), f32),
        pltpu.VMEM((2,) + piece, f32),
        dma((8,)),
    ]
    scratch += [dma((STEPS, 2, hops)) for _ in range(8)]
    scratch += [dma((STEPS, 4, side - 1)) for _ in range(2)]

    def call(*refs):
        kernel(total_rows, side, *refs)

    whole = pl.BlockSpec(memory_space=pl.ANY)
    table = pl.BlockSpec(memory_space=pltpu.VMEM)
    return pl.pallas_call(
        call,
        name="fit",
        out_shape=jax.ShapeDtypeStruct(effects_init.shape, f32),
        in_specs=[whole] * 5 + [table] * 2,
        out_specs=whole,
        scratch_shapes=scratch,
        compiler_params=pltpu.CompilerParams(
            collective_id=0, has_side_effects=True, vmem_limit_bytes=60 * 1024 * 1024
        ),
    )(ld_band, marginal, effects_init, factor_in, factor_out, ld_width[None, :], ld_starts[None, :])


def solution(mesh):
    side = 4
    total_rows = mesh.shape["snp"] * 512

    def run(*args):
        return body(total_rows, side, *args)

    return jax.shard_map(
        run,
        mesh=mesh,
        in_specs=(
            P("snp", None),
            P("snp", "trait"),
            P("snp", "trait"),
            P("trait", None),
            P("trait", None),
            P(),
            P(),
        ),
        out_specs=P("snp", "trait"),
        check_vma=False,
    )
```

```python
import jax
import jax.numpy as jnp
from jax import lax
from jax.experimental import pallas as pl
from jax.experimental.pallas import tpu as pltpu
from jax.sharding import PartitionSpec as P

STEPS = 2
MESH = pl.DeviceIdType.MESH
LANES = 128
GROUP = 16

step_size = 0.5
shrinkage = 0.5


def split(values):
    high = values.astype(jnp.bfloat16)
    low = (values - high.astype(jnp.float32)).astype(jnp.bfloat16)
    return high, low


def dot(left, right, contract=((1,), (0,))):
    return lax.dot_general(left, right, (contract, ((), ())), preferred_element_type=jnp.float32)


def kernel(
    total_rows,
    side,
    band_hbm,
    marginal_hbm,
    effects_hbm,
    factor_in_hbm,
    factor_out_hbm,
    width_hbm,
    starts_hbm,
    out_hbm,
    width,
    starts,
    band,
    reach,
    upper,
    own,
    own_split,
    own_stack,
    marginal,
    total,
    ahead,
    beside,
    chain,
    crossed,
    crossing,
    first,
    later,
    home,
    factor_in,
    factor_out,
    into_scores,
    from_scores,
    partial,
    from_x,
    over_x,
    from_y,
    over_y,
    scores,
    projected,
    load_sem,
    ahead_send,
    ahead_recv,
    beside_send,
    beside_recv,
    chain_send,
    chain_recv,
    cross_send,
    cross_recv,
    score_send,
    score_recv,
):
    rows = band.shape[0]
    span = band.shape[1]
    hops = span // (2 * rows)
    blocks = 2 * hops + 1
    device = lax.axis_index("snp")
    column = lax.axis_index("trait")
    devices = lax.axis_size("snp")
    core = lax.rem(device, 2)
    behind_id = (lax.rem(device + devices - 2, devices), column)
    ahead_id = (lax.rem(device + 2, devices), column)
    beside_id = (device + 1 - 2 * core, column)
    my_y = lax.div(column, side)
    my_x = lax.rem(column, side)

    def x_peer(offset):
        return lax.rem(my_x + offset, side)

    def y_peer(offset):
        return lax.rem(my_y + offset, side)

    def x_id(offset):
        return (device, my_y * side + x_peer(offset))

    def y_id(offset):
        return (device, y_peer(offset) * side + my_x)

    near = 2 * rows * (hops - 1)
    loads = [
        (width_hbm, width),
        (starts_hbm, starts),
        (effects_hbm.at[:, pl.ds(0, LANES)], own.at[0, 0]),
        (effects_hbm.at[:, pl.ds(LANES, LANES)], own.at[0, 1]),
        (band_hbm.at[:, pl.ds(near, span - near)], band.at[:, pl.ds(near, span - near)]),
        (band_hbm.at[:, pl.ds(0, near)], band.at[:, pl.ds(0, near)]),
        (factor_in_hbm, factor_in),
        (factor_out_hbm, factor_out),
        (marginal_hbm.at[:, pl.ds(0, LANES)], marginal.at[0]),
        (marginal_hbm.at[:, pl.ds(LANES, LANES)], marginal.at[1]),
    ]
    loading = [pltpu.make_async_copy(a, b, load_sem.at[i]) for i, (a, b) in enumerate(loads)]
    for copy in loading:
        copy.start()

    partners = [behind_id, ahead_id, beside_id]
    for offset in range(1, side):
        partners += [x_id(offset), y_id(offset)]
    barrier = pltpu.get_barrier_semaphore()
    for partner in partners:
        pl.semaphore_signal(barrier, inc=1, device_id=partner, device_id_type=MESH)
    pl.semaphore_wait(barrier, len(partners))

    def remote(source, target, send, recv, to):
        return pltpu.make_async_remote_copy(
            src_ref=source, dst_ref=target, send_sem=send, recv_sem=recv, device_id=to, device_id_type=MESH
        )

    def ahead_copy(step, half, slot, source=None):
        if source is None:
            source = own.at[step, half] if slot == 0 else ahead.at[step, half, slot - 1]
        return remote(
            source,
            ahead.at[step, half, slot],
            ahead_send.at[step, half, slot],
            ahead_recv.at[step, half, slot],
            behind_id,
        )

    def beside_copy(source, step, half, slot):
        return remote(
            source,
            beside.at[step, half, slot],
            beside_send.at[step, half, slot],
            beside_recv.at[step, half, slot],
            beside_id,
        )

    def chain_copy(step, half, slot):
        source = first.at[step, half] if slot == 0 else chain.at[step, half, slot - 1]
        return remote(
            source,
            chain.at[step, half, slot],
            chain_send.at[step, half, slot],
            chain_recv.at[step, half, slot],
            ahead_id,
        )

    def cross_copy(step, half, slot):
        return remote(
            crossing.at[step, half, slot],
            crossed.at[step, half, slot],
            cross_send.at[step, half, slot],
            cross_recv.at[step, half, slot],
            beside_id,
        )

    def send_own(step, half):
        ahead_copy(step, half, 0).start()

        @pl.when(core == 1)
        def _():
            beside_copy(own.at[step, half], step, half, 0).start()

    for half in range(2):
        source = effects_hbm.at[:, pl.ds(half * LANES, LANES)]
        ahead_copy(0, half, 0, source).start()

        @pl.when(core == 1)
        def _():
            beside_copy(source, 0, half, 0).start()

    def find_reach():
        for base in range(0, rows, LANES):
            index = lax.broadcasted_iota(jnp.int32, (LANES, width.shape[1]), 0) + (device * rows + base)
            entry = lax.broadcasted_iota(jnp.int32, index.shape, 1)
            covered = jnp.where(starts[...] <= index, 1, 0)
            last = jnp.sum(covered, axis=1, keepdims=True) - 1
            found = jnp.sum(jnp.where(entry == last, width[...], 0), axis=1, keepdims=True)
            limit = jnp.minimum(found, total_rows - 1 - index[:, :1])
            reach[base : base + LANES, :] = jnp.broadcast_to(limit, (LANES, LANES))

    half_rows = rows // 2
    per_block = rows // LANES

    def shear(low_block, high_block):
        def body(group, carry):
            shift = group * GROUP
            lane = lax.broadcasted_iota(jnp.int32, (GROUP, LANES), 1)
            row = lax.broadcasted_iota(jnp.int32, (GROUP, LANES), 0)
            row8 = lax.broadcasted_iota(jnp.int32, (8, LANES), 0)
            from_left = lane < row + (shift + 1)
            for base in range(rows // LANES):
                at = pl.multiple_of(base * LANES + shift, GROUP)
                limit = reach[pl.ds(at, GROUP), :]

                def turned(tile):
                    if tile < 0 or tile >= span // LANES:
                        return jnp.zeros((GROUP, LANES), jnp.float32)
                    values = band[pl.ds(at, GROUP), tile * LANES : (tile + 1) * LANES]
                    values = jnp.where(lane + tile * LANES < limit, values, 0.0)
                    parts = []
                    for top in range(0, GROUP, 8):
                        part = pltpu.roll(values[top : top + 8], shift + (top + 1), 1)
                        for bit in (1, 2, 4):
                            part = jnp.where(row8 & bit != 0, pltpu.roll(part, bit, 1), part)
                        parts.append(part)
                    return jnp.concatenate(parts, axis=0)

                left = turned(low_block * per_block - base - 1)
                for tile in range(low_block * per_block, high_block * per_block):
                    right = turned(tile - base)
                    high, low = split(jnp.where(from_left, left, right))
                    left = right
                    block, at_tile = tile // per_block, tile % per_block
                    row_half = base * LANES // half_rows
                    inner = pl.multiple_of(at - row_half * half_rows, GROUP)
                    lanes = slice(at_tile * LANES, (at_tile + 1) * LANES)
                    upper[block, row_half, 0, pl.ds(inner, GROUP), lanes] = high
                    upper[block, row_half, 1, pl.ds(inner, GROUP), lanes] = low
            return carry

        lax.fori_loop(0, LANES // GROUP, body, 0)

    def product(block, right, put):
        for i in range(2):
            found = dot(upper[block, i].reshape(rows, rows), right)
            found = found[:, :LANES] + found[:, LANES:]
            put(i, found[:half_rows] + found[half_rows:])

    def store_to(ref):
        def put(i, values):
            ref[i * half_rows : (i + 1) * half_rows, :] = values

        return put

    def add_to(ref):
        def put(i, values):
            ref[i * half_rows : (i + 1) * half_rows, :] += values

        return put

    def lower_part(block, half, ref):
        for i in range(2):
            lanes = slice(i * half_rows, (i + 1) * half_rows)
            left = upper[block, :, :, :, lanes].reshape(2 * rows, half_rows)
            found = dot(left, own_stack[half], ((0,), (0,)))
            ref[lanes, :] = found[:, :LANES] + found[:, LANES:]

    def joined(values):
        return jnp.concatenate(split(values), axis=1)

    def take_own(step, half):
        found = joined(own[step, half])
        own_split[half] = found
        for i in range(2):
            for copy in range(2):
                at = (2 * i + copy) * half_rows
                own_stack[half, at : at + half_rows] = found[i * half_rows : (i + 1) * half_rows]

    def start(step, half):
        lower_part(2 * hops - 1, half, crossing.at[step, half, 0])
        cross_copy(step, half, 0).start()
        lower_part(2 * hops, half, first.at[step, half])

        @pl.when(core == 0)
        def _():
            cross_copy(step, half, 0).wait_recv()
            first[step, half] += crossed[step, half, 0]

        chain_copy(step, half, 0).start()

    def finish(step, half):
        last = hops - 1
        ahead_copy(step, half, last).wait_recv()

        @pl.when(core == 0)
        def _():
            beside_copy(ahead.at[step, half, last], step, half, last).start()

        product(2 * hops, joined(ahead[step, half, last]), add_to(total.at[half]))

        @pl.when(core == 1)
        def _():
            cross_copy(step, half, last).wait_recv()
            home[half] += crossed[step, half, last]

        beside_copy(own.at[step, half], step, half, last).wait_recv()
        product(2 * hops - 1, joined(beside[step, half, last]), add_to(total.at[half]))
        chain_copy(step, half, last).wait_recv()
        effects = own[step, half]
        product_sum = total[half] + (home[half] + chain[step, half, last])
        gradient = effects + product_sum - marginal[half] + shrinkage * (effects - projected[half])
        own[step + 1, half] = effects - step_size * gradient

    def arrive_ahead(step, half, slot):
        ahead_copy(step, half, slot).wait_recv()
        ahead_copy(step, half, slot + 1).start()
        beside_copy(ahead.at[step, half, slot], step, half, slot + core).start()

    def arrive_chain(step, half, slot):
        cross_copy(step, half, slot + 1 - core).wait_recv()
        later[half] += crossed[step, half, slot + 1 - core]
        chain_copy(step, half, slot).wait_recv()
        chain[step, half, slot] += later[half]
        chain_copy(step, half, slot + 1).start()

    def pass_on(step, half, slot):
        block = 2 * (hops - 1 - slot)
        lower_part(block - 1, half, crossing.at[step, half, slot + 1])
        cross_copy(step, half, slot + 1).start()
        lower_part(block, half, later.at[half])

    def diagonal(half):
        lower_part(0, half, home.at[half])
        product(0, own_split[half], store_to(total.at[half]))

    def upper_parts(step, half, slot):
        product(2 * slot + 2, joined(ahead[step, half, slot]), add_to(total.at[half]))
        beside_copy(own.at[step, half], step, half, slot).wait_recv()
        product(2 * slot + 1, joined(beside[step, half, slot]), add_to(total.at[half]))

    quarter = rows // side
    piece = quarter // side
    x_rows = pl.ds(pl.multiple_of(my_x * quarter, quarter), quarter)
    y_rows = pl.ds(pl.multiple_of(my_y * piece, piece), piece)

    def score_copy(step, phase, offset):
        to_x = pl.ds(pl.multiple_of(x_peer(offset) * quarter, quarter), quarter)
        to_y = pl.ds(pl.multiple_of(y_peer(offset) * piece, piece), piece)
        source, target, to = [
            (partial.at[step, to_x], from_x.at[step, offset - 1], x_id(offset)),
            (over_x.at[step, to_y], from_y.at[step, offset - 1], y_id(offset)),
            (over_y.at[step, y_rows], over_y.at[step, y_rows], y_id(offset)),
            (over_y.at[step], scores.at[step, x_rows], x_id(offset)),
        ][phase]
        return remote(
            source, target, score_send.at[step, phase, offset - 1], score_recv.at[step, phase, offset - 1], to
        )

    def score_recv_wait(step, phase, offset):
        score_copy(step, phase, offset).wait_recv()

    def score_start(step):
        for i in range(2):
            at = slice(i * half_rows, (i + 1) * half_rows)
            found = dot(own_split[0, at], into_scores[0, 0])
            for half, part in ((0, 1), (1, 0), (1, 1)):
                found += dot(own_split[half, at], into_scores[half, part])
            partial[step, at] = found
        for offset in range(1, side):
            score_copy(step, 0, offset).start()

    def score_step(step, phase):
        for offset in range(1, side):
            score_copy(step, phase - 1, offset).wait_recv()
        if phase == 1:
            over_x[step] = partial[step, x_rows] + from_x[step, 0] + from_x[step, 1] + from_x[step, 2]
        if phase == 2:
            over_y[step, y_rows] = over_x[step, y_rows] + from_y[step, 0] + from_y[step, 1] + from_y[step, 2]
        if phase == 3:
            scores[step, x_rows] = over_y[step]
        if phase == 4:
            for i in range(2):
                at = slice(i * half_rows, (i + 1) * half_rows)
                high, low = split(scores[step, at])
                for half in range(2):
                    found = dot(high, from_scores[half], ((1,), (1,)))
                    found += dot(low, from_scores[half], ((1,), (1,)))
                    projected[half, at] = found[:, :LANES] + found[:, LANES:]
            return
        for offset in range(1, side):
            score_copy(step, phase, offset).start()

    loading[0].wait()
    loading[1].wait()
    find_reach()
    loading[2].wait()
    loading[3].wait()
    take_own(0, 0)
    loading[4].wait()
    shear(2 * hops - 1, 2 * hops + 1)

    def set_up(step, low, high):
        @pl.when(step == 0)
        def _():
            for block in range(high - 1, low - 1, -1):
                shear(block, block + 1)

    def set_up_far(step):
        @pl.when(step == 0)
        def _():
            loading[5].wait()
            shear(2 * hops - 2, 2 * hops - 1)
            shear(2 * hops - 3, 2 * hops - 2)

    def set_up_factors(step):
        @pl.when(step == 0)
        def _():
            loading[6].wait()
            loading[7].wait()
            for half in range(2):
                at = slice(half * LANES, (half + 1) * LANES)
                for part, values in enumerate(split(factor_in[at, :])):
                    into_scores[half, part, :LANES] = values
                    into_scores[half, part, LANES:] = values
                high, low = split(factor_out[at, :])
                from_scores[half, :LANES] = high
                from_scores[half, LANES:] = low
            loading[8].wait()
            loading[9].wait()

    def step_body(step, carry):
        @pl.when(step > 0)
        def _():
            score_step(step - 1, 4)

        for half in range(2):
            @pl.when(step > 0)
            def _():
                if half == 1:
                    upper_parts(step - 1, half, 1)
                finish(step - 1, half)

            @pl.when(step == STEPS)
            def _():
                write(half).start()

            @pl.when(step == 1)
            def _():
                send_own(step, half)
                take_own(step, half)

            if half == 1:
                @pl.when(step == 0)
                def _():
                    take_own(step, half)

            @pl.when(step < STEPS)
            def _():
                start(step, half)

        @pl.when(step < STEPS)
        def _():
            arrive_ahead(step, 0, 0)
            set_up_far(step)
            pass_on(step, 0, 0)
            arrive_chain(step, 0, 0)
            arrive_ahead(step, 1, 0)
            pass_on(step, 1, 0)
            set_up_factors(step)
            score_start(step)
            arrive_chain(step, 1, 0)
            set_up(step, 1, 3)
            arrive_ahead(step, 0, 1)
            pass_on(step, 0, 1)
            arrive_chain(step, 0, 1)
            score_step(step, 1)
            arrive_ahead(step, 1, 1)
            pass_on(step, 1, 1)
            set_up(step, 0, 1)
            diagonal(0)
            arrive_chain(step, 1, 1)
            score_step(step, 2)
            diagonal(1)
            upper_parts(step, 0, 0)
            upper_parts(step, 1, 0)
            score_step(step, 3)
            upper_parts(step, 0, 1)

        return carry

    def write(half):
        return pltpu.make_async_copy(
            own.at[STEPS, half], out_hbm.at[:, pl.ds(half * LANES, LANES)], load_sem.at[half]
        )

    lax.fori_loop(0, STEPS + 1, step_body, 0)

    def drain(index, carry):
        step = lax.div(index, 2)
        half = lax.rem(index, 2)
        for slot in range(hops):
            ahead_copy(step, half, slot).wait_send()
            chain_copy(step, half, slot).wait_send()
            cross_copy(step, half, slot).wait_send()
            beside_copy(own.at[step, half], step, half, slot).wait_send()
        return carry

    lax.fori_loop(0, 2 * STEPS, drain, 0)
    for step in range(STEPS):
        for phase in range(4):
            for offset in range(1, side):
                score_copy(step, phase, offset).wait_send()
    for half in range(2):
        write(half).wait()


def body(total_rows, side, ld_band, marginal, effects_init, factor_in, factor_out, ld_width, ld_starts):
    rows, span = ld_band.shape
    traits, factors = factor_in.shape
    hops = span // (2 * rows)
    blocks = 2 * hops + 1
    f32, bf16 = jnp.float32, jnp.bfloat16
    piece = (rows, LANES)
    quarter = rows // side
    dma = pltpu.SemaphoreType.DMA
    scratch = [
        pltpu.VMEM((1,) + ld_width.shape, jnp.int32),
        pltpu.VMEM((1,) + ld_starts.shape, jnp.int32),
        pltpu.VMEM((rows, span), f32),
        pltpu.VMEM((rows, LANES), jnp.int32),
        pltpu.VMEM((blocks, 2, 2, rows // 2, rows), bf16),
        pltpu.VMEM((STEPS + 1, 2) + piece, f32),
        pltpu.VMEM((2, rows, 2 * LANES), bf16),
        pltpu.VMEM((2, 2 * rows, 2 * LANES), bf16),
        pltpu.VMEM((2,) + piece, f32),
        pltpu.VMEM((2,) + piece, f32),
        pltpu.VMEM((STEPS, 2, hops) + piece, f32),
        pltpu.VMEM((STEPS, 2, hops) + piece, f32),
        pltpu.VMEM((STEPS, 2, hops) + piece, f32),
        pltpu.VMEM((STEPS, 2, hops) + piece, f32),
        pltpu.VMEM((STEPS, 2, hops) + piece, f32),
        pltpu.VMEM((STEPS, 2) + piece, f32),
        pltpu.VMEM((2,) + piece, f32),
        pltpu.VMEM((2,) + piece, f32),
        pltpu.VMEM((traits, factors), f32),
        pltpu.VMEM((traits, factors), f32),
        pltpu.VMEM((2, 2, 2 * LANES, factors), bf16),
        pltpu.VMEM((2, 2 * LANES, factors), bf16),
        pltpu.VMEM((STEPS, rows, factors), f32),
        pltpu.VMEM((STEPS, side - 1, quarter, factors), f32),
        pltpu.VMEM((STEPS, quarter, factors), f32),
        pltpu.VMEM((STEPS, side - 1, quarter // side, factors), f32),
        pltpu.VMEM((STEPS, quarter, factors), f32),
        pltpu.VMEM((STEPS, rows, factors), f32),
        pltpu.VMEM((2,) + piece, f32),
        dma((10,)),
    ]
    scratch += [dma((STEPS, 2, hops)) for _ in range(8)]
    scratch += [dma((STEPS, 4, side - 1)) for _ in range(2)]

    def call(*refs):
        kernel(total_rows, side, *refs)

    whole = pl.BlockSpec(memory_space=pl.ANY)
    return pl.pallas_call(
        call,
        name="fit",
        out_shape=jax.ShapeDtypeStruct(effects_init.shape, f32),
        in_specs=[whole] * 7,
        out_specs=whole,
        scratch_shapes=scratch,
        compiler_params=pltpu.CompilerParams(
            collective_id=0, has_side_effects=True, vmem_limit_bytes=60 * 1024 * 1024
        ),
    )(ld_band, marginal, effects_init, factor_in, factor_out, ld_width[None, :], ld_starts[None, :])


def solution(mesh):
    side = 4
    total_rows = mesh.shape["snp"] * 512

    def run(*args):
        return body(total_rows, side, *args)

    return jax.shard_map(
        run,
        mesh=mesh,
        in_specs=(
            P("snp", None),
            P("snp", "trait"),
            P("snp", "trait"),
            P("trait", None),
            P("trait", None),
            P(),
            P(),
        ),
        out_specs=P("snp", "trait"),
        check_vma=False,
    )
```

```python
import jax
import jax.numpy as jnp
from jax import lax
from jax.experimental import pallas as pl
from jax.experimental.pallas import tpu as pltpu
from jax.sharding import PartitionSpec as P

STEPS = 2
MESH = pl.DeviceIdType.MESH
LANES = 128
GROUP = 16

step_size = 0.5
shrinkage = 0.5


def split(values):
    high = values.astype(jnp.bfloat16)
    low = (values - high.astype(jnp.float32)).astype(jnp.bfloat16)
    return high, low


def dot(left, right, contract=((1,), (0,))):
    return lax.dot_general(left, right, (contract, ((), ())), preferred_element_type=jnp.float32)


def kernel(
    total_rows,
    side,
    band_hbm,
    marginal_hbm,
    effects_hbm,
    factor_in_hbm,
    factor_out_hbm,
    width_hbm,
    starts_hbm,
    out_hbm,
    width,
    starts,
    band,
    reach,
    upper,
    own,
    own_split,
    own_stack,
    marginal,
    total,
    ahead,
    beside,
    chain,
    crossed,
    crossing,
    first,
    later,
    home,
    factor_in,
    factor_out,
    into_scores,
    from_scores,
    partial,
    from_along,
    over_along,
    from_across,
    over_both,
    scores,
    projected,
    load_sem,
    ahead_send,
    ahead_recv,
    beside_send,
    beside_recv,
    chain_send,
    chain_recv,
    cross_send,
    cross_recv,
    score_send,
    score_recv,
):
    rows = band.shape[0]
    span = band.shape[1]
    hops = span // (2 * rows)
    blocks = 2 * hops + 1
    device = lax.axis_index("snp")
    column = lax.axis_index("trait")
    devices = lax.axis_size("snp")
    core = lax.rem(device, 2)
    behind_id = (lax.rem(device + devices - 2, devices), column)
    ahead_id = (lax.rem(device + 2, devices), column)
    beside_id = (device + 1 - 2 * core, column)
    my_y = lax.div(column, side)
    my_x = lax.rem(column, side)

    def x_peer(offset):
        return lax.rem(my_x + offset, side)

    def y_peer(offset):
        return lax.rem(my_y + offset, side)

    def x_id(offset):
        return (device, my_y * side + x_peer(offset))

    def y_id(offset):
        return (device, y_peer(offset) * side + my_x)

    near = 2 * rows * (hops - 1)
    loads = [
        (width_hbm, width),
        (starts_hbm, starts),
        (effects_hbm.at[:, pl.ds(0, LANES)], own.at[0, 0]),
        (effects_hbm.at[:, pl.ds(LANES, LANES)], own.at[0, 1]),
        (band_hbm.at[:, pl.ds(near, span - near)], band.at[:, pl.ds(near, span - near)]),
        (band_hbm.at[:, pl.ds(0, near)], band.at[:, pl.ds(0, near)]),
        (factor_in_hbm, factor_in),
        (factor_out_hbm, factor_out),
        (marginal_hbm.at[:, pl.ds(0, LANES)], marginal.at[0]),
        (marginal_hbm.at[:, pl.ds(LANES, LANES)], marginal.at[1]),
    ]
    loading = [pltpu.make_async_copy(a, b, load_sem.at[i]) for i, (a, b) in enumerate(loads)]
    for copy in loading:
        copy.start()

    partners = [behind_id, ahead_id, beside_id]
    for offset in range(1, side):
        partners += [x_id(offset), y_id(offset)]
    barrier = pltpu.get_barrier_semaphore()
    for partner in partners:
        pl.semaphore_signal(barrier, inc=1, device_id=partner, device_id_type=MESH)
    pl.semaphore_wait(barrier, len(partners))

    def remote(source, target, send, recv, to):
        return pltpu.make_async_remote_copy(
            src_ref=source, dst_ref=target, send_sem=send, recv_sem=recv, device_id=to, device_id_type=MESH
        )

    def ahead_copy(step, half, slot, source=None):
        if source is None:
            source = own.at[step, half] if slot == 0 else ahead.at[step, half, slot - 1]
        return remote(
            source,
            ahead.at[step, half, slot],
            ahead_send.at[step, half, slot],
            ahead_recv.at[step, half, slot],
            behind_id,
        )

    def beside_copy(source, step, half, slot):
        return remote(
            source,
            beside.at[step, half, slot],
            beside_send.at[step, half, slot],
            beside_recv.at[step, half, slot],
            beside_id,
        )

    def chain_copy(step, half, slot):
        source = first.at[step, half] if slot == 0 else chain.at[step, half, slot - 1]
        return remote(
            source,
            chain.at[step, half, slot],
            chain_send.at[step, half, slot],
            chain_recv.at[step, half, slot],
            ahead_id,
        )

    def cross_copy(step, half, slot):
        return remote(
            crossing.at[step, half, slot],
            crossed.at[step, half, slot],
            cross_send.at[step, half, slot],
            cross_recv.at[step, half, slot],
            beside_id,
        )

    def send_own(step, half):
        ahead_copy(step, half, 0).start()

        @pl.when(core == 1)
        def _():
            beside_copy(own.at[step, half], step, half, 0).start()

    for half in range(2):
        source = effects_hbm.at[:, pl.ds(half * LANES, LANES)]
        ahead_copy(0, half, 0, source).start()

        @pl.when(core == 1)
        def _():
            beside_copy(source, 0, half, 0).start()

    def find_reach():
        for base in range(0, rows, LANES):
            index = lax.broadcasted_iota(jnp.int32, (LANES, width.shape[1]), 0) + (device * rows + base)
            entry = lax.broadcasted_iota(jnp.int32, index.shape, 1)
            covered = jnp.where(starts[...] <= index, 1, 0)
            last = jnp.sum(covered, axis=1, keepdims=True) - 1
            found = jnp.sum(jnp.where(entry == last, width[...], 0), axis=1, keepdims=True)
            limit = jnp.minimum(found, total_rows - 1 - index[:, :1])
            reach[base : base + LANES, :] = jnp.broadcast_to(limit, (LANES, LANES))

    half_rows = rows // 2
    per_block = rows // LANES

    def shear(low_block, high_block):
        def body(group, carry):
            shift = group * GROUP
            lane = lax.broadcasted_iota(jnp.int32, (GROUP, LANES), 1)
            row = lax.broadcasted_iota(jnp.int32, (GROUP, LANES), 0)
            row8 = lax.broadcasted_iota(jnp.int32, (8, LANES), 0)
            from_left = lane < row + (shift + 1)
            for base in range(rows // LANES):
                at = pl.multiple_of(base * LANES + shift, GROUP)
                limit = reach[pl.ds(at, GROUP), :]

                def turned(tile):
                    if tile < 0 or tile >= span // LANES:
                        return jnp.zeros((GROUP, LANES), jnp.float32)
                    values = band[pl.ds(at, GROUP), tile * LANES : (tile + 1) * LANES]
                    values = jnp.where(lane + tile * LANES < limit, values, 0.0)
                    parts = []
                    for top in range(0, GROUP, 8):
                        part = pltpu.roll(values[top : top + 8], shift + (top + 1), 1)
                        for bit in (1, 2, 4):
                            part = jnp.where(row8 & bit != 0, pltpu.roll(part, bit, 1), part)
                        parts.append(part)
                    return jnp.concatenate(parts, axis=0)

                left = turned(low_block * per_block - base - 1)
                for tile in range(low_block * per_block, high_block * per_block):
                    right = turned(tile - base)
                    high, low = split(jnp.where(from_left, left, right))
                    left = right
                    block, at_tile = tile // per_block, tile % per_block
                    row_half = base * LANES // half_rows
                    inner = pl.multiple_of(at - row_half * half_rows, GROUP)
                    lanes = slice(at_tile * LANES, (at_tile + 1) * LANES)
                    upper[block, row_half, 0, pl.ds(inner, GROUP), lanes] = high
                    upper[block, row_half, 1, pl.ds(inner, GROUP), lanes] = low
            return carry

        lax.fori_loop(0, LANES // GROUP, body, 0)

    def product(block, right, put):
        for i in range(2):
            found = dot(upper[block, i].reshape(rows, rows), right)
            found = found[:, :LANES] + found[:, LANES:]
            put(i, found[:half_rows] + found[half_rows:])

    def store_to(ref):
        def put(i, values):
            ref[i * half_rows : (i + 1) * half_rows, :] = values

        return put

    def add_to(ref):
        def put(i, values):
            ref[i * half_rows : (i + 1) * half_rows, :] += values

        return put

    def lower_part(block, half, ref):
        for i in range(2):
            lanes = slice(i * half_rows, (i + 1) * half_rows)
            left = upper[block, :, :, :, lanes].reshape(2 * rows, half_rows)
            found = dot(left, own_stack[half], ((0,), (0,)))
            ref[lanes, :] = found[:, :LANES] + found[:, LANES:]

    def joined(values):
        return jnp.concatenate(split(values), axis=1)

    def take_own(step, half):
        found = joined(own[step, half])
        own_split[half] = found
        for i in range(2):
            for copy in range(2):
                at = (2 * i + copy) * half_rows
                own_stack[half, at : at + half_rows] = found[i * half_rows : (i + 1) * half_rows]

    def start(step, half):
        lower_part(2 * hops - 1, half, crossing.at[step, half, 0])
        cross_copy(step, half, 0).start()
        lower_part(2 * hops, half, first.at[step, half])

        @pl.when(core == 0)
        def _():
            cross_copy(step, half, 0).wait_recv()
            first[step, half] += crossed[step, half, 0]

        chain_copy(step, half, 0).start()

    def finish_ahead(step, half):
        last = hops - 1
        ahead_copy(step, half, last).wait_recv()

        @pl.when(core == 0)
        def _():
            beside_copy(ahead.at[step, half, last], step, half, last).start()

        product(2 * hops, joined(ahead[step, half, last]), add_to(total.at[half]))

        @pl.when(core == 1)
        def _():
            cross_copy(step, half, last).wait_recv()
            home[half] += crossed[step, half, last]

        beside_copy(own.at[step, half], step, half, last).wait_recv()
        product(2 * hops - 1, joined(beside[step, half, last]), add_to(total.at[half]))

    def finish_chain(step, half):
        last = hops - 1
        chain_copy(step, half, last).wait_recv()
        effects = own[step, half]
        product_sum = total[half] + (home[half] + chain[step, half, last])
        gradient = effects + product_sum - marginal[half] + shrinkage * (effects - projected[half])
        own[step + 1, half] = effects - step_size * gradient

    def arrive_ahead(step, half, slot):
        ahead_copy(step, half, slot).wait_recv()
        ahead_copy(step, half, slot + 1).start()
        beside_copy(ahead.at[step, half, slot], step, half, slot + core).start()

    def arrive_chain(step, half, slot):
        cross_copy(step, half, slot + 1 - core).wait_recv()
        later[half] += crossed[step, half, slot + 1 - core]
        chain_copy(step, half, slot).wait_recv()
        chain[step, half, slot] += later[half]
        chain_copy(step, half, slot + 1).start()

    def pass_on(step, half, slot):
        block = 2 * (hops - 1 - slot)
        lower_part(block - 1, half, crossing.at[step, half, slot + 1])
        cross_copy(step, half, slot + 1).start()
        lower_part(block, half, later.at[half])

    def diagonal(half):
        lower_part(0, half, home.at[half])
        product(0, own_split[half], store_to(total.at[half]))

    def upper_parts(step, half, slot):
        product(2 * slot + 2, joined(ahead[step, half, slot]), add_to(total.at[half]))
        beside_copy(own.at[step, half], step, half, slot).wait_recv()
        product(2 * slot + 1, joined(beside[step, half, slot]), add_to(total.at[half]))

    quarter = half_rows // side
    piece = quarter // side
    places = (my_x, my_y)
    peers = (x_peer, y_peer)
    ids = (x_id, y_id)

    def stripe(group, index):
        return pl.ds(pl.multiple_of(group * half_rows + index * quarter, quarter), quarter)

    def strip(index):
        return pl.ds(pl.multiple_of(index * piece, piece), piece)

    def score_copy(step, group, phase, offset):
        along, across = group, 1 - group
        source, target, to = [
            (
                partial.at[step, stripe(group, peers[along](offset))],
                from_along.at[step, group, offset - 1],
                ids[along](offset),
            ),
            (
                over_along.at[step, group, strip(peers[across](offset))],
                from_across.at[step, group, offset - 1],
                ids[across](offset),
            ),
            (
                over_both.at[step, group, strip(places[across])],
                over_both.at[step, group, strip(places[across])],
                ids[across](offset),
            ),
            (
                over_both.at[step, group],
                scores.at[step, stripe(group, places[along])],
                ids[along](offset),
            ),
        ][phase]
        return remote(
            source,
            target,
            score_send.at[step, group, phase, offset - 1],
            score_recv.at[step, group, phase, offset - 1],
            to,
        )

    def score_send_all(step, phase):
        for offset in range(1, side):
            for group in range(2):
                score_copy(step, group, phase, offset).start()

    def score_start(step):
        for i in range(2):
            at = slice(i * half_rows, (i + 1) * half_rows)
            found = dot(own_split[0, at], into_scores[0, 0])
            for half, part in ((0, 1), (1, 0), (1, 1)):
                found += dot(own_split[half, at], into_scores[half, part])
            partial[step, at] = found
        score_send_all(step, 0)

    def score_step(step, phase):
        for group in range(2):
            for offset in range(1, side):
                score_copy(step, group, phase - 1, offset).wait_recv()
            mine = strip(places[1 - group])
            if phase == 1:
                found = partial[step, stripe(group, places[group])]
                for other in range(side - 1):
                    found += from_along[step, group, other]
                over_along[step, group] = found
            if phase == 2:
                found = over_along[step, group, mine]
                for other in range(side - 1):
                    found += from_across[step, group, other]
                over_both[step, group, mine] = found
            if phase == 3:
                scores[step, stripe(group, places[group])] = over_both[step, group]
        if phase == 4:
            for i in range(2):
                at = slice(i * half_rows, (i + 1) * half_rows)
                high, low = split(scores[step, at])
                for half in range(2):
                    found = dot(high, from_scores[half], ((1,), (1,)))
                    found += dot(low, from_scores[half], ((1,), (1,)))
                    projected[half, at] = found[:, :LANES] + found[:, LANES:]
            return
        score_send_all(step, phase)

    loading[0].wait()
    loading[1].wait()
    find_reach()
    loading[2].wait()
    loading[3].wait()
    take_own(0, 0)
    loading[4].wait()
    shear(2 * hops - 1, 2 * hops + 1)

    def set_up(step, low, high):
        @pl.when(step == 0)
        def _():
            for block in range(high - 1, low - 1, -1):
                shear(block, block + 1)

    def set_up_far(step):
        @pl.when(step == 0)
        def _():
            loading[5].wait()
            shear(2 * hops - 2, 2 * hops - 1)
            shear(2 * hops - 3, 2 * hops - 2)

    def set_up_factors(step):
        @pl.when(step == 0)
        def _():
            loading[6].wait()
            loading[7].wait()
            for half in range(2):
                at = slice(half * LANES, (half + 1) * LANES)
                for part, values in enumerate(split(factor_in[at, :])):
                    into_scores[half, part, :LANES] = values
                    into_scores[half, part, LANES:] = values
                high, low = split(factor_out[at, :])
                from_scores[half, :LANES] = high
                from_scores[half, LANES:] = low
            loading[8].wait()
            loading[9].wait()

    def step_body(step, carry):
        for half in range(2):
            @pl.when(step > 0)
            def _():
                if half == 1:
                    upper_parts(step - 1, half, 1)
                finish_ahead(step - 1, half)
                if half == 0:
                    score_step(step - 1, 4)
                finish_chain(step - 1, half)

            @pl.when(step == STEPS)
            def _():
                write(half).start()

            @pl.when(step == 1)
            def _():
                send_own(step, half)
                take_own(step, half)

            if half == 1:
                @pl.when(step == 0)
                def _():
                    take_own(step, half)

            @pl.when(step < STEPS)
            def _():
                start(step, half)

        @pl.when(step < STEPS)
        def _():
            set_up_factors(step)
            score_start(step)
            arrive_ahead(step, 0, 0)
            set_up_far(step)
            pass_on(step, 0, 0)
            arrive_chain(step, 0, 0)
            arrive_ahead(step, 1, 0)
            pass_on(step, 1, 0)
            arrive_chain(step, 1, 0)
            score_step(step, 1)
            set_up(step, 1, 3)
            arrive_ahead(step, 0, 1)
            pass_on(step, 0, 1)
            arrive_chain(step, 0, 1)
            score_step(step, 2)
            arrive_ahead(step, 1, 1)
            pass_on(step, 1, 1)
            set_up(step, 0, 1)
            diagonal(0)
            arrive_chain(step, 1, 1)
            score_step(step, 3)
            diagonal(1)
            upper_parts(step, 0, 0)
            upper_parts(step, 1, 0)
            upper_parts(step, 0, 1)

        return carry

    def write(half):
        return pltpu.make_async_copy(
            own.at[STEPS, half], out_hbm.at[:, pl.ds(half * LANES, LANES)], load_sem.at[half]
        )

    lax.fori_loop(0, STEPS + 1, step_body, 0)

    def drain(index, carry):
        step = lax.div(index, 2)
        half = lax.rem(index, 2)
        for slot in range(hops):
            ahead_copy(step, half, slot).wait_send()
            chain_copy(step, half, slot).wait_send()
            cross_copy(step, half, slot).wait_send()
            beside_copy(own.at[step, half], step, half, slot).wait_send()
        return carry

    lax.fori_loop(0, 2 * STEPS, drain, 0)
    for step in range(STEPS):
        for phase in range(4):
            for group in range(2):
                for offset in range(1, side):
                    score_copy(step, group, phase, offset).wait_send()
    for half in range(2):
        write(half).wait()


def body(total_rows, side, ld_band, marginal, effects_init, factor_in, factor_out, ld_width, ld_starts):
    rows, span = ld_band.shape
    traits, factors = factor_in.shape
    hops = span // (2 * rows)
    blocks = 2 * hops + 1
    f32, bf16 = jnp.float32, jnp.bfloat16
    piece = (rows, LANES)
    quarter = rows // (2 * side)
    dma = pltpu.SemaphoreType.DMA
    scratch = [
        pltpu.VMEM((1,) + ld_width.shape, jnp.int32),
        pltpu.VMEM((1,) + ld_starts.shape, jnp.int32),
        pltpu.VMEM((rows, span), f32),
        pltpu.VMEM((rows, LANES), jnp.int32),
        pltpu.VMEM((blocks, 2, 2, rows // 2, rows), bf16),
        pltpu.VMEM((STEPS + 1, 2) + piece, f32),
        pltpu.VMEM((2, rows, 2 * LANES), bf16),
        pltpu.VMEM((2, 2 * rows, 2 * LANES), bf16),
        pltpu.VMEM((2,) + piece, f32),
        pltpu.VMEM((2,) + piece, f32),
        pltpu.VMEM((STEPS, 2, hops) + piece, f32),
        pltpu.VMEM((STEPS, 2, hops) + piece, f32),
        pltpu.VMEM((STEPS, 2, hops) + piece, f32),
        pltpu.VMEM((STEPS, 2, hops) + piece, f32),
        pltpu.VMEM((STEPS, 2, hops) + piece, f32),
        pltpu.VMEM((STEPS, 2) + piece, f32),
        pltpu.VMEM((2,) + piece, f32),
        pltpu.VMEM((2,) + piece, f32),
        pltpu.VMEM((traits, factors), f32),
        pltpu.VMEM((traits, factors), f32),
        pltpu.VMEM((2, 2, 2 * LANES, factors), bf16),
        pltpu.VMEM((2, 2 * LANES, factors), bf16),
        pltpu.VMEM((STEPS, rows, factors), f32),
        pltpu.VMEM((STEPS, 2, side - 1, quarter, factors), f32),
        pltpu.VMEM((STEPS, 2, quarter, factors), f32),
        pltpu.VMEM((STEPS, 2, side - 1, quarter // side, factors), f32),
        pltpu.VMEM((STEPS, 2, quarter, factors), f32),
        pltpu.VMEM((STEPS, rows, factors), f32),
        pltpu.VMEM((2,) + piece, f32),
        dma((10,)),
    ]
    scratch += [dma((STEPS, 2, hops)) for _ in range(8)]
    scratch += [dma((STEPS, 2, 4, side - 1)) for _ in range(2)]

    def call(*refs):
        kernel(total_rows, side, *refs)

    whole = pl.BlockSpec(memory_space=pl.ANY)
    return pl.pallas_call(
        call,
        name="fit",
        out_shape=jax.ShapeDtypeStruct(effects_init.shape, f32),
        in_specs=[whole] * 7,
        out_specs=whole,
        scratch_shapes=scratch,
        compiler_params=pltpu.CompilerParams(
            collective_id=0, has_side_effects=True, vmem_limit_bytes=60 * 1024 * 1024
        ),
    )(ld_band, marginal, effects_init, factor_in, factor_out, ld_width[None, :], ld_starts[None, :])


def solution(mesh):
    side = 4
    total_rows = mesh.shape["snp"] * 512

    def run(*args):
        return body(total_rows, side, *args)

    return jax.shard_map(
        run,
        mesh=mesh,
        in_specs=(
            P("snp", None),
            P("snp", "trait"),
            P("snp", "trait"),
            P("trait", None),
            P("trait", None),
            P(),
            P(),
        ),
        out_specs=P("snp", "trait"),
        check_vma=False,
    )
```

```python
import jax
import jax.numpy as jnp
from jax import lax
from jax.experimental import pallas as pl
from jax.experimental.pallas import tpu as pltpu
from jax.sharding import PartitionSpec as P

STEPS = 2
MESH = pl.DeviceIdType.MESH
LANES = 128
GROUP = 16

step_size = 0.5
shrinkage = 0.5


def split(values):
    high = values.astype(jnp.bfloat16)
    low = (values - high.astype(jnp.float32)).astype(jnp.bfloat16)
    return high, low


def dot(left, right, contract=((1,), (0,))):
    return lax.dot_general(left, right, (contract, ((), ())), preferred_element_type=jnp.float32)


def kernel(
    total_rows,
    side,
    band_hbm,
    marginal_hbm,
    effects_hbm,
    factor_in_hbm,
    factor_out_hbm,
    width_hbm,
    starts_hbm,
    out_hbm,
    width,
    starts,
    band,
    reach,
    upper,
    own,
    own_split,
    own_stack,
    marginal,
    total,
    ahead,
    beside,
    chain,
    crossed,
    crossing,
    first,
    later,
    home,
    factor_in,
    factor_out,
    into_scores,
    from_scores,
    partial,
    from_along,
    over_along,
    from_across,
    over_both,
    scores,
    projected,
    load_sem,
    ahead_send,
    ahead_recv,
    beside_send,
    beside_recv,
    chain_send,
    chain_recv,
    cross_send,
    cross_recv,
    score_send,
    score_recv,
):
    rows = band.shape[0]
    span = band.shape[1]
    hops = span // (2 * rows)
    blocks = 2 * hops + 1
    device = lax.axis_index("snp")
    column = lax.axis_index("trait")
    devices = lax.axis_size("snp")
    core = lax.rem(device, 2)
    chip = lax.div(device, 2)
    chips = devices // 2
    behind_id = (lax.rem(device + devices - 2, devices), column)
    ahead_id = (lax.rem(device + 2, devices), column)
    beside_id = (device + 1 - 2 * core, column)
    my_y = lax.div(column, side)
    my_x = lax.rem(column, side)

    def x_peer(offset):
        return lax.rem(my_x + offset, side)

    def y_peer(offset):
        return lax.rem(my_y + offset, side)

    def x_id(offset):
        return (device, my_y * side + x_peer(offset))

    def y_id(offset):
        return (device, y_peer(offset) * side + my_x)

    near = 2 * rows * (hops - 1)
    loads = [
        (width_hbm, width),
        (starts_hbm, starts),
        (effects_hbm.at[:, pl.ds(0, LANES)], own.at[0, 0]),
        (effects_hbm.at[:, pl.ds(LANES, LANES)], own.at[0, 1]),
        (band_hbm.at[:, pl.ds(near, span - near)], band.at[:, pl.ds(near, span - near)]),
        (band_hbm.at[:, pl.ds(0, near)], band.at[:, pl.ds(0, near)]),
        (factor_in_hbm, factor_in),
        (factor_out_hbm, factor_out),
        (marginal_hbm.at[:, pl.ds(0, LANES)], marginal.at[0]),
        (marginal_hbm.at[:, pl.ds(LANES, LANES)], marginal.at[1]),
    ]
    loading = [pltpu.make_async_copy(a, b, load_sem.at[i]) for i, (a, b) in enumerate(loads)]
    for copy in loading:
        copy.start()

    partners = [beside_id]
    for offset in range(1, side):
        partners += [x_id(offset), y_id(offset)]
    barrier = pltpu.get_barrier_semaphore()
    for partner in partners:
        pl.semaphore_signal(barrier, inc=1, device_id=partner, device_id_type=MESH)

    @pl.when(chip >= 1)
    def _():
        pl.semaphore_signal(barrier, inc=1, device_id=behind_id, device_id_type=MESH)

    @pl.when(chip + 1 < chips)
    def _():
        pl.semaphore_signal(barrier, inc=1, device_id=ahead_id, device_id_type=MESH)

    ends = jnp.where(chip >= 1, 1, 0) + jnp.where(chip + 1 < chips, 1, 0)
    pl.semaphore_wait(barrier, len(partners) + ends)

    def remote(source, target, send, recv, to):
        return pltpu.make_async_remote_copy(
            src_ref=source, dst_ref=target, send_sem=send, recv_sem=recv, device_id=to, device_id_type=MESH
        )

    def ahead_copy(step, half, slot, source=None):
        if source is None:
            source = own.at[step, half] if slot == 0 else ahead.at[step, half, slot - 1]
        return remote(
            source,
            ahead.at[step, half, slot],
            ahead_send.at[step, half, slot],
            ahead_recv.at[step, half, slot],
            behind_id,
        )

    def beside_copy(source, step, half, slot):
        return remote(
            source,
            beside.at[step, half, slot],
            beside_send.at[step, half, slot],
            beside_recv.at[step, half, slot],
            beside_id,
        )

    def chain_copy(step, half, slot):
        source = first.at[step, half] if slot == 0 else chain.at[step, half, slot - 1]
        return remote(
            source,
            chain.at[step, half, slot],
            chain_send.at[step, half, slot],
            chain_recv.at[step, half, slot],
            ahead_id,
        )

    def cross_copy(step, half, slot):
        return remote(
            crossing.at[step, half, slot],
            crossed.at[step, half, slot],
            cross_send.at[step, half, slot],
            cross_recv.at[step, half, slot],
            beside_id,
        )

    def sends_ahead(slot):
        return (chip >= 1) & (chip + slot < chips)

    def takes_ahead(slot):
        return chip + 1 + slot < chips

    def takes_beside(slot):
        return chip + slot + core < chips

    def sends_beside(slot):
        return chip + 1 - core + slot < chips

    def sends_chain(slot):
        return chip + hops - slot < chips

    def takes_chain(slot):
        return (chip >= 1) & (chip + hops - 1 - slot < chips)

    def send_own(step, half):
        @pl.when(sends_ahead(0))
        def _():
            ahead_copy(step, half, 0).start()

        @pl.when(core == 1)
        def _():
            beside_copy(own.at[step, half], step, half, 0).start()

    for half in range(2):
        source = effects_hbm.at[:, pl.ds(half * LANES, LANES)]

        @pl.when(sends_ahead(0))
        def _():
            ahead_copy(0, half, 0, source).start()

        @pl.when(core == 1)
        def _():
            beside_copy(source, 0, half, 0).start()

    def find_reach():
        for base in range(0, rows, LANES):
            index = lax.broadcasted_iota(jnp.int32, (LANES, width.shape[1]), 0) + (device * rows + base)
            entry = lax.broadcasted_iota(jnp.int32, index.shape, 1)
            covered = jnp.where(starts[...] <= index, 1, 0)
            last = jnp.sum(covered, axis=1, keepdims=True) - 1
            found = jnp.sum(jnp.where(entry == last, width[...], 0), axis=1, keepdims=True)
            limit = jnp.minimum(found, total_rows - 1 - index[:, :1])
            reach[base : base + LANES, :] = jnp.broadcast_to(limit, (LANES, LANES))

    half_rows = rows // 2
    per_block = rows // LANES

    def shear(low_block, high_block):
        def body(group, carry):
            shift = group * GROUP
            lane = lax.broadcasted_iota(jnp.int32, (GROUP, LANES), 1)
            row = lax.broadcasted_iota(jnp.int32, (GROUP, LANES), 0)
            row8 = lax.broadcasted_iota(jnp.int32, (8, LANES), 0)
            from_left = lane < row + (shift + 1)
            for base in range(rows // LANES):
                at = pl.multiple_of(base * LANES + shift, GROUP)
                limit = reach[pl.ds(at, GROUP), :]

                def turned(tile):
                    if tile < 0 or tile >= span // LANES:
                        return jnp.zeros((GROUP, LANES), jnp.float32)
                    values = band[pl.ds(at, GROUP), tile * LANES : (tile + 1) * LANES]
                    values = jnp.where(lane + tile * LANES < limit, values, 0.0)
                    parts = []
                    for top in range(0, GROUP, 8):
                        part = pltpu.roll(values[top : top + 8], shift + (top + 1), 1)
                        for bit in (1, 2, 4):
                            part = jnp.where(row8 & bit != 0, pltpu.roll(part, bit, 1), part)
                        parts.append(part)
                    return jnp.concatenate(parts, axis=0)

                left = turned(low_block * per_block - base - 1)
                for tile in range(low_block * per_block, high_block * per_block):
                    right = turned(tile - base)
                    high, low = split(jnp.where(from_left, left, right))
                    left = right
                    block, at_tile = tile // per_block, tile % per_block
                    row_half = base * LANES // half_rows
                    inner = pl.multiple_of(at - row_half * half_rows, GROUP)
                    lanes = slice(at_tile * LANES, (at_tile + 1) * LANES)
                    upper[block, row_half, 0, pl.ds(inner, GROUP), lanes] = high
                    upper[block, row_half, 1, pl.ds(inner, GROUP), lanes] = low
            return carry

        lax.fori_loop(0, LANES // GROUP, body, 0)

    def product(block, right, put):
        for i in range(2):
            found = dot(upper[block, i].reshape(rows, rows), right)
            found = found[:, :LANES] + found[:, LANES:]
            put(i, found[:half_rows] + found[half_rows:])

    def store_to(ref):
        def put(i, values):
            ref[i * half_rows : (i + 1) * half_rows, :] = values

        return put

    def add_to(ref):
        def put(i, values):
            ref[i * half_rows : (i + 1) * half_rows, :] += values

        return put

    def lower_part(block, half, ref):
        for i in range(2):
            lanes = slice(i * half_rows, (i + 1) * half_rows)
            left = upper[block, :, :, :, lanes].reshape(2 * rows, half_rows)
            found = dot(left, own_stack[half], ((0,), (0,)))
            ref[lanes, :] = found[:, :LANES] + found[:, LANES:]

    def joined(values):
        return jnp.concatenate(split(values), axis=1)

    def take_own(step, half):
        found = joined(own[step, half])
        own_split[half] = found
        for i in range(2):
            for copy in range(2):
                at = (2 * i + copy) * half_rows
                own_stack[half, at : at + half_rows] = found[i * half_rows : (i + 1) * half_rows]

    def start(step, half):
        lower_part(2 * hops - 1, half, crossing.at[step, half, 0])
        cross_copy(step, half, 0).start()
        lower_part(2 * hops, half, first.at[step, half])

        @pl.when(core == 0)
        def _():
            cross_copy(step, half, 0).wait_recv()
            first[step, half] += crossed[step, half, 0]

        @pl.when(sends_chain(0))
        def _():
            chain_copy(step, half, 0).start()

    def ahead_part(step, half, slot):
        @pl.when(takes_ahead(slot))
        def _():
            product(2 * slot + 2, joined(ahead[step, half, slot]), add_to(total.at[half]))

    def beside_part(step, half, slot):
        @pl.when(takes_beside(slot))
        def _():
            beside_copy(own.at[step, half], step, half, slot).wait_recv()
            product(2 * slot + 1, joined(beside[step, half, slot]), add_to(total.at[half]))

    def finish_ahead(step, half):
        last = hops - 1

        @pl.when(takes_ahead(last))
        def _():
            ahead_copy(step, half, last).wait_recv()

            @pl.when(core == 0)
            def _():
                beside_copy(ahead.at[step, half, last], step, half, last).start()

        ahead_part(step, half, last)

        @pl.when(core == 1)
        def _():
            cross_copy(step, half, last).wait_recv()
            home[half] += crossed[step, half, last]

        beside_part(step, half, last)
        total[half] += home[half]

    def finish_chain(step, half):
        last = hops - 1

        @pl.when(takes_chain(last))
        def _():
            chain_copy(step, half, last).wait_recv()
            total[half] += chain[step, half, last]

        effects = own[step, half]
        gradient = effects + total[half] - marginal[half] + shrinkage * (effects - projected[half])
        own[step + 1, half] = effects - step_size * gradient

    def arrive_ahead(step, half, slot):
        @pl.when(takes_ahead(slot))
        def _():
            ahead_copy(step, half, slot).wait_recv()
            beside_copy(ahead.at[step, half, slot], step, half, slot + core).start()

        @pl.when(sends_ahead(slot + 1))
        def _():
            ahead_copy(step, half, slot + 1).start()

    def arrive_chain(step, half, slot):
        cross_copy(step, half, slot + 1 - core).wait_recv()
        later[half] += crossed[step, half, slot + 1 - core]

        @pl.when(takes_chain(slot))
        def _():
            chain_copy(step, half, slot).wait_recv()
            chain[step, half, slot] += later[half]

        @pl.when(chip == 0)
        def _():
            chain[step, half, slot] = later[half]

        @pl.when(sends_chain(slot + 1))
        def _():
            chain_copy(step, half, slot + 1).start()

    def pass_on(step, half, slot):
        block = 2 * (hops - 1 - slot)
        lower_part(block - 1, half, crossing.at[step, half, slot + 1])
        cross_copy(step, half, slot + 1).start()
        lower_part(block, half, later.at[half])

    def diagonal(half):
        lower_part(0, half, home.at[half])
        product(0, own_split[half], store_to(total.at[half]))

    def upper_parts(step, half, slot):
        ahead_part(step, half, slot)
        beside_part(step, half, slot)

    quarter = half_rows // side
    piece = quarter // side
    places = (my_x, my_y)
    peers = (x_peer, y_peer)
    ids = (x_id, y_id)

    def stripe(group, index):
        return pl.ds(pl.multiple_of(group * half_rows + index * quarter, quarter), quarter)

    def strip(index):
        return pl.ds(pl.multiple_of(index * piece, piece), piece)

    def score_copy(step, group, phase, offset):
        along, across = group, 1 - group
        source, target, to = [
            (
                partial.at[step, stripe(group, peers[along](offset))],
                from_along.at[step, group, offset - 1],
                ids[along](offset),
            ),
            (
                over_along.at[step, group, strip(peers[across](offset))],
                from_across.at[step, group, offset - 1],
                ids[across](offset),
            ),
            (
                over_both.at[step, group, strip(places[across])],
                over_both.at[step, group, strip(places[across])],
                ids[across](offset),
            ),
            (
                over_both.at[step, group],
                scores.at[step, stripe(group, places[along])],
                ids[along](offset),
            ),
        ][phase]
        return remote(
            source,
            target,
            score_send.at[step, group, phase, offset - 1],
            score_recv.at[step, group, phase, offset - 1],
            to,
        )

    def score_send_all(step, phase):
        for offset in range(1, side):
            for group in range(2):
                score_copy(step, group, phase, offset).start()

    def score_start(step):
        for i in range(2):
            at = slice(i * half_rows, (i + 1) * half_rows)
            found = dot(own_split[0, at], into_scores[0, 0])
            for half, part in ((0, 1), (1, 0), (1, 1)):
                found += dot(own_split[half, at], into_scores[half, part])
            partial[step, at] = found
        score_send_all(step, 0)

    def score_step(step, phase):
        for group in range(2):
            for offset in range(1, side):
                score_copy(step, group, phase - 1, offset).wait_recv()
            mine = strip(places[1 - group])
            if phase == 1:
                found = partial[step, stripe(group, places[group])]
                for other in range(side - 1):
                    found += from_along[step, group, other]
                over_along[step, group] = found
            if phase == 2:
                found = over_along[step, group, mine]
                for other in range(side - 1):
                    found += from_across[step, group, other]
                over_both[step, group, mine] = found
            if phase == 3:
                scores[step, stripe(group, places[group])] = over_both[step, group]
        if phase == 4:
            for i in range(2):
                at = slice(i * half_rows, (i + 1) * half_rows)
                high, low = split(scores[step, at])
                for half in range(2):
                    found = dot(high, from_scores[half], ((1,), (1,)))
                    found += dot(low, from_scores[half], ((1,), (1,)))
                    projected[half, at] = found[:, :LANES] + found[:, LANES:]
            return
        score_send_all(step, phase)

    loading[0].wait()
    loading[1].wait()
    find_reach()
    loading[2].wait()
    loading[3].wait()
    take_own(0, 0)
    loading[4].wait()
    shear(2 * hops - 1, 2 * hops + 1)

    def set_up(step, low, high):
        @pl.when(step == 0)
        def _():
            for block in range(high - 1, low - 1, -1):
                shear(block, block + 1)

    def set_up_far(step):
        @pl.when(step == 0)
        def _():
            loading[5].wait()
            shear(2 * hops - 2, 2 * hops - 1)
            shear(2 * hops - 3, 2 * hops - 2)

    def set_up_factors(step):
        @pl.when(step == 0)
        def _():
            loading[6].wait()
            loading[7].wait()
            for half in range(2):
                at = slice(half * LANES, (half + 1) * LANES)
                for part, values in enumerate(split(factor_in[at, :])):
                    into_scores[half, part, :LANES] = values
                    into_scores[half, part, LANES:] = values
                high, low = split(factor_out[at, :])
                from_scores[half, :LANES] = high
                from_scores[half, LANES:] = low
            loading[8].wait()
            loading[9].wait()

    def step_body(step, carry):
        for half in range(2):
            @pl.when(step > 0)
            def _():
                if half == 1:
                    upper_parts(step - 1, half, 1)
                finish_ahead(step - 1, half)
                if half == 0:
                    score_step(step - 1, 4)
                finish_chain(step - 1, half)

            @pl.when(step == STEPS)
            def _():
                write(half).start()

            @pl.when(step == 1)
            def _():
                send_own(step, half)
                take_own(step, half)

            if half == 1:
                @pl.when(step == 0)
                def _():
                    take_own(step, half)

            @pl.when(step < STEPS)
            def _():
                start(step, half)

        @pl.when(step < STEPS)
        def _():
            set_up_factors(step)
            score_start(step)
            arrive_ahead(step, 0, 0)
            set_up_far(step)
            pass_on(step, 0, 0)
            arrive_chain(step, 0, 0)
            arrive_ahead(step, 1, 0)
            pass_on(step, 1, 0)
            arrive_chain(step, 1, 0)
            score_step(step, 1)
            set_up(step, 1, 3)
            arrive_ahead(step, 0, 1)
            pass_on(step, 0, 1)
            arrive_chain(step, 0, 1)
            score_step(step, 2)
            arrive_ahead(step, 1, 1)
            pass_on(step, 1, 1)
            set_up(step, 0, 1)
            diagonal(0)
            arrive_chain(step, 1, 1)
            score_step(step, 3)
            diagonal(1)
            upper_parts(step, 0, 0)
            upper_parts(step, 1, 0)
            upper_parts(step, 0, 1)

        return carry

    def write(half):
        return pltpu.make_async_copy(
            own.at[STEPS, half], out_hbm.at[:, pl.ds(half * LANES, LANES)], load_sem.at[half]
        )

    lax.fori_loop(0, STEPS + 1, step_body, 0)

    def drain(index, carry):
        step = lax.div(index, 2)
        half = lax.rem(index, 2)
        for slot in range(hops):
            cross_copy(step, half, slot).wait_send()

            @pl.when(sends_ahead(slot))
            def _():
                ahead_copy(step, half, slot).wait_send()

            @pl.when(sends_chain(slot))
            def _():
                chain_copy(step, half, slot).wait_send()

            @pl.when(sends_beside(slot))
            def _():
                beside_copy(own.at[step, half], step, half, slot).wait_send()
        return carry

    lax.fori_loop(0, 2 * STEPS, drain, 0)
    for step in range(STEPS):
        for phase in range(4):
            for group in range(2):
                for offset in range(1, side):
                    score_copy(step, group, phase, offset).wait_send()
    for half in range(2):
        write(half).wait()


def body(total_rows, side, ld_band, marginal, effects_init, factor_in, factor_out, ld_width, ld_starts):
    rows, span = ld_band.shape
    traits, factors = factor_in.shape
    hops = span // (2 * rows)
    blocks = 2 * hops + 1
    f32, bf16 = jnp.float32, jnp.bfloat16
    piece = (rows, LANES)
    quarter = rows // (2 * side)
    dma = pltpu.SemaphoreType.DMA
    scratch = [
        pltpu.VMEM((1,) + ld_width.shape, jnp.int32),
        pltpu.VMEM((1,) + ld_starts.shape, jnp.int32),
        pltpu.VMEM((rows, span), f32),
        pltpu.VMEM((rows, LANES), jnp.int32),
        pltpu.VMEM((blocks, 2, 2, rows // 2, rows), bf16),
        pltpu.VMEM((STEPS + 1, 2) + piece, f32),
        pltpu.VMEM((2, rows, 2 * LANES), bf16),
        pltpu.VMEM((2, 2 * rows, 2 * LANES), bf16),
        pltpu.VMEM((2,) + piece, f32),
        pltpu.VMEM((2,) + piece, f32),
        pltpu.VMEM((STEPS, 2, hops) + piece, f32),
        pltpu.VMEM((STEPS, 2, hops) + piece, f32),
        pltpu.VMEM((STEPS, 2, hops) + piece, f32),
        pltpu.VMEM((STEPS, 2, hops) + piece, f32),
        pltpu.VMEM((STEPS, 2, hops) + piece, f32),
        pltpu.VMEM((STEPS, 2) + piece, f32),
        pltpu.VMEM((2,) + piece, f32),
        pltpu.VMEM((2,) + piece, f32),
        pltpu.VMEM((traits, factors), f32),
        pltpu.VMEM((traits, factors), f32),
        pltpu.VMEM((2, 2, 2 * LANES, factors), bf16),
        pltpu.VMEM((2, 2 * LANES, factors), bf16),
        pltpu.VMEM((STEPS, rows, factors), f32),
        pltpu.VMEM((STEPS, 2, side - 1, quarter, factors), f32),
        pltpu.VMEM((STEPS, 2, quarter, factors), f32),
        pltpu.VMEM((STEPS, 2, side - 1, quarter // side, factors), f32),
        pltpu.VMEM((STEPS, 2, quarter, factors), f32),
        pltpu.VMEM((STEPS, rows, factors), f32),
        pltpu.VMEM((2,) + piece, f32),
        dma((10,)),
    ]
    scratch += [dma((STEPS, 2, hops)) for _ in range(8)]
    scratch += [dma((STEPS, 2, 4, side - 1)) for _ in range(2)]

    def call(*refs):
        kernel(total_rows, side, *refs)

    whole = pl.BlockSpec(memory_space=pl.ANY)
    return pl.pallas_call(
        call,
        name="fit",
        out_shape=jax.ShapeDtypeStruct(effects_init.shape, f32),
        in_specs=[whole] * 7,
        out_specs=whole,
        scratch_shapes=scratch,
        compiler_params=pltpu.CompilerParams(
            collective_id=0, has_side_effects=True, vmem_limit_bytes=60 * 1024 * 1024
        ),
    )(ld_band, marginal, effects_init, factor_in, factor_out, ld_width[None, :], ld_starts[None, :])


def solution(mesh):
    side = 4
    total_rows = mesh.shape["snp"] * 512

    def run(*args):
        return body(total_rows, side, *args)

    return jax.shard_map(
        run,
        mesh=mesh,
        in_specs=(
            P("snp", None),
            P("snp", "trait"),
            P("snp", "trait"),
            P("trait", None),
            P("trait", None),
            P(),
            P(),
        ),
        out_specs=P("snp", "trait"),
        check_vma=False,
    )
```

```python
import jax
import jax.numpy as jnp
from jax import lax
from jax.experimental import pallas as pl
from jax.experimental.pallas import tpu as pltpu
from jax.sharding import PartitionSpec as P

STEPS = 2
MESH = pl.DeviceIdType.MESH
LANES = 128
GROUP = 16

step_size = 0.5
shrinkage = 0.5


def split(values):
    high = values.astype(jnp.bfloat16)
    low = (values - high.astype(jnp.float32)).astype(jnp.bfloat16)
    return high, low


def dot(left, right, contract=((1,), (0,))):
    return lax.dot_general(left, right, (contract, ((), ())), preferred_element_type=jnp.float32)


def kernel(
    total_rows,
    side,
    band_hbm,
    marginal_hbm,
    effects_hbm,
    factor_in_hbm,
    factor_out_hbm,
    width_hbm,
    starts_hbm,
    out_hbm,
    width,
    starts,
    band,
    reach,
    stacked,
    rotated,
    upper,
    own,
    own_split,
    own_stack,
    marginal,
    total,
    ahead,
    beside,
    chain,
    crossed,
    crossing,
    first,
    later,
    home,
    factor_in,
    factor_out,
    into_scores,
    from_scores,
    partial,
    from_along,
    over_along,
    from_across,
    over_both,
    scores,
    projected,
    load_sem,
    ahead_send,
    ahead_recv,
    beside_send,
    beside_recv,
    chain_send,
    chain_recv,
    cross_send,
    cross_recv,
    score_send,
    score_recv,
):
    rows = band.shape[0]
    span = band.shape[1]
    hops = span // (2 * rows)
    blocks = 2 * hops + 1
    device = lax.axis_index("snp")
    column = lax.axis_index("trait")
    devices = lax.axis_size("snp")
    core = lax.rem(device, 2)
    chip = lax.div(device, 2)
    chips = devices // 2
    behind_id = (lax.rem(device + devices - 2, devices), column)
    ahead_id = (lax.rem(device + 2, devices), column)
    beside_id = (device + 1 - 2 * core, column)
    my_y = lax.div(column, side)
    my_x = lax.rem(column, side)

    def x_peer(offset):
        return lax.rem(my_x + offset, side)

    def y_peer(offset):
        return lax.rem(my_y + offset, side)

    def x_id(offset):
        return (device, my_y * side + x_peer(offset))

    def y_id(offset):
        return (device, y_peer(offset) * side + my_x)

    partners = [beside_id]
    for offset in range(1, side):
        partners += [x_id(offset), y_id(offset)]
    barrier = pltpu.get_barrier_semaphore()
    for partner in partners:
        pl.semaphore_signal(barrier, inc=1, device_id=partner, device_id_type=MESH)

    @pl.when(chip >= 1)
    def _():
        pl.semaphore_signal(barrier, inc=1, device_id=behind_id, device_id_type=MESH)

    @pl.when(chip + 1 < chips)
    def _():
        pl.semaphore_signal(barrier, inc=1, device_id=ahead_id, device_id_type=MESH)

    near = 2 * rows * (hops - 1)
    loads = [
        (width_hbm, width),
        (starts_hbm, starts),
        (effects_hbm.at[:, pl.ds(0, LANES)], own.at[0, 0]),
        (effects_hbm.at[:, pl.ds(LANES, LANES)], own.at[0, 1]),
        (band_hbm.at[:, pl.ds(near, span - near)], band.at[:, pl.ds(near, span - near)]),
        (band_hbm.at[:, pl.ds(0, near)], band.at[:, pl.ds(0, near)]),
        (factor_in_hbm, factor_in),
        (factor_out_hbm, factor_out),
        (marginal_hbm.at[:, pl.ds(0, LANES)], marginal.at[0]),
        (marginal_hbm.at[:, pl.ds(LANES, LANES)], marginal.at[1]),
    ]
    loading = [pltpu.make_async_copy(a, b, load_sem.at[i]) for i, (a, b) in enumerate(loads)]
    for index in (4, 0, 1, 2, 3, 5, 6, 7, 8, 9):
        loading[index].start()

    ends = jnp.where(chip >= 1, 1, 0) + jnp.where(chip + 1 < chips, 1, 0)
    pl.semaphore_wait(barrier, len(partners) + ends)

    def remote(source, target, send, recv, to):
        return pltpu.make_async_remote_copy(
            src_ref=source, dst_ref=target, send_sem=send, recv_sem=recv, device_id=to, device_id_type=MESH
        )

    def ahead_copy(step, half, slot, source=None):
        if source is None:
            source = own.at[step, half] if slot == 0 else ahead.at[step, half, slot - 1]
        return remote(
            source,
            ahead.at[step, half, slot],
            ahead_send.at[step, half, slot],
            ahead_recv.at[step, half, slot],
            behind_id,
        )

    def beside_copy(source, step, half, slot):
        return remote(
            source,
            beside.at[step, half, slot],
            beside_send.at[step, half, slot],
            beside_recv.at[step, half, slot],
            beside_id,
        )

    def chain_copy(step, half, slot):
        source = first.at[step, half] if slot == 0 else chain.at[step, half, slot - 1]
        return remote(
            source,
            chain.at[step, half, slot],
            chain_send.at[step, half, slot],
            chain_recv.at[step, half, slot],
            ahead_id,
        )

    def cross_copy(step, half, slot):
        return remote(
            crossing.at[step, half, slot],
            crossed.at[step, half, slot],
            cross_send.at[step, half, slot],
            cross_recv.at[step, half, slot],
            beside_id,
        )

    def sends_ahead(slot):
        return (chip >= 1) & (chip + slot < chips)

    def takes_ahead(slot):
        return chip + 1 + slot < chips

    def takes_beside(slot):
        return chip + slot + core < chips

    def sends_beside(slot):
        return chip + 1 - core + slot < chips

    def sends_chain(slot):
        return chip + hops - slot < chips

    def takes_chain(slot):
        return (chip >= 1) & (chip + hops - 1 - slot < chips)

    def send_own(step, half):
        @pl.when(sends_ahead(0))
        def _():
            ahead_copy(step, half, 0).start()

        @pl.when(core == 1)
        def _():
            beside_copy(own.at[step, half], step, half, 0).start()

    for half in range(2):
        source = effects_hbm.at[:, pl.ds(half * LANES, LANES)]

        @pl.when(sends_ahead(0))
        def _():
            ahead_copy(0, half, 0, source).start()

        @pl.when(core == 1)
        def _():
            beside_copy(source, 0, half, 0).start()

    def find_reach():
        for base in range(0, rows, LANES):
            index = lax.broadcasted_iota(jnp.int32, (LANES, width.shape[1]), 0) + (device * rows + base)
            entry = lax.broadcasted_iota(jnp.int32, index.shape, 1)
            covered = jnp.where(starts[...] <= index, 1, 0)
            last = jnp.sum(covered, axis=1, keepdims=True) - 1
            found = jnp.sum(jnp.where(entry == last, width[...], 0), axis=1, keepdims=True)
            limit = jnp.minimum(found, total_rows - 1 - index[:, :1])
            reach[base : base + LANES, :] = jnp.broadcast_to(limit, (LANES, LANES))

    half_rows = rows // 2
    per_block = rows // LANES

    def turn(chunk):
        def spread(group, carry):
            for part in range(2):
                at = pl.multiple_of(group * GROUP + part * 8, 8)
                for tile in range(8):
                    lanes = slice((chunk * 8 + tile) * LANES, (chunk * 8 + tile + 1) * LANES)
                    stacked[pl.ds((chunk * rows + at) * 8 + tile, 8, stride=8), :] = band[pl.ds(at, 8), lanes]
            return carry

        def rotate(group, carry):
            for row in range(LANES):
                at = pl.multiple_of((chunk * rows + group * LANES + row) * 8, 8)
                values = stacked[pl.ds(at, 8), :]
                rotated[pl.ds(at, 8), :] = values if row + 1 == LANES else pltpu.roll(values, row + 1, 1)
            return carry

        lax.fori_loop(0, rows // GROUP, spread, 0)
        lax.fori_loop(0, rows // LANES, rotate, 0)

    def shear(low_block, high_block):
        def body(group, carry):
            shift = group * GROUP
            lane = lax.broadcasted_iota(jnp.int32, (GROUP, LANES), 1)
            row = lax.broadcasted_iota(jnp.int32, (GROUP, LANES), 0)
            from_left = lane < row + (shift + 1)
            for base in range(rows // LANES):
                at = pl.multiple_of(base * LANES + shift, GROUP)
                limit = reach[pl.ds(at, GROUP), :] + (row - lane) + (at + 1)

                def turned(tile):
                    if tile < 0 or tile >= span // LANES:
                        return jnp.zeros((GROUP, LANES), jnp.float32)
                    return rotated[pl.ds((tile // 8 * rows + at) * 8 + tile % 8, GROUP, stride=8), :]

                left = turned(low_block * per_block - base - 1)
                for tile in range(low_block * per_block, high_block * per_block):
                    right = turned(tile - base)
                    values = jnp.where(from_left, left, right)
                    high, low = split(jnp.where(tile * LANES < limit, values, 0.0))
                    left = right
                    block, at_tile = tile // per_block, tile % per_block
                    row_half = base * LANES // half_rows
                    inner = pl.multiple_of(at - row_half * half_rows, GROUP)
                    lanes = slice(at_tile * LANES, (at_tile + 1) * LANES)
                    upper[block, row_half, 0, pl.ds(inner, GROUP), lanes] = high
                    upper[block, row_half, 1, pl.ds(inner, GROUP), lanes] = low
            return carry

        lax.fori_loop(0, LANES // GROUP, body, 0)

    def product(block, right, put):
        for i in range(2):
            found = dot(upper[block, i].reshape(rows, rows), right)
            found = found[:, :LANES] + found[:, LANES:]
            put(i, found[:half_rows] + found[half_rows:])

    def store_to(ref):
        def put(i, values):
            ref[i * half_rows : (i + 1) * half_rows, :] = values

        return put

    def add_to(ref):
        def put(i, values):
            ref[i * half_rows : (i + 1) * half_rows, :] += values

        return put

    def lower_part(block, half, ref):
        for i in range(2):
            lanes = slice(i * half_rows, (i + 1) * half_rows)
            left = upper[block, :, :, :, lanes].reshape(2 * rows, half_rows)
            found = dot(left, own_stack[half], ((0,), (0,)))
            ref[lanes, :] = found[:, :LANES] + found[:, LANES:]

    def joined(values):
        return jnp.concatenate(split(values), axis=1)

    def take_own(step, half):
        found = joined(own[step, half])
        own_split[half] = found
        for i in range(2):
            for copy in range(2):
                at = (2 * i + copy) * half_rows
                own_stack[half, at : at + half_rows] = found[i * half_rows : (i + 1) * half_rows]

    def start(step, half):
        def send_beside():
            lower_part(2 * hops - 1, half, crossing.at[step, half, 0])
            cross_copy(step, half, 0).start()

        @pl.when(core == 1)
        def _():
            send_beside()

        lower_part(2 * hops, half, first.at[step, half])

        @pl.when(core == 0)
        def _():
            cross_copy(step, half, 0).wait_recv()
            first[step, half] += crossed[step, half, 0]

        @pl.when(sends_chain(0))
        def _():
            chain_copy(step, half, 0).start()

        @pl.when(core == 0)
        def _():
            send_beside()

    def ahead_part(step, half, slot):
        @pl.when(takes_ahead(slot))
        def _():
            product(2 * slot + 2, joined(ahead[step, half, slot]), add_to(total.at[half]))

    def beside_part(step, half, slot):
        @pl.when(takes_beside(slot))
        def _():
            beside_copy(own.at[step, half], step, half, slot).wait_recv()
            product(2 * slot + 1, joined(beside[step, half, slot]), add_to(total.at[half]))

    def finish_ahead(step, half):
        last = hops - 1

        @pl.when(takes_ahead(last))
        def _():
            ahead_copy(step, half, last).wait_recv()

            @pl.when(core == 0)
            def _():
                beside_copy(ahead.at[step, half, last], step, half, last).start()

        ahead_part(step, half, last)

        @pl.when(core == 1)
        def _():
            cross_copy(step, half, last).wait_recv()
            home[half] += crossed[step, half, last]

        beside_part(step, half, last)
        total[half] += home[half]

    def finish_chain(step, half):
        last = hops - 1

        @pl.when(takes_chain(last))
        def _():
            chain_copy(step, half, last).wait_recv()
            total[half] += chain[step, half, last]

        effects = own[step, half]
        gradient = effects + total[half] - marginal[half] + shrinkage * (effects - projected[half])
        own[step + 1, half] = effects - step_size * gradient

    def arrive_ahead(step, half, slot):
        @pl.when(takes_ahead(slot))
        def _():
            ahead_copy(step, half, slot).wait_recv()
            beside_copy(ahead.at[step, half, slot], step, half, slot + core).start()

        @pl.when(sends_ahead(slot + 1))
        def _():
            ahead_copy(step, half, slot + 1).start()

    def arrive_chain(step, half, slot):
        cross_copy(step, half, slot + 1 - core).wait_recv()
        later[half] += crossed[step, half, slot + 1 - core]

        @pl.when(takes_chain(slot))
        def _():
            chain_copy(step, half, slot).wait_recv()
            chain[step, half, slot] += later[half]

        @pl.when(chip == 0)
        def _():
            chain[step, half, slot] = later[half]

        @pl.when(sends_chain(slot + 1))
        def _():
            chain_copy(step, half, slot + 1).start()

    def pass_on(step, half, slot):
        block = 2 * (hops - 1 - slot)
        lower_part(block - 1, half, crossing.at[step, half, slot + 1])
        cross_copy(step, half, slot + 1).start()
        lower_part(block, half, later.at[half])

    def diagonal(half):
        lower_part(0, half, home.at[half])
        product(0, own_split[half], store_to(total.at[half]))

    def upper_parts(step, half, slot):
        ahead_part(step, half, slot)
        beside_part(step, half, slot)

    quarter = half_rows // side
    piece = quarter // side
    places = (my_x, my_y)
    peers = (x_peer, y_peer)
    ids = (x_id, y_id)

    def stripe(group, index):
        return pl.ds(pl.multiple_of(group * half_rows + index * quarter, quarter), quarter)

    def strip(index):
        return pl.ds(pl.multiple_of(index * piece, piece), piece)

    def score_copy(step, group, phase, offset):
        along, across = group, 1 - group
        source, target, to = [
            (
                partial.at[step, stripe(group, peers[along](offset))],
                from_along.at[step, group, offset - 1],
                ids[along](offset),
            ),
            (
                over_along.at[step, group, strip(peers[across](offset))],
                from_across.at[step, group, offset - 1],
                ids[across](offset),
            ),
            (
                over_both.at[step, group, strip(places[across])],
                over_both.at[step, group, strip(places[across])],
                ids[across](offset),
            ),
            (
                over_both.at[step, group],
                scores.at[step, stripe(group, places[along])],
                ids[along](offset),
            ),
        ][phase]
        return remote(
            source,
            target,
            score_send.at[step, group, phase, offset - 1],
            score_recv.at[step, group, phase, offset - 1],
            to,
        )

    def score_send_all(step, phase):
        for offset in range(1, side):
            for group in range(2):
                score_copy(step, group, phase, offset).start()

    def score_start(step):
        for i in range(2):
            at = slice(i * half_rows, (i + 1) * half_rows)
            found = dot(own_split[0, at], into_scores[0, 0])
            for half, part in ((0, 1), (1, 0), (1, 1)):
                found += dot(own_split[half, at], into_scores[half, part])
            partial[step, at] = found
        score_send_all(step, 0)

    def score_step(step, phase):
        for group in range(2):
            for offset in range(1, side):
                score_copy(step, group, phase - 1, offset).wait_recv()
            mine = strip(places[1 - group])
            if phase == 1:
                found = partial[step, stripe(group, places[group])]
                for other in range(side - 1):
                    found += from_along[step, group, other]
                over_along[step, group] = found
            if phase == 2:
                found = over_along[step, group, mine]
                for other in range(side - 1):
                    found += from_across[step, group, other]
                over_both[step, group, mine] = found
            if phase == 3:
                scores[step, stripe(group, places[group])] = over_both[step, group]
        if phase == 4:
            for i in range(2):
                at = slice(i * half_rows, (i + 1) * half_rows)
                high, low = split(scores[step, at])
                for half in range(2):
                    found = dot(high, from_scores[half], ((1,), (1,)))
                    found += dot(low, from_scores[half], ((1,), (1,)))
                    projected[half, at] = found[:, :LANES] + found[:, LANES:]
            return
        score_send_all(step, phase)

    loading[0].wait()
    loading[1].wait()
    find_reach()
    loading[2].wait()
    loading[3].wait()
    take_own(0, 0)
    loading[4].wait()
    turn(2)
    shear(2 * hops - 1, 2 * hops + 1)

    def set_up(step, low, high):
        @pl.when(step == 0)
        def _():
            shear(low, high)

    def set_up_far(step):
        @pl.when(step == 0)
        def _():
            loading[5].wait()
            turn(1)
            shear(2 * hops - 3, 2 * hops - 1)
            turn(0)

    def set_up_factors(step):
        @pl.when(step == 0)
        def _():
            loading[6].wait()
            loading[7].wait()
            for half in range(2):
                at = slice(half * LANES, (half + 1) * LANES)
                for part, values in enumerate(split(factor_in[at, :])):
                    into_scores[half, part, :LANES] = values
                    into_scores[half, part, LANES:] = values
                high, low = split(factor_out[at, :])
                from_scores[half, :LANES] = high
                from_scores[half, LANES:] = low
            loading[8].wait()
            loading[9].wait()

    def step_body(step, carry):
        for half in range(2):
            @pl.when(step > 0)
            def _():
                if half == 1:
                    upper_parts(step - 1, half, 1)
                finish_ahead(step - 1, half)
                if half == 0:
                    score_step(step - 1, 4)
                finish_chain(step - 1, half)

            @pl.when(step == STEPS)
            def _():
                write(half).start()

            @pl.when(step == 1)
            def _():
                send_own(step, half)
                take_own(step, half)

            if half == 1:
                @pl.when(step == 0)
                def _():
                    take_own(step, half)

            @pl.when(step < STEPS)
            def _():
                start(step, half)

        @pl.when(step < STEPS)
        def _():
            set_up_factors(step)
            score_start(step)
            arrive_ahead(step, 0, 0)
            set_up_far(step)
            pass_on(step, 0, 0)
            arrive_chain(step, 0, 0)
            arrive_ahead(step, 1, 0)
            pass_on(step, 1, 0)
            arrive_chain(step, 1, 0)
            score_step(step, 1)
            set_up(step, 1, 3)
            arrive_ahead(step, 0, 1)
            pass_on(step, 0, 1)
            arrive_chain(step, 0, 1)
            score_step(step, 2)
            arrive_ahead(step, 1, 1)
            pass_on(step, 1, 1)
            set_up(step, 0, 1)
            diagonal(0)
            arrive_chain(step, 1, 1)
            score_step(step, 3)
            diagonal(1)
            upper_parts(step, 0, 0)
            upper_parts(step, 1, 0)
            upper_parts(step, 0, 1)

        return carry

    def write(half):
        return pltpu.make_async_copy(
            own.at[STEPS, half], out_hbm.at[:, pl.ds(half * LANES, LANES)], load_sem.at[half]
        )

    lax.fori_loop(0, STEPS + 1, step_body, 0)

    def drain(index, carry):
        step = lax.div(index, 2)
        half = lax.rem(index, 2)
        for slot in range(hops):
            cross_copy(step, half, slot).wait_send()

            @pl.when(sends_ahead(slot))
            def _():
                ahead_copy(step, half, slot).wait_send()

            @pl.when(sends_chain(slot))
            def _():
                chain_copy(step, half, slot).wait_send()

            @pl.when(sends_beside(slot))
            def _():
                beside_copy(own.at[step, half], step, half, slot).wait_send()
        return carry

    lax.fori_loop(0, 2 * STEPS, drain, 0)
    for step in range(STEPS):
        for phase in range(4):
            for group in range(2):
                for offset in range(1, side):
                    score_copy(step, group, phase, offset).wait_send()
    for half in range(2):
        write(half).wait()


def body(total_rows, side, ld_band, marginal, effects_init, factor_in, factor_out, ld_width, ld_starts):
    rows, span = ld_band.shape
    traits, factors = factor_in.shape
    hops = span // (2 * rows)
    blocks = 2 * hops + 1
    f32, bf16 = jnp.float32, jnp.bfloat16
    piece = (rows, LANES)
    quarter = rows // (2 * side)
    dma = pltpu.SemaphoreType.DMA
    scratch = [
        pltpu.VMEM((1,) + ld_width.shape, jnp.int32),
        pltpu.VMEM((1,) + ld_starts.shape, jnp.int32),
        pltpu.VMEM((rows, span), f32),
        pltpu.VMEM((rows, LANES), jnp.int32),
        pltpu.VMEM((rows * span // LANES, LANES), f32),
        pltpu.VMEM((rows * span // LANES, LANES), f32),
        pltpu.VMEM((blocks, 2, 2, rows // 2, rows), bf16),
        pltpu.VMEM((STEPS + 1, 2) + piece, f32),
        pltpu.VMEM((2, rows, 2 * LANES), bf16),
        pltpu.VMEM((2, 2 * rows, 2 * LANES), bf16),
        pltpu.VMEM((2,) + piece, f32),
        pltpu.VMEM((2,) + piece, f32),
        pltpu.VMEM((STEPS, 2, hops) + piece, f32),
        pltpu.VMEM((STEPS, 2, hops) + piece, f32),
        pltpu.VMEM((STEPS, 2, hops) + piece, f32),
        pltpu.VMEM((STEPS, 2, hops) + piece, f32),
        pltpu.VMEM((STEPS, 2, hops) + piece, f32),
        pltpu.VMEM((STEPS, 2) + piece, f32),
        pltpu.VMEM((2,) + piece, f32),
        pltpu.VMEM((2,) + piece, f32),
        pltpu.VMEM((traits, factors), f32),
        pltpu.VMEM((traits, factors), f32),
        pltpu.VMEM((2, 2, 2 * LANES, factors), bf16),
        pltpu.VMEM((2, 2 * LANES, factors), bf16),
        pltpu.VMEM((STEPS, rows, factors), f32),
        pltpu.VMEM((STEPS, 2, side - 1, quarter, factors), f32),
        pltpu.VMEM((STEPS, 2, quarter, factors), f32),
        pltpu.VMEM((STEPS, 2, side - 1, quarter // side, factors), f32),
        pltpu.VMEM((STEPS, 2, quarter, factors), f32),
        pltpu.VMEM((STEPS, rows, factors), f32),
        pltpu.VMEM((2,) + piece, f32),
        dma((10,)),
    ]
    scratch += [dma((STEPS, 2, hops)) for _ in range(8)]
    scratch += [dma((STEPS, 2, 4, side - 1)) for _ in range(2)]

    def call(*refs):
        kernel(total_rows, side, *refs)

    whole = pl.BlockSpec(memory_space=pl.ANY)
    return pl.pallas_call(
        call,
        name="fit",
        out_shape=jax.ShapeDtypeStruct(effects_init.shape, f32),
        in_specs=[whole] * 7,
        out_specs=whole,
        scratch_shapes=scratch,
        compiler_params=pltpu.CompilerParams(
            collective_id=0, has_side_effects=True, vmem_limit_bytes=60 * 1024 * 1024
        ),
    )(ld_band, marginal, effects_init, factor_in, factor_out, ld_width[None, :], ld_starts[None, :])


def solution(mesh):
    side = 4
    total_rows = mesh.shape["snp"] * 512

    def run(*args):
        return body(total_rows, side, *args)

    return jax.shard_map(
        run,
        mesh=mesh,
        in_specs=(
            P("snp", None),
            P("snp", "trait"),
            P("snp", "trait"),
            P("trait", None),
            P("trait", None),
            P(),
            P(),
        ),
        out_specs=P("snp", "trait"),
        check_vma=False,
    )
```

```python
import jax
import jax.numpy as jnp
from jax import lax
from jax.experimental import pallas as pl
from jax.experimental.pallas import tpu as pltpu
from jax.sharding import PartitionSpec as P

STEPS = 2
MESH = pl.DeviceIdType.MESH
LANES = 128
GROUP = 16

step_size = 0.5
shrinkage = 0.5


def split(values):
    high = values.astype(jnp.bfloat16)
    low = (values - high.astype(jnp.float32)).astype(jnp.bfloat16)
    return high, low


def dot(left, right, contract=((1,), (0,))):
    return lax.dot_general(left, right, (contract, ((), ())), preferred_element_type=jnp.float32)


def kernel(
    total_rows,
    side,
    band_hbm,
    marginal_hbm,
    effects_hbm,
    factor_in_hbm,
    factor_out_hbm,
    width_hbm,
    starts_hbm,
    out_hbm,
    width,
    starts,
    band,
    reach,
    stacked,
    rotated,
    upper,
    own,
    own_split,
    own_stack,
    marginal,
    total,
    ahead,
    beside,
    chain,
    crossed,
    crossing,
    first,
    later,
    home,
    factor_in,
    factor_out,
    into_scores,
    from_scores,
    partial,
    from_along,
    over_along,
    from_across,
    over_both,
    scores,
    projected,
    load_sem,
    ahead_send,
    ahead_recv,
    beside_send,
    beside_recv,
    chain_send,
    chain_recv,
    cross_send,
    cross_recv,
    score_send,
    score_recv,
):
    rows = band.shape[0]
    span = band.shape[1]
    hops = span // (2 * rows)
    blocks = 2 * hops + 1
    device = lax.axis_index("snp")
    column = lax.axis_index("trait")
    devices = lax.axis_size("snp")
    core = lax.rem(device, 2)
    chip = lax.div(device, 2)
    chips = devices // 2
    behind_id = (lax.rem(device + devices - 2, devices), column)
    ahead_id = (lax.rem(device + 2, devices), column)
    beside_id = (device + 1 - 2 * core, column)
    my_y = lax.div(column, side)
    my_x = lax.rem(column, side)

    def x_peer(offset):
        return lax.rem(my_x + offset, side)

    def y_peer(offset):
        return lax.rem(my_y + offset, side)

    def x_id(offset):
        return (device, my_y * side + x_peer(offset))

    def y_id(offset):
        return (device, y_peer(offset) * side + my_x)

    partners = [beside_id]
    for offset in range(1, side):
        partners += [x_id(offset), y_id(offset)]
    barrier = pltpu.get_barrier_semaphore()
    for partner in partners:
        pl.semaphore_signal(barrier, inc=1, device_id=partner, device_id_type=MESH)

    @pl.when(chip >= 1)
    def _():
        pl.semaphore_signal(barrier, inc=1, device_id=behind_id, device_id_type=MESH)

    @pl.when(chip + 1 < chips)
    def _():
        pl.semaphore_signal(barrier, inc=1, device_id=ahead_id, device_id_type=MESH)

    near = 2 * rows * (hops - 1)
    loads = [
        (width_hbm, width),
        (starts_hbm, starts),
        (effects_hbm.at[:, pl.ds(0, LANES)], own.at[0, 0]),
        (effects_hbm.at[:, pl.ds(LANES, LANES)], own.at[0, 1]),
        (band_hbm.at[:, pl.ds(0, near)], band.at[:, pl.ds(0, near)]),
        (factor_in_hbm, factor_in),
        (factor_out_hbm, factor_out),
        (marginal_hbm.at[:, pl.ds(0, LANES)], marginal.at[0]),
        (marginal_hbm.at[:, pl.ds(LANES, LANES)], marginal.at[1]),
    ]
    for top in range(0, rows, LANES):
        part = (pl.ds(top, LANES), pl.ds(near, span - near))
        loads.append((band_hbm.at[part], band.at[part]))
    loading = [pltpu.make_async_copy(a, b, load_sem.at[i]) for i, (a, b) in enumerate(loads)]
    for index in (0, 1, 9, 10, 11, 12, 2, 3):
        loading[index].start()

    ends = jnp.where(chip >= 1, 1, 0) + jnp.where(chip + 1 < chips, 1, 0)
    pl.semaphore_wait(barrier, len(partners) + ends)

    def remote(source, target, send, recv, to):
        return pltpu.make_async_remote_copy(
            src_ref=source, dst_ref=target, send_sem=send, recv_sem=recv, device_id=to, device_id_type=MESH
        )

    def ahead_copy(step, half, slot, source=None):
        if source is None:
            source = own.at[step, half] if slot == 0 else ahead.at[step, half, slot - 1]
        return remote(
            source,
            ahead.at[step, half, slot],
            ahead_send.at[step, half, slot],
            ahead_recv.at[step, half, slot],
            behind_id,
        )

    def beside_copy(source, step, half, slot):
        return remote(
            source,
            beside.at[step, half, slot],
            beside_send.at[step, half, slot],
            beside_recv.at[step, half, slot],
            beside_id,
        )

    def chain_copy(step, half, slot):
        source = first.at[step, half] if slot == 0 else chain.at[step, half, slot - 1]
        return remote(
            source,
            chain.at[step, half, slot],
            chain_send.at[step, half, slot],
            chain_recv.at[step, half, slot],
            ahead_id,
        )

    def cross_copy(step, half, slot):
        return remote(
            crossing.at[step, half, slot],
            crossed.at[step, half, slot],
            cross_send.at[step, half, slot],
            cross_recv.at[step, half, slot],
            beside_id,
        )

    def sends_ahead(slot):
        return (chip >= 1) & (chip + slot < chips)

    def takes_ahead(slot):
        return chip + 1 + slot < chips

    def takes_beside(slot):
        return chip + slot + core < chips

    def sends_beside(slot):
        return chip + 1 - core + slot < chips

    def sends_chain(slot):
        return chip + hops - slot < chips

    def takes_chain(slot):
        return (chip >= 1) & (chip + hops - 1 - slot < chips)

    def send_own(step, half):
        @pl.when(sends_ahead(0))
        def _():
            ahead_copy(step, half, 0).start()

        @pl.when(core == 1)
        def _():
            beside_copy(own.at[step, half], step, half, 0).start()

    for half in range(2):
        source = effects_hbm.at[:, pl.ds(half * LANES, LANES)]

        @pl.when(sends_ahead(0))
        def _():
            ahead_copy(0, half, 0, source).start()

        @pl.when(core == 1)
        def _():
            beside_copy(source, 0, half, 0).start()

    def find_reach():
        for base in range(0, rows, LANES):
            index = lax.broadcasted_iota(jnp.int32, (LANES, width.shape[1]), 0) + (device * rows + base)
            entry = lax.broadcasted_iota(jnp.int32, index.shape, 1)
            covered = jnp.where(starts[...] <= index, 1, 0)
            last = jnp.sum(covered, axis=1, keepdims=True) - 1
            found = jnp.sum(jnp.where(entry == last, width[...], 0), axis=1, keepdims=True)
            limit = jnp.minimum(found, total_rows - 1 - index[:, :1])
            reach[base : base + LANES, :] = jnp.broadcast_to(limit, (LANES, LANES))

    half_rows = rows // 2
    per_block = rows // LANES

    def turn(chunk, low=0, high=rows // LANES):
        def spread(group, carry):
            for part in range(2):
                at = pl.multiple_of(group * GROUP + part * 8, 8)
                for tile in range(8):
                    lanes = slice((chunk * 8 + tile) * LANES, (chunk * 8 + tile + 1) * LANES)
                    stacked[pl.ds((chunk * rows + at) * 8 + tile, 8, stride=8), :] = band[pl.ds(at, 8), lanes]
            return carry

        def rotate(group, carry):
            for row in range(LANES):
                at = pl.multiple_of((chunk * rows + group * LANES + row) * 8, 8)
                values = stacked[pl.ds(at, 8), :]
                rotated[pl.ds(at, 8), :] = values if row + 1 == LANES else pltpu.roll(values, row + 1, 1)
            return carry

        lax.fori_loop(low * (LANES // GROUP), high * (LANES // GROUP), spread, 0)
        lax.fori_loop(low, high, rotate, 0)

    def shear(low_block, high_block):
        def body(group, carry):
            shift = group * GROUP
            lane = lax.broadcasted_iota(jnp.int32, (GROUP, LANES), 1)
            row = lax.broadcasted_iota(jnp.int32, (GROUP, LANES), 0)
            from_left = lane < row + (shift + 1)
            for base in range(rows // LANES):
                at = pl.multiple_of(base * LANES + shift, GROUP)
                limit = reach[pl.ds(at, GROUP), :] + (row - lane) + (at + 1)

                def turned(tile):
                    if tile < 0 or tile >= span // LANES:
                        return jnp.zeros((GROUP, LANES), jnp.float32)
                    return rotated[pl.ds((tile // 8 * rows + at) * 8 + tile % 8, GROUP, stride=8), :]

                left = turned(low_block * per_block - base - 1)
                for tile in range(low_block * per_block, high_block * per_block):
                    right = turned(tile - base)
                    values = jnp.where(from_left, left, right)
                    high, low = split(jnp.where(tile * LANES < limit, values, 0.0))
                    left = right
                    block, at_tile = tile // per_block, tile % per_block
                    row_half = base * LANES // half_rows
                    inner = pl.multiple_of(at - row_half * half_rows, GROUP)
                    lanes = slice(at_tile * LANES, (at_tile + 1) * LANES)
                    upper[block, row_half, 0, pl.ds(inner, GROUP), lanes] = high
                    upper[block, row_half, 1, pl.ds(inner, GROUP), lanes] = low
            return carry

        lax.fori_loop(0, LANES // GROUP, body, 0)

    def product(block, right, put):
        for i in range(2):
            found = dot(upper[block, i].reshape(rows, rows), right)
            found = found[:, :LANES] + found[:, LANES:]
            put(i, found[:half_rows] + found[half_rows:])

    def store_to(ref):
        def put(i, values):
            ref[i * half_rows : (i + 1) * half_rows, :] = values

        return put

    def add_to(ref):
        def put(i, values):
            ref[i * half_rows : (i + 1) * half_rows, :] += values

        return put

    def lower_part(block, half, ref):
        for i in range(2):
            lanes = slice(i * half_rows, (i + 1) * half_rows)
            left = upper[block, :, :, :, lanes].reshape(2 * rows, half_rows)
            found = dot(left, own_stack[half], ((0,), (0,)))
            ref[lanes, :] = found[:, :LANES] + found[:, LANES:]

    def joined(values):
        return jnp.concatenate(split(values), axis=1)

    def take_own(step, half):
        found = joined(own[step, half])
        own_split[half] = found
        for i in range(2):
            for copy in range(2):
                at = (2 * i + copy) * half_rows
                own_stack[half, at : at + half_rows] = found[i * half_rows : (i + 1) * half_rows]

    def start(step, half):
        def send_beside():
            lower_part(2 * hops - 1, half, crossing.at[step, half, 0])
            cross_copy(step, half, 0).start()

        @pl.when(core == 1)
        def _():
            send_beside()

        lower_part(2 * hops, half, first.at[step, half])

        @pl.when(core == 0)
        def _():
            cross_copy(step, half, 0).wait_recv()
            first[step, half] += crossed[step, half, 0]

        @pl.when(sends_chain(0))
        def _():
            chain_copy(step, half, 0).start()

        @pl.when(core == 0)
        def _():
            send_beside()

    def ahead_part(step, half, slot):
        @pl.when(takes_ahead(slot))
        def _():
            product(2 * slot + 2, joined(ahead[step, half, slot]), add_to(total.at[half]))

    def beside_part(step, half, slot):
        @pl.when(takes_beside(slot))
        def _():
            beside_copy(own.at[step, half], step, half, slot).wait_recv()
            product(2 * slot + 1, joined(beside[step, half, slot]), add_to(total.at[half]))

    def finish_ahead(step, half):
        last = hops - 1

        @pl.when(takes_ahead(last))
        def _():
            ahead_copy(step, half, last).wait_recv()

            @pl.when(core == 0)
            def _():
                beside_copy(ahead.at[step, half, last], step, half, last).start()

        ahead_part(step, half, last)

        @pl.when(core == 1)
        def _():
            cross_copy(step, half, last).wait_recv()
            home[half] += crossed[step, half, last]

        beside_part(step, half, last)
        total[half] += home[half]

    def finish_chain(step, half):
        last = hops - 1

        @pl.when(takes_chain(last))
        def _():
            chain_copy(step, half, last).wait_recv()
            total[half] += chain[step, half, last]

        for i in range(2):
            at = slice(i * half_rows, (i + 1) * half_rows)
            effects = own[step, half, at]
            gradient = (
                effects
                + total[half, at]
                - marginal[half, at]
                + shrinkage * (effects - projected[half, at])
            )
            own[step + 1, half, at] = effects - step_size * gradient

            @pl.when(step + 1 == STEPS)
            def _():
                write(half, i).start()

    def write(half, i):
        at = pl.ds(i * half_rows, half_rows)
        return pltpu.make_async_copy(
            own.at[STEPS, half, at], out_hbm.at[at, pl.ds(half * LANES, LANES)], load_sem.at[2 * half + i]
        )

    def arrive_ahead(step, half, slot):
        @pl.when(takes_ahead(slot))
        def _():
            ahead_copy(step, half, slot).wait_recv()
            beside_copy(ahead.at[step, half, slot], step, half, slot + core).start()

        @pl.when(sends_ahead(slot + 1))
        def _():
            ahead_copy(step, half, slot + 1).start()

    def arrive_chain(step, half, slot):
        cross_copy(step, half, slot + 1 - core).wait_recv()
        later[half] += crossed[step, half, slot + 1 - core]

        @pl.when(takes_chain(slot))
        def _():
            chain_copy(step, half, slot).wait_recv()
            chain[step, half, slot] += later[half]

        @pl.when(chip == 0)
        def _():
            chain[step, half, slot] = later[half]

        @pl.when(sends_chain(slot + 1))
        def _():
            chain_copy(step, half, slot + 1).start()

    def pass_on(step, half, slot):
        block = 2 * (hops - 1 - slot)
        lower_part(block - 1, half, crossing.at[step, half, slot + 1])
        cross_copy(step, half, slot + 1).start()
        lower_part(block, half, later.at[half])

    def diagonal(half):
        lower_part(0, half, home.at[half])
        product(0, own_split[half], store_to(total.at[half]))

    def upper_parts(step, half, slot):
        ahead_part(step, half, slot)
        beside_part(step, half, slot)

    quarter = half_rows // side
    piece = quarter // side
    places = (my_x, my_y)
    peers = (x_peer, y_peer)
    ids = (x_id, y_id)

    def stripe(group, index):
        return pl.ds(pl.multiple_of(group * half_rows + index * quarter, quarter), quarter)

    def strip(index):
        return pl.ds(pl.multiple_of(index * piece, piece), piece)

    def score_copy(step, group, phase, offset):
        along, across = group, 1 - group
        source, target, to = [
            (
                partial.at[step, stripe(group, peers[along](offset))],
                from_along.at[step, group, offset - 1],
                ids[along](offset),
            ),
            (
                over_along.at[step, group, strip(peers[across](offset))],
                from_across.at[step, group, offset - 1],
                ids[across](offset),
            ),
            (
                over_both.at[step, group, strip(places[across])],
                over_both.at[step, group, strip(places[across])],
                ids[across](offset),
            ),
            (
                over_both.at[step, group],
                scores.at[step, stripe(group, places[along])],
                ids[along](offset),
            ),
        ][phase]
        return remote(
            source,
            target,
            score_send.at[step, group, phase, offset - 1],
            score_recv.at[step, group, phase, offset - 1],
            to,
        )

    def score_send_all(step, phase):
        for offset in range(1, side):
            for group in range(2):
                score_copy(step, group, phase, offset).start()

    def score_start(step):
        for i in range(2):
            at = slice(i * half_rows, (i + 1) * half_rows)
            found = dot(own_split[0, at], into_scores[0, 0])
            for half, part in ((0, 1), (1, 0), (1, 1)):
                found += dot(own_split[half, at], into_scores[half, part])
            partial[step, at] = found
        score_send_all(step, 0)

    def score_step(step, phase):
        for group in range(2):
            for offset in range(1, side):
                score_copy(step, group, phase - 1, offset).wait_recv()
            mine = strip(places[1 - group])
            if phase == 1:
                found = partial[step, stripe(group, places[group])]
                for other in range(side - 1):
                    found += from_along[step, group, other]
                over_along[step, group] = found
            if phase == 2:
                found = over_along[step, group, mine]
                for other in range(side - 1):
                    found += from_across[step, group, other]
                over_both[step, group, mine] = found
            if phase == 3:
                scores[step, stripe(group, places[group])] = over_both[step, group]
        if phase == 4:
            for i in range(2):
                at = slice(i * half_rows, (i + 1) * half_rows)
                high, low = split(scores[step, at])
                for half in range(2):
                    found = dot(high, from_scores[half], ((1,), (1,)))
                    found += dot(low, from_scores[half], ((1,), (1,)))
                    projected[half, at] = found[:, :LANES] + found[:, LANES:]
            return
        score_send_all(step, phase)

    def drain(step, half, slot):
        cross_copy(step, half, slot).wait_send()

        @pl.when(sends_ahead(slot))
        def _():
            ahead_copy(step, half, slot).wait_send()

        @pl.when(sends_chain(slot))
        def _():
            chain_copy(step, half, slot).wait_send()

        @pl.when(sends_beside(slot))
        def _():
            beside_copy(own.at[step, half], step, half, slot).wait_send()

    def drain_step(step):
        for half in range(2):
            for slot in range(hops):
                if half == 0 or slot < hops - 1:
                    drain(step, half, slot)
        for phase in range(4):
            for group in range(2):
                for offset in range(1, side):
                    score_copy(step, group, phase, offset).wait_send()

    loading[0].wait()
    loading[1].wait()
    find_reach()
    for part in range(rows // LANES):
        loading[9 + part].wait()
        turn(2, part, part + 1)
    for index in range(4, 9):
        loading[index].start()
    loading[2].wait()
    loading[3].wait()
    take_own(0, 0)
    shear(2 * hops - 1, 2 * hops + 1)

    def set_up(step, low, high):
        @pl.when(step == 0)
        def _():
            shear(low, high)

    def set_up_far(step):
        @pl.when(step == 0)
        def _():
            loading[4].wait()
            turn(1)
            shear(2 * hops - 3, 2 * hops - 1)
            turn(0)

    def set_up_factors(step):
        @pl.when(step == 0)
        def _():
            loading[5].wait()
            loading[6].wait()
            for half in range(2):
                at = slice(half * LANES, (half + 1) * LANES)
                for part, values in enumerate(split(factor_in[at, :])):
                    into_scores[half, part, :LANES] = values
                    into_scores[half, part, LANES:] = values
                high, low = split(factor_out[at, :])
                from_scores[half, :LANES] = high
                from_scores[half, LANES:] = low
            loading[7].wait()
            loading[8].wait()

    def step_body(step, carry):
        for half in range(2):
            @pl.when(step > 0)
            def _():
                if half == 1:
                    upper_parts(step - 1, half, 1)
                finish_ahead(step - 1, half)
                if half == 0:
                    score_step(step - 1, 4)
                else:

                    @pl.when(step == STEPS)
                    def _():
                        drain_step(step - 1)

                finish_chain(step - 1, half)

            @pl.when(step == 1)
            def _():
                send_own(step, half)
                take_own(step, half)

            if half == 1:
                @pl.when(step == 0)
                def _():
                    take_own(step, half)

            @pl.when(step < STEPS)
            def _():
                start(step, half)

        @pl.when(step < STEPS)
        def _():
            set_up_factors(step)
            score_start(step)
            arrive_ahead(step, 0, 0)
            set_up_far(step)
            pass_on(step, 0, 0)
            arrive_chain(step, 0, 0)
            arrive_ahead(step, 1, 0)
            pass_on(step, 1, 0)
            arrive_chain(step, 1, 0)
            score_step(step, 1)
            set_up(step, 1, 3)
            arrive_ahead(step, 0, 1)
            pass_on(step, 0, 1)
            arrive_chain(step, 0, 1)
            score_step(step, 2)
            arrive_ahead(step, 1, 1)
            pass_on(step, 1, 1)
            set_up(step, 0, 1)
            diagonal(0)
            arrive_chain(step, 1, 1)
            score_step(step, 3)

            @pl.when(step > 0)
            def _():
                drain_step(step - 1)
                drain(step - 1, 1, hops - 1)

            diagonal(1)
            upper_parts(step, 0, 0)
            upper_parts(step, 1, 0)
            upper_parts(step, 0, 1)

        return carry

    lax.fori_loop(0, STEPS + 1, step_body, 0)

    drain(STEPS - 1, 1, hops - 1)
    for half in range(2):
        for i in range(2):
            write(half, i).wait()


def body(total_rows, side, ld_band, marginal, effects_init, factor_in, factor_out, ld_width, ld_starts):
    rows, span = ld_band.shape
    traits, factors = factor_in.shape
    hops = span // (2 * rows)
    blocks = 2 * hops + 1
    f32, bf16 = jnp.float32, jnp.bfloat16
    piece = (rows, LANES)
    quarter = rows // (2 * side)
    dma = pltpu.SemaphoreType.DMA
    scratch = [
        pltpu.VMEM((1,) + ld_width.shape, jnp.int32),
        pltpu.VMEM((1,) + ld_starts.shape, jnp.int32),
        pltpu.VMEM((rows, span), f32),
        pltpu.VMEM((rows, LANES), jnp.int32),
        pltpu.VMEM((rows * span // LANES, LANES), f32),
        pltpu.VMEM((rows * span // LANES, LANES), f32),
        pltpu.VMEM((blocks, 2, 2, rows // 2, rows), bf16),
        pltpu.VMEM((STEPS + 1, 2) + piece, f32),
        pltpu.VMEM((2, rows, 2 * LANES), bf16),
        pltpu.VMEM((2, 2 * rows, 2 * LANES), bf16),
        pltpu.VMEM((2,) + piece, f32),
        pltpu.VMEM((2,) + piece, f32),
        pltpu.VMEM((STEPS, 2, hops) + piece, f32),
        pltpu.VMEM((STEPS, 2, hops) + piece, f32),
        pltpu.VMEM((STEPS, 2, hops) + piece, f32),
        pltpu.VMEM((STEPS, 2, hops) + piece, f32),
        pltpu.VMEM((STEPS, 2, hops) + piece, f32),
        pltpu.VMEM((STEPS, 2) + piece, f32),
        pltpu.VMEM((2,) + piece, f32),
        pltpu.VMEM((2,) + piece, f32),
        pltpu.VMEM((traits, factors), f32),
        pltpu.VMEM((traits, factors), f32),
        pltpu.VMEM((2, 2, 2 * LANES, factors), bf16),
        pltpu.VMEM((2, 2 * LANES, factors), bf16),
        pltpu.VMEM((STEPS, rows, factors), f32),
        pltpu.VMEM((STEPS, 2, side - 1, quarter, factors), f32),
        pltpu.VMEM((STEPS, 2, quarter, factors), f32),
        pltpu.VMEM((STEPS, 2, side - 1, quarter // side, factors), f32),
        pltpu.VMEM((STEPS, 2, quarter, factors), f32),
        pltpu.VMEM((STEPS, rows, factors), f32),
        pltpu.VMEM((2,) + piece, f32),
        dma((9 + rows // LANES,)),
    ]
    scratch += [dma((STEPS, 2, hops)) for _ in range(8)]
    scratch += [dma((STEPS, 2, 4, side - 1)) for _ in range(2)]

    def call(*refs):
        kernel(total_rows, side, *refs)

    whole = pl.BlockSpec(memory_space=pl.ANY)
    return pl.pallas_call(
        call,
        name="fit",
        out_shape=jax.ShapeDtypeStruct(effects_init.shape, f32),
        in_specs=[whole] * 7,
        out_specs=whole,
        scratch_shapes=scratch,
        compiler_params=pltpu.CompilerParams(
            collective_id=0, has_side_effects=True, vmem_limit_bytes=60 * 1024 * 1024
        ),
    )(ld_band, marginal, effects_init, factor_in, factor_out, ld_width[None, :], ld_starts[None, :])


def solution(mesh):
    side = 4
    total_rows = mesh.shape["snp"] * 512

    def run(*args):
        return body(total_rows, side, *args)

    return jax.shard_map(
        run,
        mesh=mesh,
        in_specs=(
            P("snp", None),
            P("snp", "trait"),
            P("snp", "trait"),
            P("trait", None),
            P("trait", None),
            P(),
            P(),
        ),
        out_specs=P("snp", "trait"),
        check_vma=False,
    )
```

```python
import jax
import jax.numpy as jnp
from jax import lax
from jax.experimental import pallas as pl
from jax.experimental.pallas import tpu as pltpu
from jax.sharding import PartitionSpec as P

STEPS = 2
MESH = pl.DeviceIdType.MESH
LANES = 128
GROUP = 16

step_size = 0.5
shrinkage = 0.5


def split(values):
    high = values.astype(jnp.bfloat16)
    low = (values - high.astype(jnp.float32)).astype(jnp.bfloat16)
    return high, low


def dot(left, right, contract=((1,), (0,))):
    return lax.dot_general(left, right, (contract, ((), ())), preferred_element_type=jnp.float32)


def kernel(
    total_rows,
    side,
    band_hbm,
    marginal_hbm,
    effects_hbm,
    factor_in_hbm,
    factor_out_hbm,
    width_hbm,
    starts_hbm,
    out_hbm,
    width,
    starts,
    band,
    reach,
    stacked,
    rotated,
    upper,
    own,
    own_split,
    own_stack,
    marginal,
    total,
    ahead,
    beside,
    chain,
    crossed,
    crossing,
    first,
    later,
    home,
    factor_in,
    factor_out,
    into_scores,
    from_scores,
    partial,
    from_along,
    over_along,
    from_across,
    over_both,
    scores,
    projected,
    load_sem,
    ahead_send,
    ahead_recv,
    beside_send,
    beside_recv,
    chain_send,
    chain_recv,
    cross_send,
    cross_recv,
    score_send,
    score_recv,
):
    rows = band.shape[0]
    span = band.shape[1]
    hops = span // (2 * rows)
    blocks = 2 * hops + 1
    device = lax.axis_index("snp")
    column = lax.axis_index("trait")
    devices = lax.axis_size("snp")
    core = lax.rem(device, 2)
    chip = lax.div(device, 2)
    chips = devices // 2
    behind_id = (lax.rem(device + devices - 2, devices), column)
    ahead_id = (lax.rem(device + 2, devices), column)
    beside_id = (device + 1 - 2 * core, column)
    my_y = lax.div(column, side)
    my_x = lax.rem(column, side)

    def x_peer(offset):
        return lax.rem(my_x + offset, side)

    def y_peer(offset):
        return lax.rem(my_y + offset, side)

    def x_id(offset):
        return (device, my_y * side + x_peer(offset))

    def y_id(offset):
        return (device, y_peer(offset) * side + my_x)

    partners = [beside_id]
    for offset in range(1, side):
        partners += [x_id(offset), y_id(offset)]
    barrier = pltpu.get_barrier_semaphore()
    for partner in partners:
        pl.semaphore_signal(barrier, inc=1, device_id=partner, device_id_type=MESH)

    @pl.when(chip >= 1)
    def _():
        pl.semaphore_signal(barrier, inc=1, device_id=behind_id, device_id_type=MESH)

    @pl.when(chip + 1 < chips)
    def _():
        pl.semaphore_signal(barrier, inc=1, device_id=ahead_id, device_id_type=MESH)

    near = 2 * rows * (hops - 1)
    loads = [
        (width_hbm, width),
        (starts_hbm, starts),
        (effects_hbm.at[:, pl.ds(0, LANES)], own.at[0, 0]),
        (effects_hbm.at[:, pl.ds(LANES, LANES)], own.at[0, 1]),
        (band_hbm.at[:, pl.ds(0, near)], band.at[:, pl.ds(0, near)]),
        (factor_in_hbm, factor_in),
        (factor_out_hbm, factor_out),
        (marginal_hbm.at[:, pl.ds(0, LANES)], marginal.at[0]),
        (marginal_hbm.at[:, pl.ds(LANES, LANES)], marginal.at[1]),
    ]
    for top in range(0, rows, LANES):
        part = (pl.ds(top, LANES), pl.ds(near, span - near))
        loads.append((band_hbm.at[part], band.at[part]))
    loading = [pltpu.make_async_copy(a, b, load_sem.at[i]) for i, (a, b) in enumerate(loads)]
    for index in (0, 1, 9, 10, 11, 12, 2, 3):
        loading[index].start()

    ends = jnp.where(chip >= 1, 1, 0) + jnp.where(chip + 1 < chips, 1, 0)

    def remote(source, target, send, recv, to):
        return pltpu.make_async_remote_copy(
            src_ref=source, dst_ref=target, send_sem=send, recv_sem=recv, device_id=to, device_id_type=MESH
        )

    def ahead_copy(step, half, slot, source=None):
        if source is None:
            source = own.at[step, half] if slot == 0 else ahead.at[step, half, slot - 1]
        return remote(
            source,
            ahead.at[step, half, slot],
            ahead_send.at[step, half, slot],
            ahead_recv.at[step, half, slot],
            behind_id,
        )

    def beside_copy(source, step, half, slot):
        return remote(
            source,
            beside.at[step, half, slot],
            beside_send.at[step, half, slot],
            beside_recv.at[step, half, slot],
            beside_id,
        )

    def chain_copy(step, half, slot):
        source = first.at[step, half] if slot == 0 else chain.at[step, half, slot - 1]
        return remote(
            source,
            chain.at[step, half, slot],
            chain_send.at[step, half, slot],
            chain_recv.at[step, half, slot],
            ahead_id,
        )

    def cross_copy(step, half, slot):
        return remote(
            crossing.at[step, half, slot],
            crossed.at[step, half, slot],
            cross_send.at[step, half, slot],
            cross_recv.at[step, half, slot],
            beside_id,
        )

    def sends_ahead(slot):
        return (chip >= 1) & (chip + slot < chips)

    def takes_ahead(slot):
        return chip + 1 + slot < chips

    def takes_beside(slot):
        return chip + slot + core < chips

    def sends_beside(slot):
        return chip + 1 - core + slot < chips

    def sends_chain(slot):
        return chip + hops - slot < chips

    def takes_chain(slot):
        return (chip >= 1) & (chip + hops - 1 - slot < chips)

    def send_own(step, half):
        @pl.when(sends_ahead(0))
        def _():
            ahead_copy(step, half, 0).start()

        @pl.when(core == 1)
        def _():
            beside_copy(own.at[step, half], step, half, 0).start()

    def enter():
        pl.semaphore_wait(barrier, len(partners) + ends)
        for half in range(2):
            source = effects_hbm.at[:, pl.ds(half * LANES, LANES)]
            at_first = ahead_copy(0, half, 0, source)
            to_beside = beside_copy(source, 0, half, 0)

            @pl.when(sends_ahead(0))
            def _():
                at_first.start()

            @pl.when(core == 1)
            def _():
                to_beside.start()

    early = chip < chips // 2

    @pl.when(jnp.logical_not(early))
    def _():
        enter()

    def find_reach():
        for base in range(0, rows, LANES):
            index = lax.broadcasted_iota(jnp.int32, (LANES, width.shape[1]), 0) + (device * rows + base)
            entry = lax.broadcasted_iota(jnp.int32, index.shape, 1)
            covered = jnp.where(starts[...] <= index, 1, 0)
            last = jnp.sum(covered, axis=1, keepdims=True) - 1
            found = jnp.sum(jnp.where(entry == last, width[...], 0), axis=1, keepdims=True)
            limit = jnp.minimum(found, total_rows - 1 - index[:, :1])
            reach[base : base + LANES, :] = jnp.broadcast_to(limit, (LANES, LANES))

    half_rows = rows // 2
    per_block = rows // LANES

    def turn(chunk, low=0, high=rows // LANES):
        def spread(group, carry):
            for part in range(2):
                at = pl.multiple_of(group * GROUP + part * 8, 8)
                for tile in range(8):
                    lanes = slice((chunk * 8 + tile) * LANES, (chunk * 8 + tile + 1) * LANES)
                    stacked[pl.ds((chunk * rows + at) * 8 + tile, 8, stride=8), :] = band[pl.ds(at, 8), lanes]
            return carry

        def rotate(group, carry):
            for row in range(LANES):
                at = pl.multiple_of((chunk * rows + group * LANES + row) * 8, 8)
                values = stacked[pl.ds(at, 8), :]
                rotated[pl.ds(at, 8), :] = values if row + 1 == LANES else pltpu.roll(values, row + 1, 1)
            return carry

        lax.fori_loop(low * (LANES // GROUP), high * (LANES // GROUP), spread, 0)
        lax.fori_loop(low, high, rotate, 0)

    def shear(low_block, high_block):
        def body(group, carry):
            shift = group * GROUP
            lane = lax.broadcasted_iota(jnp.int32, (GROUP, LANES), 1)
            row = lax.broadcasted_iota(jnp.int32, (GROUP, LANES), 0)
            from_left = lane < row + (shift + 1)
            for base in range(rows // LANES):
                at = pl.multiple_of(base * LANES + shift, GROUP)
                limit = reach[pl.ds(at, GROUP), :] + (row - lane) + (at + 1)

                def turned(tile):
                    if tile < 0 or tile >= span // LANES:
                        return jnp.zeros((GROUP, LANES), jnp.float32)
                    return rotated[pl.ds((tile // 8 * rows + at) * 8 + tile % 8, GROUP, stride=8), :]

                left = turned(low_block * per_block - base - 1)
                for tile in range(low_block * per_block, high_block * per_block):
                    right = turned(tile - base)
                    values = jnp.where(from_left, left, right)
                    high, low = split(jnp.where(tile * LANES < limit, values, 0.0))
                    left = right
                    block, at_tile = tile // per_block, tile % per_block
                    row_half = base * LANES // half_rows
                    inner = pl.multiple_of(at - row_half * half_rows, GROUP)
                    lanes = slice(at_tile * LANES, (at_tile + 1) * LANES)
                    upper[block, row_half, 0, pl.ds(inner, GROUP), lanes] = high
                    upper[block, row_half, 1, pl.ds(inner, GROUP), lanes] = low
            return carry

        lax.fori_loop(0, LANES // GROUP, body, 0)

    def product(block, right, put):
        for i in range(2):
            found = dot(upper[block, i].reshape(rows, rows), right)
            found = found[:, :LANES] + found[:, LANES:]
            put(i, found[:half_rows] + found[half_rows:])

    def store_to(ref):
        def put(i, values):
            ref[i * half_rows : (i + 1) * half_rows, :] = values

        return put

    def add_to(ref):
        def put(i, values):
            ref[i * half_rows : (i + 1) * half_rows, :] += values

        return put

    def lower_part(block, half, ref):
        for i in range(2):
            lanes = slice(i * half_rows, (i + 1) * half_rows)
            left = upper[block, :, :, :, lanes].reshape(2 * rows, half_rows)
            found = dot(left, own_stack[half], ((0,), (0,)))
            ref[lanes, :] = found[:, :LANES] + found[:, LANES:]

    def joined(values):
        return jnp.concatenate(split(values), axis=1)

    def take_own(step, half):
        found = joined(own[step, half])
        own_split[half] = found
        for i in range(2):
            for copy in range(2):
                at = (2 * i + copy) * half_rows
                own_stack[half, at : at + half_rows] = found[i * half_rows : (i + 1) * half_rows]

    def start(step, half):
        def send_beside():
            lower_part(2 * hops - 1, half, crossing.at[step, half, 0])
            cross_copy(step, half, 0).start()

        @pl.when(core == 1)
        def _():
            send_beside()

        lower_part(2 * hops, half, first.at[step, half])

        @pl.when(core == 0)
        def _():
            cross_copy(step, half, 0).wait_recv()
            first[step, half] += crossed[step, half, 0]

        @pl.when(sends_chain(0))
        def _():
            chain_copy(step, half, 0).start()

        @pl.when(core == 0)
        def _():
            send_beside()

    def ahead_part(step, half, slot):
        @pl.when(takes_ahead(slot))
        def _():
            product(2 * slot + 2, joined(ahead[step, half, slot]), add_to(total.at[half]))

    def beside_part(step, half, slot):
        @pl.when(takes_beside(slot))
        def _():
            beside_copy(own.at[step, half], step, half, slot).wait_recv()
            product(2 * slot + 1, joined(beside[step, half, slot]), add_to(total.at[half]))

    def finish_ahead(step, half):
        last = hops - 1

        @pl.when(takes_ahead(last))
        def _():
            ahead_copy(step, half, last).wait_recv()

            @pl.when(core == 0)
            def _():
                beside_copy(ahead.at[step, half, last], step, half, last).start()

        ahead_part(step, half, last)

        @pl.when(core == 1)
        def _():
            cross_copy(step, half, last).wait_recv()
            home[half] += crossed[step, half, last]

        beside_part(step, half, last)
        total[half] += home[half]

    def finish_chain(step, half):
        last = hops - 1

        @pl.when(takes_chain(last))
        def _():
            chain_copy(step, half, last).wait_recv()
            total[half] += chain[step, half, last]

        for i in range(2):
            at = slice(i * half_rows, (i + 1) * half_rows)
            effects = own[step, half, at]
            gradient = (
                effects
                + total[half, at]
                - marginal[half, at]
                + shrinkage * (effects - projected[half, at])
            )
            own[step + 1, half, at] = effects - step_size * gradient

            @pl.when(step + 1 == STEPS)
            def _():
                write(half, i).start()

    def write(half, i):
        at = pl.ds(i * half_rows, half_rows)
        return pltpu.make_async_copy(
            own.at[STEPS, half, at], out_hbm.at[at, pl.ds(half * LANES, LANES)], load_sem.at[2 * half + i]
        )

    def arrive_ahead(step, half, slot):
        @pl.when(takes_ahead(slot))
        def _():
            ahead_copy(step, half, slot).wait_recv()
            beside_copy(ahead.at[step, half, slot], step, half, slot + core).start()

        @pl.when(sends_ahead(slot + 1))
        def _():
            ahead_copy(step, half, slot + 1).start()

    def arrive_chain(step, half, slot):
        cross_copy(step, half, slot + 1 - core).wait_recv()
        later[half] += crossed[step, half, slot + 1 - core]

        @pl.when(takes_chain(slot))
        def _():
            chain_copy(step, half, slot).wait_recv()
            chain[step, half, slot] += later[half]

        @pl.when(chip == 0)
        def _():
            chain[step, half, slot] = later[half]

        @pl.when(sends_chain(slot + 1))
        def _():
            chain_copy(step, half, slot + 1).start()

    def pass_on(step, half, slot):
        block = 2 * (hops - 1 - slot)
        lower_part(block - 1, half, crossing.at[step, half, slot + 1])
        cross_copy(step, half, slot + 1).start()
        lower_part(block, half, later.at[half])

    def diagonal(half):
        lower_part(0, half, home.at[half])
        product(0, own_split[half], store_to(total.at[half]))

    def upper_parts(step, half, slot):
        ahead_part(step, half, slot)
        beside_part(step, half, slot)

    quarter = half_rows // side
    piece = quarter // side
    places = (my_x, my_y)
    peers = (x_peer, y_peer)
    ids = (x_id, y_id)

    def stripe(group, index):
        return pl.ds(pl.multiple_of(group * half_rows + index * quarter, quarter), quarter)

    def strip(index):
        return pl.ds(pl.multiple_of(index * piece, piece), piece)

    def score_copy(step, group, phase, offset):
        along, across = group, 1 - group
        source, target, to = [
            (
                partial.at[step, stripe(group, peers[along](offset))],
                from_along.at[step, group, offset - 1],
                ids[along](offset),
            ),
            (
                over_along.at[step, group, strip(peers[across](offset))],
                from_across.at[step, group, offset - 1],
                ids[across](offset),
            ),
            (
                over_both.at[step, group, strip(places[across])],
                over_both.at[step, group, strip(places[across])],
                ids[across](offset),
            ),
            (
                over_both.at[step, group],
                scores.at[step, stripe(group, places[along])],
                ids[along](offset),
            ),
        ][phase]
        return remote(
            source,
            target,
            score_send.at[step, group, phase, offset - 1],
            score_recv.at[step, group, phase, offset - 1],
            to,
        )

    def score_send_all(step, phase):
        for offset in range(1, side):
            for group in range(2):
                score_copy(step, group, phase, offset).start()

    def score_start(step):
        for i in range(2):
            at = slice(i * half_rows, (i + 1) * half_rows)
            found = dot(own_split[0, at], into_scores[0, 0])
            for half, part in ((0, 1), (1, 0), (1, 1)):
                found += dot(own_split[half, at], into_scores[half, part])
            partial[step, at] = found
        score_send_all(step, 0)

    def score_step(step, phase):
        for group in range(2):
            for offset in range(1, side):
                score_copy(step, group, phase - 1, offset).wait_recv()
            mine = strip(places[1 - group])
            if phase == 1:
                found = partial[step, stripe(group, places[group])]
                for other in range(side - 1):
                    found += from_along[step, group, other]
                over_along[step, group] = found
            if phase == 2:
                found = over_along[step, group, mine]
                for other in range(side - 1):
                    found += from_across[step, group, other]
                over_both[step, group, mine] = found
            if phase == 3:
                scores[step, stripe(group, places[group])] = over_both[step, group]
        if phase == 4:
            for i in range(2):
                at = slice(i * half_rows, (i + 1) * half_rows)
                high, low = split(scores[step, at])
                for half in range(2):
                    found = dot(high, from_scores[half], ((1,), (1,)))
                    found += dot(low, from_scores[half], ((1,), (1,)))
                    projected[half, at] = found[:, :LANES] + found[:, LANES:]
            return
        score_send_all(step, phase)

    def drain(step, half, slot):
        cross_copy(step, half, slot).wait_send()

        @pl.when(sends_ahead(slot))
        def _():
            ahead_copy(step, half, slot).wait_send()

        @pl.when(sends_chain(slot))
        def _():
            chain_copy(step, half, slot).wait_send()

        @pl.when(sends_beside(slot))
        def _():
            beside_copy(own.at[step, half], step, half, slot).wait_send()

    def drain_step(step):
        for half in range(2):
            for slot in range(hops):
                if half == 0 or slot < hops - 1:
                    drain(step, half, slot)
        for phase in range(4):
            for group in range(2):
                for offset in range(1, side):
                    score_copy(step, group, phase, offset).wait_send()

    loading[0].wait()
    loading[1].wait()
    find_reach()
    for part in range(rows // LANES):
        loading[9 + part].wait()
        turn(2, part, part + 1)
    for index in range(4, 9):
        loading[index].start()
    loading[2].wait()
    loading[3].wait()
    take_own(0, 0)
    shear(2 * hops - 1, 2 * hops + 1)

    @pl.when(early)
    def _():
        enter()

    def set_up(step, low, high):
        @pl.when(step == 0)
        def _():
            shear(low, high)

    def set_up_far(step):
        @pl.when(step == 0)
        def _():
            loading[4].wait()
            turn(1)
            shear(2 * hops - 3, 2 * hops - 1)
            turn(0)

    def set_up_factors(step):
        @pl.when(step == 0)
        def _():
            loading[5].wait()
            loading[6].wait()
            for half in range(2):
                at = slice(half * LANES, (half + 1) * LANES)
                for part, values in enumerate(split(factor_in[at, :])):
                    into_scores[half, part, :LANES] = values
                    into_scores[half, part, LANES:] = values
                high, low = split(factor_out[at, :])
                from_scores[half, :LANES] = high
                from_scores[half, LANES:] = low
            loading[7].wait()
            loading[8].wait()

    def step_body(step, carry):
        for half in range(2):
            @pl.when(step > 0)
            def _():
                if half == 1:
                    upper_parts(step - 1, half, 1)
                finish_ahead(step - 1, half)
                if half == 0:
                    score_step(step - 1, 4)
                else:

                    @pl.when(step == STEPS)
                    def _():
                        drain_step(step - 1)

                finish_chain(step - 1, half)

            @pl.when(step == 1)
            def _():
                send_own(step, half)
                take_own(step, half)

            if half == 1:
                @pl.when(step == 0)
                def _():
                    take_own(step, half)

            @pl.when(step < STEPS)
            def _():
                start(step, half)

        @pl.when(step < STEPS)
        def _():
            set_up_factors(step)
            score_start(step)
            arrive_ahead(step, 0, 0)
            set_up_far(step)
            pass_on(step, 0, 0)
            arrive_chain(step, 0, 0)
            arrive_ahead(step, 1, 0)
            pass_on(step, 1, 0)
            arrive_chain(step, 1, 0)
            score_step(step, 1)
            set_up(step, 1, 3)
            arrive_ahead(step, 0, 1)
            pass_on(step, 0, 1)
            arrive_chain(step, 0, 1)
            score_step(step, 2)
            arrive_ahead(step, 1, 1)
            pass_on(step, 1, 1)
            set_up(step, 0, 1)
            diagonal(0)
            arrive_chain(step, 1, 1)
            score_step(step, 3)

            @pl.when(step > 0)
            def _():
                drain_step(step - 1)
                drain(step - 1, 1, hops - 1)

            diagonal(1)
            upper_parts(step, 0, 0)
            upper_parts(step, 1, 0)
            upper_parts(step, 0, 1)

        return carry

    lax.fori_loop(0, STEPS + 1, step_body, 0)

    drain(STEPS - 1, 1, hops - 1)
    for half in range(2):
        for i in range(2):
            write(half, i).wait()


def body(total_rows, side, ld_band, marginal, effects_init, factor_in, factor_out, ld_width, ld_starts):
    rows, span = ld_band.shape
    traits, factors = factor_in.shape
    hops = span // (2 * rows)
    blocks = 2 * hops + 1
    f32, bf16 = jnp.float32, jnp.bfloat16
    piece = (rows, LANES)
    quarter = rows // (2 * side)
    dma = pltpu.SemaphoreType.DMA
    scratch = [
        pltpu.VMEM((1,) + ld_width.shape, jnp.int32),
        pltpu.VMEM((1,) + ld_starts.shape, jnp.int32),
        pltpu.VMEM((rows, span), f32),
        pltpu.VMEM((rows, LANES), jnp.int32),
        pltpu.VMEM((rows * span // LANES, LANES), f32),
        pltpu.VMEM((rows * span // LANES, LANES), f32),
        pltpu.VMEM((blocks, 2, 2, rows // 2, rows), bf16),
        pltpu.VMEM((STEPS + 1, 2) + piece, f32),
        pltpu.VMEM((2, rows, 2 * LANES), bf16),
        pltpu.VMEM((2, 2 * rows, 2 * LANES), bf16),
        pltpu.VMEM((2,) + piece, f32),
        pltpu.VMEM((2,) + piece, f32),
        pltpu.VMEM((STEPS, 2, hops) + piece, f32),
        pltpu.VMEM((STEPS, 2, hops) + piece, f32),
        pltpu.VMEM((STEPS, 2, hops) + piece, f32),
        pltpu.VMEM((STEPS, 2, hops) + piece, f32),
        pltpu.VMEM((STEPS, 2, hops) + piece, f32),
        pltpu.VMEM((STEPS, 2) + piece, f32),
        pltpu.VMEM((2,) + piece, f32),
        pltpu.VMEM((2,) + piece, f32),
        pltpu.VMEM((traits, factors), f32),
        pltpu.VMEM((traits, factors), f32),
        pltpu.VMEM((2, 2, 2 * LANES, factors), bf16),
        pltpu.VMEM((2, 2 * LANES, factors), bf16),
        pltpu.VMEM((STEPS, rows, factors), f32),
        pltpu.VMEM((STEPS, 2, side - 1, quarter, factors), f32),
        pltpu.VMEM((STEPS, 2, quarter, factors), f32),
        pltpu.VMEM((STEPS, 2, side - 1, quarter // side, factors), f32),
        pltpu.VMEM((STEPS, 2, quarter, factors), f32),
        pltpu.VMEM((STEPS, rows, factors), f32),
        pltpu.VMEM((2,) + piece, f32),
        dma((9 + rows // LANES,)),
    ]
    scratch += [dma((STEPS, 2, hops)) for _ in range(8)]
    scratch += [dma((STEPS, 2, 4, side - 1)) for _ in range(2)]

    def call(*refs):
        kernel(total_rows, side, *refs)

    whole = pl.BlockSpec(memory_space=pl.ANY)
    return pl.pallas_call(
        call,
        name="fit",
        out_shape=jax.ShapeDtypeStruct(effects_init.shape, f32),
        in_specs=[whole] * 7,
        out_specs=whole,
        scratch_shapes=scratch,
        compiler_params=pltpu.CompilerParams(
            collective_id=0, has_side_effects=True, vmem_limit_bytes=60 * 1024 * 1024
        ),
    )(ld_band, marginal, effects_init, factor_in, factor_out, ld_width[None, :], ld_starts[None, :])


def solution(mesh):
    side = 4
    total_rows = mesh.shape["snp"] * 512

    def run(*args):
        return body(total_rows, side, *args)

    return jax.shard_map(
        run,
        mesh=mesh,
        in_specs=(
            P("snp", None),
            P("snp", "trait"),
            P("snp", "trait"),
            P("trait", None),
            P("trait", None),
            P(),
            P(),
        ),
        out_specs=P("snp", "trait"),
        check_vma=False,
    )
```

```python
import jax
import jax.numpy as jnp
from jax import lax
from jax.experimental import pallas as pl
from jax.experimental.pallas import tpu as pltpu
from jax.sharding import PartitionSpec as P

STEPS = 2
MESH = pl.DeviceIdType.MESH
LANES = 128
GROUP = 16

step_size = 0.5
shrinkage = 0.5


def split(values):
    high = values.astype(jnp.bfloat16)
    low = (values - high.astype(jnp.float32)).astype(jnp.bfloat16)
    return high, low


def dot(left, right, contract=((1,), (0,))):
    return lax.dot_general(left, right, (contract, ((), ())), preferred_element_type=jnp.float32)


def kernel(
    total_rows,
    side,
    band_hbm,
    marginal_hbm,
    effects_hbm,
    factor_in_hbm,
    factor_out_hbm,
    width_hbm,
    starts_hbm,
    out_hbm,
    width,
    starts,
    band,
    reach,
    stacked,
    rotated,
    upper,
    own,
    own_split,
    own_stack,
    marginal,
    total,
    ahead,
    beside,
    chain,
    crossed,
    crossing,
    first,
    later,
    home,
    factor_in,
    factor_out,
    into_scores,
    from_scores,
    partial,
    from_along,
    over_along,
    from_across,
    over_both,
    scores,
    projected,
    load_sem,
    ahead_send,
    ahead_recv,
    beside_send,
    beside_recv,
    chain_send,
    chain_recv,
    cross_send,
    cross_recv,
    score_send,
    score_recv,
):
    rows = band.shape[0]
    span = band.shape[1]
    hops = span // (2 * rows)
    blocks = 2 * hops + 1
    device = lax.axis_index("snp")
    column = lax.axis_index("trait")
    devices = lax.axis_size("snp")
    core = lax.rem(device, 2)
    chip = lax.div(device, 2)
    chips = devices // 2
    behind_id = (lax.rem(device + devices - 2, devices), column)
    ahead_id = (lax.rem(device + 2, devices), column)
    beside_id = (device + 1 - 2 * core, column)
    my_y = lax.div(column, side)
    my_x = lax.rem(column, side)

    def x_peer(offset):
        return lax.rem(my_x + offset, side)

    def y_peer(offset):
        return lax.rem(my_y + offset, side)

    def x_id(offset):
        return (device, my_y * side + x_peer(offset))

    def y_id(offset):
        return (device, y_peer(offset) * side + my_x)

    partners = [beside_id]
    for offset in range(1, side):
        partners += [x_id(offset), y_id(offset)]
    barrier = pltpu.get_barrier_semaphore()
    for partner in partners:
        pl.semaphore_signal(barrier, inc=1, device_id=partner, device_id_type=MESH)

    @pl.when(chip >= 1)
    def _():
        pl.semaphore_signal(barrier, inc=1, device_id=behind_id, device_id_type=MESH)

    @pl.when(chip + 1 < chips)
    def _():
        pl.semaphore_signal(barrier, inc=1, device_id=ahead_id, device_id_type=MESH)

    near = 2 * rows * (hops - 1)
    loads = [
        (width_hbm, width),
        (starts_hbm, starts),
        (effects_hbm.at[:, pl.ds(0, LANES)], own.at[0, 0]),
        (effects_hbm.at[:, pl.ds(LANES, LANES)], own.at[0, 1]),
        (band_hbm.at[:, pl.ds(0, near)], band.at[:, pl.ds(0, near)]),
        (factor_in_hbm, factor_in),
        (factor_out_hbm, factor_out),
        (marginal_hbm.at[:, pl.ds(0, LANES)], marginal.at[0]),
        (marginal_hbm.at[:, pl.ds(LANES, LANES)], marginal.at[1]),
    ]
    for top in range(0, rows, LANES):
        part = (pl.ds(top, LANES), pl.ds(near, span - near))
        loads.append((band_hbm.at[part], band.at[part]))
    loading = [pltpu.make_async_copy(a, b, load_sem.at[i]) for i, (a, b) in enumerate(loads)]
    for index in (0, 1, 9, 10, 11, 12, 2, 3):
        loading[index].start()

    ends = jnp.where(chip >= 1, 1, 0) + jnp.where(chip + 1 < chips, 1, 0)

    def remote(source, target, send, recv, to):
        return pltpu.make_async_remote_copy(
            src_ref=source, dst_ref=target, send_sem=send, recv_sem=recv, device_id=to, device_id_type=MESH
        )

    def ahead_copy(step, half, slot, source=None):
        if source is None:
            source = own.at[step, half] if slot == 0 else ahead.at[step, half, slot - 1]
        return remote(
            source,
            ahead.at[step, half, slot],
            ahead_send.at[step, half, slot],
            ahead_recv.at[step, half, slot],
            behind_id,
        )

    def beside_copy(source, step, half, slot):
        return remote(
            source,
            beside.at[step, half, slot],
            beside_send.at[step, half, slot],
            beside_recv.at[step, half, slot],
            beside_id,
        )

    def chain_copy(step, half, slot):
        source = first.at[step, half] if slot == 0 else chain.at[step, half, slot - 1]
        return remote(
            source,
            chain.at[step, half, slot],
            chain_send.at[step, half, slot],
            chain_recv.at[step, half, slot],
            ahead_id,
        )

    def cross_copy(step, half, slot):
        return remote(
            crossing.at[step, half, slot],
            crossed.at[step, half, slot],
            cross_send.at[step, half, slot],
            cross_recv.at[step, half, slot],
            beside_id,
        )

    def sends_ahead(slot):
        return (chip >= 1) & (chip + slot < chips)

    def takes_ahead(slot):
        return chip + 1 + slot < chips

    def takes_beside(slot):
        return chip + slot + core < chips

    def sends_beside(slot):
        return chip + 1 - core + slot < chips

    def sends_chain(slot):
        return chip + hops - slot < chips

    def takes_chain(slot):
        return (chip >= 1) & (chip + hops - 1 - slot < chips)

    def send_own(step, half):
        @pl.when(sends_ahead(0))
        def _():
            ahead_copy(step, half, 0).start()

        @pl.when(core == 1)
        def _():
            beside_copy(own.at[step, half], step, half, 0).start()

    def enter():
        pl.semaphore_wait(barrier, len(partners) + ends)
        for half in range(2):
            source = effects_hbm.at[:, pl.ds(half * LANES, LANES)]
            at_first = ahead_copy(0, half, 0, source)
            to_beside = beside_copy(source, 0, half, 0)

            @pl.when(sends_ahead(0))
            def _():
                at_first.start()

            @pl.when(core == 1)
            def _():
                to_beside.start()

    early = chip < chips // 2

    @pl.when(jnp.logical_not(early))
    def _():
        enter()

    def find_reach():
        for base in range(0, rows, LANES):
            index = lax.broadcasted_iota(jnp.int32, (LANES, width.shape[1]), 0) + (device * rows + base)
            entry = lax.broadcasted_iota(jnp.int32, index.shape, 1)
            covered = jnp.where(starts[...] <= index, 1, 0)
            last = jnp.sum(covered, axis=1, keepdims=True) - 1
            found = jnp.sum(jnp.where(entry == last, width[...], 0), axis=1, keepdims=True)
            limit = jnp.minimum(found, total_rows - 1 - index[:, :1])
            reach[base : base + LANES, :] = jnp.broadcast_to(limit, (LANES, LANES))

    half_rows = rows // 2
    per_block = rows // LANES

    def turn(chunk, low=0, high=rows // LANES):
        def spread(group, carry):
            for part in range(2):
                at = pl.multiple_of(group * GROUP + part * 8, 8)
                for tile in range(8):
                    lanes = slice((chunk * 8 + tile) * LANES, (chunk * 8 + tile + 1) * LANES)
                    stacked[pl.ds((chunk * rows + at) * 8 + tile, 8, stride=8), :] = band[pl.ds(at, 8), lanes]
            return carry

        def rotate(group, carry):
            for row in range(LANES):
                at = pl.multiple_of((chunk * rows + group * LANES + row) * 8, 8)
                values = stacked[pl.ds(at, 8), :]
                rotated[pl.ds(at, 8), :] = values if row + 1 == LANES else pltpu.roll(values, row + 1, 1)
            return carry

        lax.fori_loop(low * (LANES // GROUP), high * (LANES // GROUP), spread, 0)
        lax.fori_loop(low, high, rotate, 0)

    def shear(low_block, high_block):
        def body(group, carry):
            shift = group * GROUP
            lane = lax.broadcasted_iota(jnp.int32, (GROUP, LANES), 1)
            row = lax.broadcasted_iota(jnp.int32, (GROUP, LANES), 0)
            from_left = lane < row + (shift + 1)
            for base in range(rows // LANES):
                at = pl.multiple_of(base * LANES + shift, GROUP)
                limit = reach[pl.ds(at, GROUP), :] + (row - lane) + (at + 1)

                def turned(tile):
                    if tile < 0 or tile >= span // LANES:
                        return jnp.zeros((GROUP, LANES), jnp.float32)
                    return rotated[pl.ds((tile // 8 * rows + at) * 8 + tile % 8, GROUP, stride=8), :]

                left = turned(low_block * per_block - base - 1)
                for tile in range(low_block * per_block, high_block * per_block):
                    right = turned(tile - base)
                    values = jnp.where(from_left, left, right)
                    high, low = split(jnp.where(tile * LANES < limit, values, 0.0))
                    left = right
                    block, at_tile = tile // per_block, tile % per_block
                    row_half = base * LANES // half_rows
                    inner = pl.multiple_of(at - row_half * half_rows, GROUP)
                    lanes = slice(at_tile * LANES, (at_tile + 1) * LANES)
                    upper[block, row_half, 0, pl.ds(inner, GROUP), lanes] = high
                    upper[block, row_half, 1, pl.ds(inner, GROUP), lanes] = low
            return carry

        lax.fori_loop(0, LANES // GROUP, body, 0)

    def product(block, right, put):
        for i in range(2):
            found = dot(upper[block, i].reshape(rows, rows), right)
            found = found[:, :LANES] + found[:, LANES:]
            put(i, found[:half_rows] + found[half_rows:])

    def store_to(ref):
        def put(i, values):
            ref[i * half_rows : (i + 1) * half_rows, :] = values

        return put

    def add_to(ref):
        def put(i, values):
            ref[i * half_rows : (i + 1) * half_rows, :] += values

        return put

    def lower_part(block, half, ref):
        for i in range(2):
            lanes = slice(i * half_rows, (i + 1) * half_rows)
            left = upper[block, :, :, :, lanes].reshape(2 * rows, half_rows)
            found = dot(left, own_stack[half], ((0,), (0,)))
            ref[lanes, :] = found[:, :LANES] + found[:, LANES:]

    def joined(values):
        return jnp.concatenate(split(values), axis=1)

    def take_own(step, half):
        found = joined(own[step, half])
        own_split[half] = found
        for i in range(2):
            for copy in range(2):
                at = (2 * i + copy) * half_rows
                own_stack[half, at : at + half_rows] = found[i * half_rows : (i + 1) * half_rows]

    def start(step, half):
        def send_beside():
            lower_part(2 * hops - 1, half, crossing.at[step, half, 0])
            cross_copy(step, half, 0).start()

        @pl.when(core == 1)
        def _():
            send_beside()

        lower_part(2 * hops, half, first.at[step, half])

        @pl.when(core == 0)
        def _():
            cross_copy(step, half, 0).wait_recv()
            first[step, half] += crossed[step, half, 0]

        @pl.when(sends_chain(0))
        def _():
            chain_copy(step, half, 0).start()

        @pl.when(core == 0)
        def _():
            send_beside()

    def ahead_part(step, half, slot):
        @pl.when(takes_ahead(slot))
        def _():
            product(2 * slot + 2, joined(ahead[step, half, slot]), add_to(total.at[half]))

    def beside_part(step, half, slot):
        @pl.when(takes_beside(slot))
        def _():
            beside_copy(own.at[step, half], step, half, slot).wait_recv()
            product(2 * slot + 1, joined(beside[step, half, slot]), add_to(total.at[half]))

    def finish_ahead(step, half):
        last = hops - 1

        @pl.when(takes_ahead(last))
        def _():
            ahead_copy(step, half, last).wait_recv()

            @pl.when(core == 0)
            def _():
                beside_copy(ahead.at[step, half, last], step, half, last).start()

        ahead_part(step, half, last)

        @pl.when(core == 1)
        def _():
            cross_copy(step, half, last).wait_recv()
            home[half] += crossed[step, half, last]

        beside_part(step, half, last)
        total[half] += home[half]

    def finish_chain(step, half):
        last = hops - 1

        @pl.when(takes_chain(last))
        def _():
            chain_copy(step, half, last).wait_recv()
            total[half] += chain[step, half, last]

        for i in range(2):
            at = slice(i * half_rows, (i + 1) * half_rows)
            effects = own[step, half, at]
            gradient = (
                effects
                + total[half, at]
                - marginal[half, at]
                + shrinkage * (effects - projected[half, at])
            )
            own[step + 1, half, at] = effects - step_size * gradient

            @pl.when(step + 1 == STEPS)
            def _():
                write(half, i).start()

    def write(half, i):
        at = pl.ds(i * half_rows, half_rows)
        return pltpu.make_async_copy(
            own.at[STEPS, half, at], out_hbm.at[at, pl.ds(half * LANES, LANES)], load_sem.at[2 * half + i]
        )

    def arrive_ahead(step, half, slot):
        @pl.when(takes_ahead(slot))
        def _():
            ahead_copy(step, half, slot).wait_recv()
            beside_copy(ahead.at[step, half, slot], step, half, slot + core).start()

        @pl.when(sends_ahead(slot + 1))
        def _():
            ahead_copy(step, half, slot + 1).start()

    def arrive_chain(step, half, slot):
        cross_copy(step, half, slot + 1 - core).wait_recv()
        later[half] += crossed[step, half, slot + 1 - core]

        @pl.when(takes_chain(slot))
        def _():
            chain_copy(step, half, slot).wait_recv()
            chain[step, half, slot] += later[half]

        @pl.when(chip == 0)
        def _():
            chain[step, half, slot] = later[half]

        @pl.when(sends_chain(slot + 1))
        def _():
            chain_copy(step, half, slot + 1).start()

    def pass_on(step, half, slot):
        block = 2 * (hops - 1 - slot)
        lower_part(block - 1, half, crossing.at[step, half, slot + 1])
        cross_copy(step, half, slot + 1).start()
        lower_part(block, half, later.at[half])

    def diagonal(half):
        lower_part(0, half, home.at[half])
        product(0, own_split[half], store_to(total.at[half]))

    def upper_parts(step, half, slot):
        ahead_part(step, half, slot)
        beside_part(step, half, slot)

    quarter = half_rows // side
    piece = quarter // side
    places = (my_x, my_y)
    peers = (x_peer, y_peer)
    ids = (x_id, y_id)

    def stripe(group, index):
        return pl.ds(pl.multiple_of(group * half_rows + index * quarter, quarter), quarter)

    def strip(index):
        return pl.ds(pl.multiple_of(index * piece, piece), piece)

    def score_copy(step, group, phase, offset):
        along, across = group, 1 - group
        source, target, to = [
            (
                partial.at[step, stripe(group, peers[along](offset))],
                from_along.at[step, group, offset - 1],
                ids[along](offset),
            ),
            (
                over_along.at[step, group, strip(peers[across](offset))],
                from_across.at[step, group, offset - 1],
                ids[across](offset),
            ),
            (
                over_both.at[step, group, strip(places[across])],
                over_both.at[step, group, strip(places[across])],
                ids[across](offset),
            ),
            (
                over_both.at[step, group],
                scores.at[step, stripe(group, places[along])],
                ids[along](offset),
            ),
        ][phase]
        return remote(
            source,
            target,
            score_send.at[step, group, phase, offset - 1],
            score_recv.at[step, group, phase, offset - 1],
            to,
        )

    def score_send_all(step, phase):
        for offset in range(1, side):
            for group in range(2):
                score_copy(step, group, phase, offset).start()

    def score_start(step):
        for i in range(2):
            at = slice(i * half_rows, (i + 1) * half_rows)
            found = dot(own_split[0, at], into_scores[0, 0])
            for half, part in ((0, 1), (1, 0), (1, 1)):
                found += dot(own_split[half, at], into_scores[half, part])
            partial[step, at] = found
        score_send_all(step, 0)

    def score_step(step, phase):
        for group in range(2):
            for offset in range(1, side):
                score_copy(step, group, phase - 1, offset).wait_recv()
            mine = strip(places[1 - group])
            if phase == 1:
                found = partial[step, stripe(group, places[group])]
                for other in range(side - 1):
                    found += from_along[step, group, other]
                over_along[step, group] = found
            if phase == 2:
                found = over_along[step, group, mine]
                for other in range(side - 1):
                    found += from_across[step, group, other]
                over_both[step, group, mine] = found
            if phase == 3:
                scores[step, stripe(group, places[group])] = over_both[step, group]
        if phase == 4:
            for i in range(2):
                at = slice(i * half_rows, (i + 1) * half_rows)
                high, low = split(scores[step, at])
                for half in range(2):
                    found = dot(high, from_scores[half], ((1,), (1,)))
                    found += dot(low, from_scores[half], ((1,), (1,)))
                    projected[half, at] = found[:, :LANES] + found[:, LANES:]
            return
        score_send_all(step, phase)

    def drain(step, half, slot):
        cross_copy(step, half, slot).wait_send()

        @pl.when(sends_ahead(slot))
        def _():
            ahead_copy(step, half, slot).wait_send()

        @pl.when(sends_chain(slot))
        def _():
            chain_copy(step, half, slot).wait_send()

        @pl.when(sends_beside(slot))
        def _():
            beside_copy(own.at[step, half], step, half, slot).wait_send()

    def drain_step(step):
        for half in range(2):
            for slot in range(hops):
                if half == 0 or slot < hops - 1:
                    drain(step, half, slot)
        for phase in range(4):
            for group in range(2):
                for offset in range(1, side):
                    score_copy(step, group, phase, offset).wait_send()

    loading[0].wait()
    loading[1].wait()
    find_reach()
    for part in range(rows // LANES):
        loading[9 + part].wait()
        turn(2, part, part + 1)
    for index in range(4, 9):
        loading[index].start()
    loading[2].wait()
    loading[3].wait()
    take_own(0, 0)
    shear(2 * hops - 1, 2 * hops + 1)

    @pl.when(early)
    def _():
        enter()

    def set_up(step, low, high):
        @pl.when(step == 0)
        def _():
            shear(low, high)

    def set_up_far(step):
        @pl.when(step == 0)
        def _():
            loading[4].wait()
            turn(1)
            shear(2 * hops - 3, 2 * hops - 1)
            turn(0)

    def set_up_factors(step):
        @pl.when(step == 0)
        def _():
            loading[5].wait()
            loading[6].wait()
            for half in range(2):
                at = slice(half * LANES, (half + 1) * LANES)
                for part, values in enumerate(split(factor_in[at, :])):
                    into_scores[half, part, :LANES] = values
                    into_scores[half, part, LANES:] = values
                high, low = split(factor_out[at, :])
                from_scores[half, :LANES] = high
                from_scores[half, LANES:] = low
            loading[7].wait()
            loading[8].wait()

    def step_body(step, carry):
        for half in range(2):
            @pl.when(step > 0)
            def _():
                if half == 1:
                    upper_parts(step - 1, half, 1)

                    @pl.when(step == STEPS)
                    def _():
                        drain_step(step - 1)

                finish_ahead(step - 1, half)
                if half == 0:
                    score_step(step - 1, 4)
                finish_chain(step - 1, half)

            @pl.when(step == 1)
            def _():
                send_own(step, half)
                take_own(step, half)

            if half == 1:
                @pl.when(step == 0)
                def _():
                    take_own(step, half)

            @pl.when(step < STEPS)
            def _():
                start(step, half)

        @pl.when(step < STEPS)
        def _():
            set_up_factors(step)
            score_start(step)
            arrive_ahead(step, 0, 0)
            set_up_far(step)
            pass_on(step, 0, 0)
            arrive_chain(step, 0, 0)
            arrive_ahead(step, 1, 0)
            pass_on(step, 1, 0)
            arrive_chain(step, 1, 0)
            score_step(step, 1)
            set_up(step, 1, 3)
            arrive_ahead(step, 0, 1)
            pass_on(step, 0, 1)
            arrive_chain(step, 0, 1)
            score_step(step, 2)
            arrive_ahead(step, 1, 1)
            pass_on(step, 1, 1)
            set_up(step, 0, 1)
            diagonal(0)
            arrive_chain(step, 1, 1)
            score_step(step, 3)

            @pl.when(step > 0)
            def _():
                drain_step(step - 1)
                drain(step - 1, 1, hops - 1)

            diagonal(1)
            upper_parts(step, 0, 0)
            upper_parts(step, 1, 0)
            upper_parts(step, 0, 1)

        return carry

    lax.fori_loop(0, STEPS + 1, step_body, 0)

    drain(STEPS - 1, 1, hops - 1)
    for half in range(2):
        for i in range(2):
            write(half, i).wait()


def body(total_rows, side, ld_band, marginal, effects_init, factor_in, factor_out, ld_width, ld_starts):
    rows, span = ld_band.shape
    traits, factors = factor_in.shape
    hops = span // (2 * rows)
    blocks = 2 * hops + 1
    f32, bf16 = jnp.float32, jnp.bfloat16
    piece = (rows, LANES)
    quarter = rows // (2 * side)
    dma = pltpu.SemaphoreType.DMA
    scratch = [
        pltpu.VMEM((1,) + ld_width.shape, jnp.int32),
        pltpu.VMEM((1,) + ld_starts.shape, jnp.int32),
        pltpu.VMEM((rows, span), f32),
        pltpu.VMEM((rows, LANES), jnp.int32),
        pltpu.VMEM((rows * span // LANES, LANES), f32),
        pltpu.VMEM((rows * span // LANES, LANES), f32),
        pltpu.VMEM((blocks, 2, 2, rows // 2, rows), bf16),
        pltpu.VMEM((STEPS + 1, 2) + piece, f32),
        pltpu.VMEM((2, rows, 2 * LANES), bf16),
        pltpu.VMEM((2, 2 * rows, 2 * LANES), bf16),
        pltpu.VMEM((2,) + piece, f32),
        pltpu.VMEM((2,) + piece, f32),
        pltpu.VMEM((STEPS, 2, hops) + piece, f32),
        pltpu.VMEM((STEPS, 2, hops) + piece, f32),
        pltpu.VMEM((STEPS, 2, hops) + piece, f32),
        pltpu.VMEM((STEPS, 2, hops) + piece, f32),
        pltpu.VMEM((STEPS, 2, hops) + piece, f32),
        pltpu.VMEM((STEPS, 2) + piece, f32),
        pltpu.VMEM((2,) + piece, f32),
        pltpu.VMEM((2,) + piece, f32),
        pltpu.VMEM((traits, factors), f32),
        pltpu.VMEM((traits, factors), f32),
        pltpu.VMEM((2, 2, 2 * LANES, factors), bf16),
        pltpu.VMEM((2, 2 * LANES, factors), bf16),
        pltpu.VMEM((STEPS, rows, factors), f32),
        pltpu.VMEM((STEPS, 2, side - 1, quarter, factors), f32),
        pltpu.VMEM((STEPS, 2, quarter, factors), f32),
        pltpu.VMEM((STEPS, 2, side - 1, quarter // side, factors), f32),
        pltpu.VMEM((STEPS, 2, quarter, factors), f32),
        pltpu.VMEM((STEPS, rows, factors), f32),
        pltpu.VMEM((2,) + piece, f32),
        dma((9 + rows // LANES,)),
    ]
    scratch += [dma((STEPS, 2, hops)) for _ in range(8)]
    scratch += [dma((STEPS, 2, 4, side - 1)) for _ in range(2)]

    def call(*refs):
        kernel(total_rows, side, *refs)

    whole = pl.BlockSpec(memory_space=pl.ANY)
    return pl.pallas_call(
        call,
        name="fit",
        out_shape=jax.ShapeDtypeStruct(effects_init.shape, f32),
        in_specs=[whole] * 7,
        out_specs=whole,
        scratch_shapes=scratch,
        compiler_params=pltpu.CompilerParams(
            collective_id=0, has_side_effects=True, vmem_limit_bytes=60 * 1024 * 1024
        ),
    )(ld_band, marginal, effects_init, factor_in, factor_out, ld_width[None, :], ld_starts[None, :])


def solution(mesh):
    side = 4
    total_rows = mesh.shape["snp"] * 512

    def run(*args):
        return body(total_rows, side, *args)

    return jax.shard_map(
        run,
        mesh=mesh,
        in_specs=(
            P("snp", None),
            P("snp", "trait"),
            P("snp", "trait"),
            P("trait", None),
            P("trait", None),
            P(),
            P(),
        ),
        out_specs=P("snp", "trait"),
        check_vma=False,
    )
```
